256 devices in a mesh: leaf: 64 (over z, x, core), front: 4 (over y).
Axes of the slice: x: 4, y: 4, z: 8, core: 2. Of those that a mesh axis runs over, the one named last changes fastest.
Arguments:
- leaf_update: float32 [32768, 512], P('leaf', 'front'), as said below
- front_entries1: float32 [4096, 1024], P('leaf', 'front'), as said below
- front_entries2: float32 [2048, 1024], replicated, as said below
- front_entries3: float32 [1024, 1024], replicated, as said below
- map_leaf: int32 [64, 4], replicated, may hold values from 0 to 7, all different within a row
- map_mid: int32 [4, 4], replicated, may hold values from 0 to 7, all different within a row
- map_top: int32 [2, 4], replicated, may hold values from 0 to 7, as said below
Outputs:
- leaf_inverse: float32 [32768, 512], P('leaf', 'front')
The draws below stay inside these ranges and needn't reach their ends.
Inputs may be any that keep to these rules, and one draw needn't show every extreme that they name: `map_leaf`: row s gives, for each block of 128 rows of subtree s's update, the block of its first level front that receives it; the entries of a row are distinct. `map_mid`: row k gives, for each block of 128 rows of the update of first level node k, the block of second level front k // 2 that receives it; the entries of a row are distinct. `map_top`: row n gives, for each block of 128 rows of the update of second level node n, the block of the top front that receives it; the entries of a row are distinct, and every block of the top front is named by at least one of the two rows. `leaf_update`: each block of 512 rows is symmetric and positive definite. `front_entries1`: each front's block is symmetric and positive definite. `front_entries2`: each front's block is symmetric and positive definite. `front_entries3`: symmetric and positive definite.
All inputs are finite; a program needn't handle non-finite values.
Results may differ from the reference program's by a relative error of at most 0.00017.
Values sent between devices are 32-bit elements; how exact they have to be, the bound alone decides.
A program may use at most 128 MiB of HBM per device.

```python
import jax
import jax.numpy as jnp
from jax import lax

BLK = 128
R0 = 512
SEP1 = 512
SEP2 = 512
SEP3 = 1024
RUP = 512
SUBTREES = 64
N_LEAF = 64


def spd_blocks(key, count, order, weight, lowest, highest):
    first_key, second_key = jax.random.split(key, 2)
    samples = jax.random.normal(first_key, (count, order, order), jnp.float32)
    gram = jnp.einsum('cik,cjk->cij', samples, samples, precision=lax.Precision.HIGHEST) / order
    gram = 0.5 * (gram + jnp.swapaxes(gram, 1, 2))
    diagonal = jax.random.uniform(second_key, (count, order), jnp.float32, lowest, highest)
    matrix = weight * (gram + diagonal[:, :, None] * jnp.eye(order, dtype=jnp.float32)[None])
    return matrix.reshape(count * order, order)


def draw_leaf_update(key, part):
    return spd_blocks(jax.random.fold_in(key, 11), SUBTREES, R0, 0.1, 0.05, 0.15)


def draw_front_entries1(key, part):
    return spd_blocks(jax.random.fold_in(key, 12), 4, SEP1 + RUP, 1.0, 0.03, 0.09)


def draw_front_entries2(key, part):
    return spd_blocks(jax.random.fold_in(key, 13), 2, SEP2 + RUP, 1.0, 0.03, 0.09)


def draw_front_entries3(key, part):
    return spd_blocks(jax.random.fold_in(key, 14), 1, SEP3, 1.0, 0.03, 0.09)


def draw_map_top(key, part):
    top_blocks = SEP3 // BLK
    child_blocks = RUP // BLK
    shuffled = jax.random.permutation(jax.random.fold_in(key, 15), jnp.arange(top_blocks, dtype=jnp.int32))
    first_row = shuffled[:child_blocks]
    second_row = shuffled[top_blocks - child_blocks:]
    return jnp.stack([first_row, second_row], axis=0).astype(jnp.int32)


def picks_of(own_key, rows, count, top, lift):
    order = jax.random.permutation(jax.random.fold_in(own_key, 1), count)
    pull = order
    for power in range(3):
        pull = pull * pull // count
    pull = pull * lift // count
    lots = jax.random.randint(jax.random.fold_in(own_key, 2), (rows, count), 0, 4096) + pull
    sure = jax.random.permutation(jax.random.fold_in(own_key, 3), rows)[jnp.arange(count) % rows]
    lots = jnp.where(jnp.arange(rows)[:, None] == sure[None, :], 1 << 14, lots)
    merit = lots * count + jnp.arange(count)
    return lax.top_k(merit.astype(jnp.int32), top)[1].astype(jnp.int32)


def setup_inputs(seed: int = 0) -> dict:
    key_list = jax.random.split(jax.random.key(seed), 8)
    return {
        "leaf_update": draw_leaf_update(jax.random.fold_in(key_list[7], 71), 0),
        "front_entries1": draw_front_entries1(jax.random.fold_in(key_list[7], 71), 0),
        "front_entries2": draw_front_entries2(jax.random.fold_in(key_list[7], 71), 0),
        "front_entries3": draw_front_entries3(jax.random.fold_in(key_list[7], 71), 0),
        "map_leaf": picks_of(key_list[4], SUBTREES, (SEP1 + RUP) // BLK, R0 // BLK, 0),
        "map_mid": picks_of(key_list[5], 4, (SEP2 + RUP) // BLK, RUP // BLK, 0),
        "map_top": draw_map_top(jax.random.fold_in(key_list[7], 71), 0),
    }


def product(left_side, right_side):
    return jnp.dot(left_side, right_side, precision=lax.Precision.HIGHEST)

def selector(block_list, parent_blocks):
    return (block_list[:, None] == jnp.arange(parent_blocks, dtype=jnp.int32)[None, :]).astype(jnp.float32)

def extend(update, picker):
    child_blocks, parent_blocks = picker.shape
    block_rows = update.shape[0] // child_blocks
    blocked = update.reshape(child_blocks, block_rows, child_blocks, block_rows)
    result = jnp.einsum('ia,jb,ixjy->axby', picker, picker, blocked, precision=lax.Precision.HIGHEST)
    return result.reshape(parent_blocks * block_rows, parent_blocks * block_rows)

def extract(sigma, picker):
    child_blocks, parent_blocks = picker.shape
    block_rows = sigma.shape[0] // parent_blocks
    blocked = sigma.reshape(parent_blocks, block_rows, parent_blocks, block_rows)
    result = jnp.einsum('ia,jb,axby->ixjy', picker, picker, blocked, precision=lax.Precision.HIGHEST)
    return result.reshape(child_blocks * block_rows, child_blocks * block_rows)

def expand(picker, block_rows):
    child_blocks, parent_blocks = picker.shape
    identity = jnp.eye(block_rows, dtype=jnp.float32)
    result = jnp.einsum('ia,xy->axiy', picker, identity, precision=lax.Precision.HIGHEST)
    return result.reshape(parent_blocks * block_rows, child_blocks * block_rows)

def factor(assembled, separator):
    factor_ss = jnp.linalg.cholesky(assembled[:separator, :separator])
    solved = lax.linalg.triangular_solve(factor_ss, assembled[:separator, separator:], left_side=True, lower=True)
    factor_rs = solved.T
    update = assembled[separator:, separator:] - product(factor_rs, solved)
    return (factor_ss, factor_rs, update)

def inverse(factor_ss, factor_rs, sigma_rr):
    separator = factor_ss.shape[0]
    identity = jnp.eye(separator, dtype=jnp.float32)
    inverse_ss = lax.linalg.triangular_solve(factor_ss, identity, left_side=True, lower=True)
    coupling = product(factor_rs, inverse_ss)
    sigma_rs = -product(sigma_rr, coupling)
    sigma_ss = product(inverse_ss.T, inverse_ss) - product(coupling.T, sigma_rs)
    upper_rows = jnp.concatenate([sigma_ss, sigma_rs.T], axis=1)
    lower_rows = jnp.concatenate([sigma_rs, sigma_rr], axis=1)
    return jnp.concatenate([upper_rows, lower_rows], axis=0)

def reference(leaf_update, front_entries1, front_entries2, front_entries3, map_leaf, map_mid, map_top):
    members = N_LEAF // 4
    order_one = SEP1 + RUP
    order_two = SEP2 + RUP
    first_level = []
    for node_index in range(4):
        assembled = front_entries1[node_index * order_one:(node_index + 1) * order_one]
        for subtree in range(node_index * members, (node_index + 1) * members):
            piece = leaf_update[subtree * R0:(subtree + 1) * R0]
            assembled = assembled + extend(piece, selector(map_leaf[subtree], order_one // BLK))
        first_level.append(factor(assembled, SEP1))
    second_level = []
    for node_index in range(2):
        assembled = front_entries2[node_index * order_two:(node_index + 1) * order_two]
        assembled = assembled + extend(first_level[2 * node_index][2], selector(map_mid[2 * node_index], order_two // BLK))
        assembled = assembled + extend(first_level[2 * node_index + 1][2], selector(map_mid[2 * node_index + 1], order_two // BLK))
        second_level.append(factor(assembled, SEP2))
    assembled = front_entries3 + extend(second_level[0][2], selector(map_top[0], SEP3 // BLK))
    assembled = assembled + extend(second_level[1][2], selector(map_top[1], SEP3 // BLK))
    factor_top = jnp.linalg.cholesky(assembled)
    sigma_second = []
    for node_index in range(2):
        basis = expand(selector(map_top[node_index], SEP3 // BLK), BLK)
        solved = lax.linalg.triangular_solve(factor_top, basis, left_side=True, lower=True)
        sigma_rr = product(solved.T, solved)
        sigma_second.append(inverse(second_level[node_index][0], second_level[node_index][1], sigma_rr))
    sigma_first = []
    for node_index in range(4):
        sigma_rr = extract(sigma_second[node_index // 2], selector(map_mid[node_index], order_two // BLK))
        sigma_first.append(inverse(first_level[node_index][0], first_level[node_index][1], sigma_rr))
    pieces = []
    for subtree in range(N_LEAF):
        pieces.append(extract(sigma_first[subtree // members], selector(map_leaf[subtree], order_one // BLK)))
    return jnp.concatenate(pieces, axis=0)
```

```python
import functools

import jax
import jax.numpy as jnp
from jax import lax
from jax.experimental import pallas as pl
from jax.experimental.pallas import tpu as pltpu
from jax.sharding import PartitionSpec as P

BLK = 128
SEP1 = 512
SEP2 = 512
SEP3 = 1024
RUP = 512


def partner_2(block, axis, distance):
    count = lax.axis_size(axis)
    route = []
    for low in range(count):
        high = low | 1 << distance
        if high != low and high < count:
            route += [(low, high), (high, low)]
    return lax.ppermute(block, axis, route)


def laid_out(tiles, dim):
    dims = list(tiles.shape[1:])
    dims[dim] *= tiles.shape[0]
    return jnp.moveaxis(tiles, 0, dim).reshape(dims)


def sent_to_all(shard, axis):
    copies = jnp.broadcast_to(shard, (lax.axis_size(axis), *shard.shape))
    return lax.all_to_all(copies, axis, split_axis=0, concat_axis=0, tiled=True)


def gathered_copies(shard, axis, dim):
    return laid_out(sent_to_all(shard, axis), dim)


def side_by_side(arrays, axis, dim, along):
    ends, at = ([], 0)
    for a in arrays[:-1]:
        at += a.shape[along]
        ends.append(at)
    both = jnp.concatenate(arrays, axis=along)
    return tuple(jnp.split(gathered_copies(both, axis, dim), ends, axis=along))


def product(left_side, right_side):
    return jnp.dot(left_side, right_side, precision=lax.Precision.HIGHEST)


def placement(block_list, parent_blocks):
    child_blocks = block_list.shape[0]
    hits = (block_list[:, None] == jnp.arange(parent_blocks, dtype=jnp.int32)[None, :]).astype(
        jnp.int32
    )
    source = jnp.sum(hits * jnp.arange(child_blocks, dtype=jnp.int32)[:, None], axis=0)
    present = jnp.sum(hits, axis=0).astype(jnp.float32)
    return (source, present)


def extend(update, block_list, parent_blocks):
    child_blocks = block_list.shape[0]
    block_rows = update.shape[0] // child_blocks
    source, present = placement(block_list, parent_blocks)
    blocked = update.reshape(child_blocks, block_rows, child_blocks, block_rows)
    picked_rows = jnp.take(blocked, source, axis=0)
    picked = jnp.take(picked_rows, source, axis=2)
    weight = present[:, None, None, None] * present[None, None, :, None]
    result = picked * weight
    return result.reshape(parent_blocks * block_rows, parent_blocks * block_rows)


F32, BF16 = jnp.float32, jnp.bfloat16


def row_of(x, k):
    return jnp.broadcast_to(x[k : k + 1, :], (8, 128))


def pick_row(x, k):
    return jnp.take_along_axis(x, jnp.full((8, 128), k, jnp.int32), axis=0)


def along(x, lanes):
    return jnp.take_along_axis(x, lanes, axis=1)


def invert(w):
    lane = lax.broadcasted_iota(jnp.int32, (8, 128), 1)
    sub = lax.broadcasted_iota(jnp.int32, (8, 128), 0)
    tiles = [w[8 * i : 8 * i + 8, :] for i in range(16)]
    diagonal = [jnp.where(lane == 8 * i + sub, x, 0.0) for i, x in enumerate(tiles)]
    total = functools.reduce(jnp.add, diagonal)
    across = lax.rsqrt(jnp.broadcast_to(jnp.sum(total, axis=0, keepdims=True), (8, 128)))
    down = [
        lax.rsqrt(jnp.broadcast_to(jnp.sum(x, axis=1, keepdims=True), (8, 128))) for x in diagonal
    ]
    for i in range(16):
        w[8 * i : 8 * i + 8, :] = tiles[i] * down[i] * across

    def panel(p, carry):
        base = 8 * p
        here = pl.ds(pl.multiple_of(base, 8), 8)
        tiles = [w[8 * i : 8 * i + 8, :] for i in range(16)]
        pivot = w[here, :]
        for k in range(0, 8, 2):
            c = jnp.full((8, 128), base + k, jnp.int32)
            at_first, at_second = lane == c, lane == c + 1
            hit = at_first | at_second
            first, second = along(pivot, c), along(pivot, c + 1)
            a, b, d = pick_row(first, k), pick_row(first, k + 1), pick_row(second, k + 1)
            upper = jnp.where(at_first, -1.0, jnp.where(at_second, 0.0, row_of(pivot, k)))
            lower = jnp.where(at_second, -1.0, jnp.where(at_first, 0.0, row_of(pivot, k + 1)))
            scale = 1.0 / (a * d - b * b)
            new_first = (d * upper - b * lower) * scale
            new_second = (a * lower - b * upper) * scale
            tiles = [
                jnp.where(hit, 0.0, x) - along(x, c) * new_first - along(x, c + 1) * new_second
                for x in tiles
            ]
            pivot = jnp.where(hit, 0.0, pivot) - first * new_first - second * new_second
            pivot = jnp.where(sub == k, new_first, jnp.where(sub == k + 1, new_second, pivot))
        for i in range(16):
            w[8 * i : 8 * i + 8, :] = tiles[i]
        w[here, :] = pivot
        return carry

    lax.fori_loop(0, 16, panel, 0)
    for i in range(16):
        w[8 * i : 8 * i + 8, :] = -w[8 * i : 8 * i + 8, :] * down[i] * across


def halves(x):
    high = x.astype(BF16)
    return high, (x - high.astype(F32)).astype(BF16)


def put_left(ref, rows, x):
    high, low = halves(x)
    width = x.shape[1]
    ref[rows, :width] = high
    ref[rows, width : 2 * width] = high
    ref[rows, 2 * width : 3 * width] = low
    if ref.shape[1] > 3 * width:
        ref[rows, 3 * width :] = low


def put_right(ref, columns, x):
    high, low = halves(x)
    depth = x.shape[0]
    ref[:depth, columns] = high
    ref[depth : 2 * depth, columns] = low
    ref[2 * depth : 3 * depth, columns] = high
    if ref.shape[0] > 3 * depth:
        ref[3 * depth :, columns] = low


def dot(a, b):
    return jnp.dot(a, b, preferred_element_type=F32)


def eliminate(o, blocks, left, right, small_left, small_right, inverted, new_rows, new_columns):
    n = o.shape[0]
    whole = slice(None)

    def step(j, carry):
        at = pl.ds(pl.multiple_of(j * BLK, BLK), BLK)
        inverted[...] = o[at, at]
        invert(inverted)
        block = inverted[...]
        put_left(small_left, whole, block)
        put_right(small_right, whole, block)
        put_right(right, whole, o[at, :])
        put_left(left, whole, o[:, at])
        new_rows[...] = dot(small_left[...], right[...])

        def column_tile(t, carry):
            these = pl.ds(pl.multiple_of(t * 256, 256), 256)
            new_columns[these, :] = dot(left[these, :], small_right[...])
            return carry

        lax.fori_loop(0, n // 256, column_tile, 0)
        put_right(right, whole, new_rows[...])

        def tile(t, carry):
            these = pl.ds(pl.multiple_of(t * 256, 256), 256)
            o[these, :] = o[these, :] - dot(left[these, :], right[...])
            return carry

        lax.fori_loop(0, n // 256, tile, 0)
        o[:, at] = new_columns[...]
        o[at, :] = new_rows[...]
        o[at, at] = -inverted[...]
        return carry

    lax.fori_loop(0, blocks, step, 0)


def scratch_for(n):
    return [
        pltpu.VMEM((n, 4 * BLK), BF16),
        pltpu.VMEM((4 * BLK, n), BF16),
        pltpu.VMEM((BLK, 4 * BLK), BF16),
        pltpu.VMEM((4 * BLK, BLK), BF16),
        pltpu.VMEM((BLK, BLK), F32),
        pltpu.VMEM((BLK, n), F32),
        pltpu.VMEM((n, BLK), F32),
    ]


def at_block(b):
    return pl.ds(pl.multiple_of(b * BLK, BLK), BLK)


def eliminate_kernel(blocks, a_ref, o_ref, *scratch):
    o_ref[...] = a_ref[...]
    eliminate(o_ref, blocks, *scratch)


def assemble_kernel(blocks, map_ref, entries_ref, first_ref, second_ref, o_ref, *scratch):
    o_ref[...] = entries_ref[...]
    for child, update in enumerate((first_ref, second_ref)):
        for i in range(4):
            for j in range(4):
                rows, columns = at_block(map_ref[child, i]), at_block(map_ref[child, j])
                part = update[i * BLK : (i + 1) * BLK, j * BLK : (j + 1) * BLK]
                o_ref[rows, columns] = o_ref[rows, columns] + part
    eliminate(o_ref, blocks, *scratch)


VMEM_SPEC = pl.BlockSpec(memory_space=pltpu.VMEM)
SMEM_SPEC = pl.BlockSpec(memory_space=pltpu.SMEM)
PARAMS = pltpu.CompilerParams(vmem_limit_bytes=60 * 1024 * 1024)


def eliminated(front, blocks):
    n = front.shape[0]
    return pl.pallas_call(
        functools.partial(eliminate_kernel, blocks),
        out_shape=jax.ShapeDtypeStruct((n, n), F32),
        in_specs=[VMEM_SPEC],
        out_specs=VMEM_SPEC,
        scratch_shapes=scratch_for(n),
        compiler_params=PARAMS,
    )(front)


def assembled_eliminated(maps, entries, first, second, blocks):
    n = entries.shape[0]
    return pl.pallas_call(
        functools.partial(assemble_kernel, blocks),
        out_shape=jax.ShapeDtypeStruct((n, n), F32),
        in_specs=[SMEM_SPEC, VMEM_SPEC, VMEM_SPEC, VMEM_SPEC],
        out_specs=VMEM_SPEC,
        scratch_shapes=scratch_for(n),
        compiler_params=PARAMS,
    )(maps, entries, first, second)


def column_of_inverse(swept, sigma, sigma_left, coupling_left, block, value, value_right, column):
    half = 4 * BLK
    whole = slice(None)

    @pl.when(block < 4)
    def _():
        put_right(value_right, whole, swept[half:, at_block(block)])
        value[...] = -dot(sigma_left[...], value_right[...])
        column[:half, :] = -swept[:half, at_block(block)]

    @pl.when(block >= 4)
    def _():
        value[...] = sigma[:, at_block(block - 4)]
        column[:half, :] = jnp.zeros((half, BLK), F32)

    lower = value[...]
    put_right(value_right, whole, lower)
    column[:half, :] = column[:half, :] - dot(coupling_left[...], value_right[...])
    column[half:, :] = lower


def back_kernel(
    map_ref, one_ref, two_ref, three_ref, o_ref, sigma, sigma_left, coupling_left, value, value_right, column, lower
):
    half = 4 * BLK
    whole = slice(None)
    for i in range(4):
        for j in range(4):
            picked = three_ref[at_block(map_ref[0, i]), at_block(map_ref[0, j])]
            sigma[i * BLK : (i + 1) * BLK, j * BLK : (j + 1) * BLK] = -picked
    put_left(sigma_left, whole, sigma[...])
    put_left(coupling_left, whole, two_ref[:half, half:])

    def step(j, carry):
        column_of_inverse(
            two_ref, sigma, sigma_left, coupling_left, map_ref[1, j], value, value_right, column
        )
        for i in range(4):
            lower[i * BLK : (i + 1) * BLK, at_block(j)] = column[at_block(map_ref[1, i]), :]
        return carry

    lax.fori_loop(0, 4, step, 0)
    put_left(sigma_left, whole, lower[...])
    put_left(coupling_left, whole, one_ref[:half, half:])
    column_of_inverse(
        one_ref, lower, sigma_left, coupling_left, map_ref[3, 0], value, value_right, column
    )
    for i in range(4):
        o_ref[i * BLK : (i + 1) * BLK, :] = column[at_block(map_ref[2, i]), :]


def back_substituted(maps, one, two, three):
    half = 4 * BLK
    return pl.pallas_call(
        back_kernel,
        out_shape=jax.ShapeDtypeStruct((half, BLK), F32),
        in_specs=[SMEM_SPEC, VMEM_SPEC, VMEM_SPEC, VMEM_SPEC],
        out_specs=VMEM_SPEC,
        scratch_shapes=[
            pltpu.VMEM((half, half), F32),
            pltpu.VMEM((half, 3 * half), BF16),
            pltpu.VMEM((half, 3 * half), BF16),
            pltpu.VMEM((half, BLK), F32),
            pltpu.VMEM((3 * half, BLK), BF16),
            pltpu.VMEM((2 * half, BLK), F32),
            pltpu.VMEM((half, half), F32),
        ],
        compiler_params=PARAMS,
    )(maps, one, two, three)


def ascended(update, bit_number, entries, maps, child_index, blocks):
    column = lax.axis_index("front")
    width = update.shape[1] // lax.axis_size("front")
    share = lax.dynamic_slice_in_dim(update, column * width, width, 1)
    partner = partner_2(share, "leaf", bit_number)
    mine_full, partner_full = side_by_side((share, partner), "front", 1, 0)
    lower_side = child_index % 2 == 0
    first = jnp.where(lower_side, mine_full, partner_full)
    second = jnp.where(lower_side, partner_full, mine_full)
    pair = lax.dynamic_slice_in_dim(maps, child_index - child_index % 2, 2, 0)
    return assembled_eliminated(pair, entries, first, second, blocks)


def body(leaf_update, front_entries1, front_entries2, front_entries3, map_leaf, map_mid, map_top):
    leaf_index = lax.axis_index("leaf")
    column = lax.axis_index("front")
    members = lax.axis_size("leaf") // 4
    low_bits = members.bit_length() - 1
    first_node = leaf_index // members
    second_node = leaf_index // (2 * members)
    order_one = SEP1 + RUP
    order_two = SEP2 + RUP
    update = gathered_copies(leaf_update, "front", 1)
    leaf_blocks = map_leaf[leaf_index]
    spread = extend(update, leaf_blocks, order_one // BLK)
    share_width = front_entries1.shape[1]
    column_share = lax.dynamic_slice_in_dim(spread, column * share_width, share_width, 1)
    entry_rows = front_entries1.shape[0]
    offset = leaf_index % members * entry_rows
    with_entries = lax.dynamic_slice_in_dim(column_share, offset, entry_rows, 0) + front_entries1
    column_share = lax.dynamic_update_slice_in_dim(column_share, with_entries, offset, 0)
    for bit_number in range(low_bits):
        halfway = column_share.shape[0] // 2
        upper_side = leaf_index >> bit_number & 1 == 1
        kept_rows = jnp.where(upper_side, column_share[halfway:], column_share[:halfway])
        sent_rows = jnp.where(upper_side, column_share[:halfway], column_share[halfway:])
        column_share = kept_rows + partner_2(sent_rows, "leaf", bit_number)
    for bit_number in reversed(range(low_bits)):
        upper_side = leaf_index >> bit_number & 1 == 1
        partner_rows = partner_2(column_share, "leaf", bit_number)
        column_share = jnp.where(
            upper_side,
            jnp.concatenate([partner_rows, column_share], axis=0),
            jnp.concatenate([column_share, partner_rows], axis=0),
        )
    front_one = lax.all_gather(column_share, "front", axis=1, tiled=True)
    one = eliminated(front_one, SEP1 // BLK)
    entries_two = lax.dynamic_slice_in_dim(front_entries2, second_node * order_two, order_two, 0)
    two = ascended(one[SEP1:, SEP1:], low_bits, entries_two, map_mid, first_node, SEP2 // BLK)
    three = ascended(
        two[SEP2:, SEP2:], low_bits + 1, front_entries3, map_top, second_node, SEP3 // BLK
    )
    own = jnp.broadcast_to(leaf_blocks[column], (4,))
    maps = jnp.stack([map_top[second_node], map_mid[first_node], leaf_blocks, own], axis=0)
    return back_substituted(maps, one, two, three)


def solution(mesh):
    in_specs = (P("leaf", "front"), P("leaf", "front"), P(), P(), P(), P(), P())
    out_specs = P("leaf", "front")
    return jax.shard_map(body, mesh=mesh, in_specs=in_specs, out_specs=out_specs, check_vma=False)
```

```python
import functools

import jax
import jax.numpy as jnp
from jax import lax
from jax.experimental import pallas as pl
from jax.experimental.pallas import tpu as pltpu
from jax.sharding import PartitionSpec as P

BLK = 128
SEP1 = 512
SEP2 = 512
SEP3 = 1024
RUP = 512


F32, BF16 = jnp.float32, jnp.bfloat16


def row_of(x, k):
    return jnp.broadcast_to(x[k : k + 1, :], (8, 128))


def pick_row(x, k):
    return jnp.take_along_axis(x, jnp.full((8, 128), k, jnp.int32), axis=0)


def along(x, lanes):
    return jnp.take_along_axis(x, lanes, axis=1)


def invert(w):
    lane = lax.broadcasted_iota(jnp.int32, (8, 128), 1)
    sub = lax.broadcasted_iota(jnp.int32, (8, 128), 0)
    tiles = [w[8 * i : 8 * i + 8, :] for i in range(16)]
    diagonal = [jnp.where(lane == 8 * i + sub, x, 0.0) for i, x in enumerate(tiles)]
    total = functools.reduce(jnp.add, diagonal)
    across = lax.rsqrt(jnp.broadcast_to(jnp.sum(total, axis=0, keepdims=True), (8, 128)))
    down = [
        lax.rsqrt(jnp.broadcast_to(jnp.sum(x, axis=1, keepdims=True), (8, 128))) for x in diagonal
    ]
    for i in range(16):
        w[8 * i : 8 * i + 8, :] = tiles[i] * down[i] * across

    def panel(p, carry):
        base = 8 * p
        here = pl.ds(pl.multiple_of(base, 8), 8)
        tiles = [w[8 * i : 8 * i + 8, :] for i in range(16)]
        pivot = w[here, :]
        for k in range(0, 8, 2):
            c = jnp.full((8, 128), base + k, jnp.int32)
            at_first, at_second = lane == c, lane == c + 1
            hit = at_first | at_second
            first, second = along(pivot, c), along(pivot, c + 1)
            a, b, d = pick_row(first, k), pick_row(first, k + 1), pick_row(second, k + 1)
            upper = jnp.where(at_first, -1.0, jnp.where(at_second, 0.0, row_of(pivot, k)))
            lower = jnp.where(at_second, -1.0, jnp.where(at_first, 0.0, row_of(pivot, k + 1)))
            scale = 1.0 / (a * d - b * b)
            new_first = (d * upper - b * lower) * scale
            new_second = (a * lower - b * upper) * scale
            tiles = [
                jnp.where(hit, 0.0, x) - along(x, c) * new_first - along(x, c + 1) * new_second
                for x in tiles
            ]
            pivot = jnp.where(hit, 0.0, pivot) - first * new_first - second * new_second
            pivot = jnp.where(sub == k, new_first, jnp.where(sub == k + 1, new_second, pivot))
        for i in range(16):
            w[8 * i : 8 * i + 8, :] = tiles[i]
        w[here, :] = pivot
        return carry

    lax.fori_loop(0, 16, panel, 0)
    for i in range(16):
        w[8 * i : 8 * i + 8, :] = -w[8 * i : 8 * i + 8, :] * down[i] * across


def halves(x):
    high = x.astype(BF16)
    return high, (x - high.astype(F32)).astype(BF16)


def put_left(ref, rows, x):
    high, low = halves(x)
    width = x.shape[1]
    ref[rows, :width] = high
    ref[rows, width : 2 * width] = high
    ref[rows, 2 * width : 3 * width] = low
    if ref.shape[1] > 3 * width:
        ref[rows, 3 * width :] = low


def put_right(ref, columns, x):
    high, low = halves(x)
    depth = x.shape[0]
    ref[:depth, columns] = high
    ref[depth : 2 * depth, columns] = low
    ref[2 * depth : 3 * depth, columns] = high
    if ref.shape[0] > 3 * depth:
        ref[3 * depth :, columns] = low


def dot(a, b):
    return jnp.dot(a, b, preferred_element_type=F32)


def eliminate(o, blocks, left, right, small_left, small_right, inverted, new_rows, new_columns):
    n = o.shape[0]
    whole = slice(None)

    def step(j, carry):
        at = pl.ds(pl.multiple_of(j * BLK, BLK), BLK)
        inverted[...] = o[at, at]
        invert(inverted)
        block = inverted[...]
        put_left(small_left, whole, block)
        put_right(small_right, whole, block)
        put_right(right, whole, o[at, :])
        put_left(left, whole, o[:, at])
        new_rows[...] = dot(small_left[...], right[...])

        def column_tile(t, carry):
            these = pl.ds(pl.multiple_of(t * 256, 256), 256)
            new_columns[these, :] = dot(left[these, :], small_right[...])
            return carry

        lax.fori_loop(0, n // 256, column_tile, 0)
        put_right(right, whole, new_rows[...])

        def tile(t, carry):
            these = pl.ds(pl.multiple_of(t * 256, 256), 256)
            o[these, :] = o[these, :] - dot(left[these, :], right[...])
            return carry

        lax.fori_loop(0, n // 256, tile, 0)
        o[:, at] = new_columns[...]
        o[at, :] = new_rows[...]
        o[at, at] = -inverted[...]
        return carry

    lax.fori_loop(0, blocks, step, 0)


def scratch_for(n):
    return [
        pltpu.VMEM((n, 4 * BLK), BF16),
        pltpu.VMEM((4 * BLK, n), BF16),
        pltpu.VMEM((BLK, 4 * BLK), BF16),
        pltpu.VMEM((4 * BLK, BLK), BF16),
        pltpu.VMEM((BLK, BLK), F32),
        pltpu.VMEM((BLK, n), F32),
        pltpu.VMEM((n, BLK), F32),
    ]


def at_block(b):
    return pl.ds(pl.multiple_of(b * BLK, BLK), BLK)


LOWER = [(a, b) for y in range(4) for a in (y, 7 - y) for b in range(a + 1)]
SHARE = [(i, j) for i in range(4) for j in range(i + 1)]


def pack_update(o, tri):
    for t, (i, j) in enumerate(SHARE):
        tri[t * BLK : (t + 1) * BLK, :] = o[
            SEP1 + i * BLK : SEP1 + (i + 1) * BLK, SEP1 + j * BLK : SEP1 + (j + 1) * BLK
        ]


def first_kernel(blocks, lower_ref, o_ref, tri_ref, *scratch):
    for t, (a, b) in enumerate(LOWER):
        part = lower_ref[t]
        o_ref[a * BLK : (a + 1) * BLK, b * BLK : (b + 1) * BLK] = part
        if a != b:
            o_ref[b * BLK : (b + 1) * BLK, a * BLK : (a + 1) * BLK] = part.T
    eliminate(o_ref, blocks, *scratch)
    pack_update(o_ref, tri_ref)


def add_child(o_ref, update, maps, child):
    for t, (i, j) in enumerate(SHARE):
        rows, columns = at_block(maps[child, i]), at_block(maps[child, j])
        part = update[t * BLK : (t + 1) * BLK, :]
        o_ref[rows, columns] = o_ref[rows, columns] + part
        if i != j:
            o_ref[columns, rows] = o_ref[columns, rows] + part.T


def next_kernel(blocks, packs, map_ref, entries_ref, mine_ref, other_ref, o_ref, *rest):
    tri_ref, rest = (rest[0], rest[1:]) if packs else (None, rest)
    copied, scratch = rest[0], rest[1:]
    n = o_ref.shape[0]
    start = pl.multiple_of(map_ref[2, 0] * n, 8)
    fetch = pltpu.make_async_copy(entries_ref.at[pl.ds(start, n), :], o_ref, copied)
    fetch.start()
    fetch.wait()
    add_child(o_ref, mine_ref, map_ref, 0)
    add_child(o_ref, other_ref, map_ref, 1)
    eliminate(o_ref, blocks, *scratch)
    if packs:
        pack_update(o_ref, tri_ref)


def remote(source, target, sent, received, leaf, front):
    return pltpu.make_async_remote_copy(
        src_ref=source,
        dst_ref=target,
        send_sem=sent,
        recv_sem=received,
        device_id=(leaf, front),
        device_id_type=pl.DeviceIdType.MESH,
    )


def greet(devices):
    barrier = pltpu.get_barrier_semaphore()
    for device in devices:
        pl.semaphore_signal(
            barrier, inc=1, device_id=device, device_id_type=pl.DeviceIdType.MESH
        )
    pl.semaphore_wait(barrier, len(devices))


def exchange_kernel(distance, tri_ref, o_ref, sent, got):
    leaf, y = lax.axis_index("leaf"), lax.axis_index("front")
    core, x = leaf % 2, (leaf // 2) % 4
    z = leaf // 8
    sibling = leaf + distance * (1 - 2 * ((leaf // distance) % 2))
    other_core = leaf + 1 - 2 * core
    rows = tri_ref.shape[0] // 32

    def in_x(d):
        return z * 8 + ((x + d) % 4) * 2 + core

    greet(
        [(sibling, y), (other_core, y)]
        + [(leaf, (y + d) % 4) for d in (1, 2, 3)]
        + [(in_x(d), y) for d in (1, 2, 3)]
    )

    def share(c, xx, yy):
        return pl.ds(pl.multiple_of(((c * 4 + xx) * 4 + yy) * rows, 8), rows)

    def row(c, xx):
        return pl.ds(pl.multiple_of((c * 4 + xx) * 4 * rows, 8), 4 * rows)

    mine = share(core, x, y)
    across = remote(tri_ref.at[mine], o_ref.at[mine], sent.at[0], got.at[0], sibling, y)
    across.start()
    across.wait_recv()
    spread = [
        remote(o_ref.at[mine], o_ref.at[mine], sent.at[d], got.at[d], leaf, (y + d) % 4)
        for d in (1, 2, 3)
    ]
    for copy in spread:
        copy.start()
    for copy in spread:
        copy.wait_recv()
    whole = row(core, x)
    wide = [
        remote(o_ref.at[whole], o_ref.at[whole], sent.at[3 + d], got.at[3 + d], in_x(d), y)
        for d in (1, 2, 3)
    ]
    for copy in wide:
        copy.start()
    last = []
    for d in (0, 3, 1, 2):
        if d:
            wide[d - 1].wait_recv()
        piece = row(core, (x - d + 4) % 4)
        copy = remote(o_ref.at[piece], o_ref.at[piece], sent.at[7 + d], got.at[7 + d], other_core, y)
        copy.start()
        last.append(copy)
    for copy in last:
        copy.wait_recv()
    for copy in [across] + spread + wide + last:
        copy.wait_send()


def gather_kernel(
    table_ref, leaf_ref, entries_ref, o_ref,
    met, partial, halves_in, own_entries,
    keep, sent, got, sent_e, got_e, sent_y, got_y, sent_x, got_x, sent_c, got_c,
):
    leaf, y = lax.axis_index("leaf"), lax.axis_index("front")
    m = leaf % 16
    base = leaf - m
    core, x, z = m % 2, (m // 2) % 4, m // 8
    me = m * 4 + y
    barrier = pltpu.get_barrier_semaphore()

    def meet(d, carry):
        other = (me + d) % 64
        pl.semaphore_signal(
            barrier,
            inc=1,
            device_id=(base + other // 4, other % 4),
            device_id_type=pl.DeviceIdType.MESH,
        )
        return carry

    lax.fori_loop(1, 64, meet, 0)
    met[:, 4] = jnp.zeros((16, 8, BLK), F32)
    pl.semaphore_wait(barrier, 63)

    kept = pltpu.make_async_copy(leaf_ref.at[:, m], met.at[m, 0:4], keep.at[0])
    kept.start()
    members = []
    for d in range(1, 16):
        to = (m + d) % 16
        members.append(
            remote(leaf_ref.at[:, to], met.at[m, 0:4], sent.at[d], got.at[d], base + to, y)
        )
        members[-1].start()
    a, half = m // 2, m % 2
    high = a // 4
    target_y = a + high * (7 - 2 * a)
    wide = pl.ds(pl.multiple_of(y * 256, 256), 256)
    for g in range(8):
        to = half * 8 + g
        source = entries_ref.at[pl.ds(8 * g, 8), :]
        target = own_entries.at[high, :, wide]
        stays = jnp.logical_and(to == m, target_y == y)

        @pl.when(stays)
        def _():
            copy = pltpu.make_async_copy(source, target, got_e.at[high, y])
            copy.start()

        @pl.when(jnp.logical_not(stays))
        def _():
            remote(
                source, target, sent_e.at[g], got_e.at[high, y], base + to, target_y
            ).start()

    kept.wait()
    for copy in members:
        copy.wait_recv()

    def sum_block(t, carry):
        total = met[table_ref[t, 0] // 5, table_ref[t, 0] % 5]
        for s in range(1, 16):
            index = table_ref[t, s]
            total = total + met[index // 5, index % 5]
        partial[t] = total
        return carry

    lax.fori_loop(0, 36, sum_block, 0)
    to_sum = []
    for d in (1, 2, 3):
        to = (y + d) % 4
        to_sum.append(
            remote(
                partial.at[pl.ds(9 * to, 9)], halves_in.at[d - 1],
                sent_y.at[d - 1], got_y.at[d - 1], leaf, to,
            )
        )
        to_sum[-1].start()
    for h in range(2):
        for c in range(4):
            pltpu.make_async_copy(
                entries_ref.at[pl.ds(0, 8), :],
                own_entries.at[h, :, pl.ds(c * 256, 256)],
                got_e.at[h, c],
            ).wait()
    for copy in to_sum:
        copy.wait_recv()
    rows = pl.ds(pl.multiple_of(m * 8, 8), 8)
    for t in range(9):
        second = (t + 8 - y) // 9
        b = t - second * (y + 1)
        entry = own_entries[second, :, pl.ds(pl.multiple_of(b * BLK, BLK), BLK)]
        value = partial[9 * y + t] + halves_in[0, t] + halves_in[1, t] + halves_in[2, t]
        o_ref[9 * y + t, rows, :] = value + entry
    spread = []
    own = o_ref.at[pl.ds(9 * y, 9), rows, :]
    for d in (1, 2, 3):
        spread.append(
            remote(own, own, sent_y.at[2 + d], got_y.at[2 + d], leaf, (y + d) % 4)
        )
        spread[-1].start()
    for copy in spread:
        copy.wait_recv()

    other_z = base + (m + 8) % 16
    other_core = base + m + 1 - 2 * core

    def piece(xx, zz, part):
        slot = pl.ds(pl.multiple_of((zz * 8 + xx * 2 + core) * 8, 8), 8)
        return o_ref.at[18 * part : 18 * part + 18, slot, :]

    def step_x(xx, zz, part, direction, slot):
        to = base + z * 8 + ((x + direction + 4) % 4) * 2 + core
        ref = piece(xx, zz, part)
        return remote(ref, ref, sent_x.at[slot], got_x.at[slot], to, y)

    def to_core(xx, zz, part, slot):
        ref = piece(xx, zz, part)
        return remote(ref, ref, sent_c.at[slot], got_c.at[slot], other_core, y)

    started = []

    def begin(copy):
        copy.start()
        started.append(copy)
        return copy

    left, right, far = (x + 3) % 4, (x + 1) % 4, (x + 2) % 4
    other = 1 - z
    over_z = []
    for part in range(2):
        ref = piece(x, z, part)
        over_z.append(begin(remote(ref, ref, sent_y.at[6 + part], got_y.at[6 + part], other_z, y)))
    passes, cores = [], []
    for stage, zz in ((0, z), (1, other)):
        if stage:
            for copy in over_z:
                copy.wait_recv()
        s = 6 * stage
        passes.append(
            [begin(step_x(x, zz, part, 1, s + part)) for part in range(2)]
            + [begin(step_x(x, zz, part, -1, s + 2 + part)) for part in range(2)]
        )
        for part in range(2):
            cores.append(begin(to_core(x, zz, part, 8 * stage + part)))
    for stage, zz in ((0, z), (1, other)):
        s = 6 * stage
        c = 8 * stage
        moves = passes[stage]
        moves[0].wait_recv()
        relay_right = begin(step_x(left, zz, 0, 1, s + 4))
        cores.append(begin(to_core(left, zz, 0, c + 2)))
        moves[3].wait_recv()
        relay_left = begin(step_x(right, zz, 1, -1, s + 5))
        cores.append(begin(to_core(right, zz, 1, c + 3)))
        moves[1].wait_recv()
        cores.append(begin(to_core(left, zz, 1, c + 4)))
        moves[2].wait_recv()
        cores.append(begin(to_core(right, zz, 0, c + 5)))
        passes.append((relay_right, relay_left))
    for stage, zz in ((0, z), (1, other)):
        relay_right, relay_left = passes[2 + stage]
        c = 8 * stage
        relay_right.wait_recv()
        cores.append(begin(to_core(far, zz, 0, c + 6)))
        relay_left.wait_recv()
        cores.append(begin(to_core(far, zz, 1, c + 7)))
    for copy in cores:
        copy.wait_recv()
    for copy in members + to_sum + spread + started:
        copy.wait_send()
    for g in range(8):
        to = half * 8 + g

        @pl.when(jnp.logical_not(jnp.logical_and(to == m, target_y == y)))
        def _():
            remote(
                entries_ref.at[pl.ds(8 * g, 8), :], own_entries.at[high, :, wide],
                sent_e.at[g], got_e.at[high, y], base + to, target_y,
            ).wait_send()


VMEM_SPEC = pl.BlockSpec(memory_space=pltpu.VMEM)
SMEM_SPEC = pl.BlockSpec(memory_space=pltpu.SMEM)
PARAMS = pltpu.CompilerParams(vmem_limit_bytes=60 * 1024 * 1024)


def gathered(table, leaf_update, entries):
    dma = pltpu.SemaphoreType.DMA
    return pl.pallas_call(
        gather_kernel,
        out_shape=jax.ShapeDtypeStruct((36, BLK, BLK), F32),
        in_specs=[SMEM_SPEC, VMEM_SPEC, VMEM_SPEC],
        out_specs=VMEM_SPEC,
        scratch_shapes=[
            pltpu.VMEM((16, 5, 8, BLK), F32),
            pltpu.VMEM((36, 8, BLK), F32),
            pltpu.VMEM((3, 9, 8, BLK), F32),
            pltpu.VMEM((2, 8, 1024), F32),
            dma((1,)), dma((16,)), dma((16,)), dma((8,)), dma((2, 4)), dma((8,)), dma((8,)),
            dma((12,)), dma((12,)), dma((16,)), dma((16,)),
        ],
        compiler_params=pltpu.CompilerParams(
            vmem_limit_bytes=32 * 1024 * 1024, collective_id=0, has_side_effects=True
        ),
    )(table, leaf_update.reshape(4, 16, 8, BLK), entries)


def exchanged(tri, distance, collective_id):
    dma = pltpu.SemaphoreType.DMA
    return pl.pallas_call(
        functools.partial(exchange_kernel, distance),
        out_shape=jax.ShapeDtypeStruct(tri.shape, F32),
        in_specs=[VMEM_SPEC],
        out_specs=VMEM_SPEC,
        scratch_shapes=[dma((11,)), dma((11,))],
        compiler_params=pltpu.CompilerParams(
            vmem_limit_bytes=16 * 1024 * 1024, collective_id=collective_id, has_side_effects=True
        ),
    )(tri)


def first_eliminated(lower, blocks):
    n = 8 * BLK
    return pl.pallas_call(
        functools.partial(first_kernel, blocks),
        out_shape=(
            jax.ShapeDtypeStruct((n, n), F32),
            jax.ShapeDtypeStruct((10 * BLK, BLK), F32),
        ),
        in_specs=[VMEM_SPEC],
        out_specs=(VMEM_SPEC, VMEM_SPEC),
        scratch_shapes=scratch_for(n),
        compiler_params=PARAMS,
    )(lower)


def next_eliminated(maps, entries, mine, other, blocks, packs):
    n = 8 * BLK
    out = [jax.ShapeDtypeStruct((n, n), F32)]
    if packs:
        out.append(jax.ShapeDtypeStruct((10 * BLK, BLK), F32))
    return pl.pallas_call(
        functools.partial(next_kernel, blocks, packs),
        out_shape=tuple(out),
        in_specs=[SMEM_SPEC, pl.BlockSpec(memory_space=pl.ANY), VMEM_SPEC, VMEM_SPEC],
        out_specs=tuple([VMEM_SPEC] * len(out)),
        scratch_shapes=[pltpu.SemaphoreType.DMA] + scratch_for(n),
        compiler_params=PARAMS,
    )(maps, entries, mine, other)


def column_of_inverse(swept, sigma, sigma_left, coupling_left, block, value, value_right, column):
    half = 4 * BLK
    whole = slice(None)

    @pl.when(block < 4)
    def _():
        put_right(value_right, whole, swept[half:, at_block(block)])
        value[...] = -dot(sigma_left[...], value_right[...])
        column[:half, :] = -swept[:half, at_block(block)]

    @pl.when(block >= 4)
    def _():
        value[...] = sigma[:, at_block(block - 4)]
        column[:half, :] = jnp.zeros((half, BLK), F32)

    lower = value[...]
    put_right(value_right, whole, lower)
    column[:half, :] = column[:half, :] - dot(coupling_left[...], value_right[...])
    column[half:, :] = lower


def back_kernel(
    map_ref, one_ref, two_ref, three_ref, o_ref, sigma, sigma_left, coupling_left, value, value_right, column, lower
):
    half = 4 * BLK
    whole = slice(None)
    for i in range(4):
        for j in range(4):
            picked = three_ref[at_block(map_ref[0, i]), at_block(map_ref[0, j])]
            sigma[i * BLK : (i + 1) * BLK, j * BLK : (j + 1) * BLK] = -picked
    put_left(sigma_left, whole, sigma[...])
    put_left(coupling_left, whole, two_ref[:half, half:])

    def step(j, carry):
        column_of_inverse(
            two_ref, sigma, sigma_left, coupling_left, map_ref[1, j], value, value_right, column
        )
        for i in range(4):
            lower[i * BLK : (i + 1) * BLK, at_block(j)] = column[at_block(map_ref[1, i]), :]
        return carry

    lax.fori_loop(0, 4, step, 0)
    put_left(sigma_left, whole, lower[...])
    put_left(coupling_left, whole, one_ref[:half, half:])
    column_of_inverse(
        one_ref, lower, sigma_left, coupling_left, map_ref[3, 0], value, value_right, column
    )
    for i in range(4):
        o_ref[i * BLK : (i + 1) * BLK, :] = column[at_block(map_ref[2, i]), :]


def back_substituted(maps, one, two, three):
    half = 4 * BLK
    return pl.pallas_call(
        back_kernel,
        out_shape=jax.ShapeDtypeStruct((half, BLK), F32),
        in_specs=[SMEM_SPEC, VMEM_SPEC, VMEM_SPEC, VMEM_SPEC],
        out_specs=VMEM_SPEC,
        scratch_shapes=[
            pltpu.VMEM((half, half), F32),
            pltpu.VMEM((half, 3 * half), BF16),
            pltpu.VMEM((half, 3 * half), BF16),
            pltpu.VMEM((half, BLK), F32),
            pltpu.VMEM((3 * half, BLK), BF16),
            pltpu.VMEM((2 * half, BLK), F32),
            pltpu.VMEM((half, half), F32),
        ],
        compiler_params=PARAMS,
    )(maps, one, two, three)


def with_place(maps, child, place):
    sibling = child + 1 - 2 * (child % 2)
    return jnp.stack([maps[child], maps[sibling], jnp.broadcast_to(place, (4,))], axis=0)


def body(leaf_update, front_entries1, front_entries2, front_entries3, map_leaf, map_mid, map_top):
    leaf_index = lax.axis_index("leaf")
    column = lax.axis_index("front")
    members = lax.axis_size("leaf") // 4
    first_node = leaf_index // members
    second_node = leaf_index // (2 * members)
    below = lax.dynamic_slice_in_dim(map_leaf, first_node * members, members, 0)
    rows = jnp.array([a for a, _ in LOWER], jnp.int32)[:, None]
    columns = jnp.array([b for _, b in LOWER], jnp.int32)[:, None]
    found = jnp.full((len(LOWER), members), 4, jnp.int32)
    for i in range(4):
        found = jnp.where(rows == below[:, i][None, :], i, found)
    landing = lax.dynamic_index_in_dim(below, column, 1, keepdims=False)
    found = jnp.where(columns == landing[None, :], found, 4)
    table = found + 5 * jnp.arange(members, dtype=jnp.int32)[None, :]
    lower = gathered(table, leaf_update, front_entries1)
    one, update = first_eliminated(lower, SEP1 // BLK)
    other = exchanged(update, members, 1)
    two, update = next_eliminated(
        with_place(map_mid, first_node, second_node), front_entries2, update, other, SEP2 // BLK, True
    )
    other = exchanged(update, 2 * members, 2)
    (three,) = next_eliminated(
        with_place(map_top, second_node, 0), front_entries3, update, other, SEP3 // BLK, False
    )
    leaf_blocks = map_leaf[leaf_index]
    own = jnp.broadcast_to(leaf_blocks[column], (4,))
    maps = jnp.stack([map_top[second_node], map_mid[first_node], leaf_blocks, own], axis=0)
    return back_substituted(maps, one, two, three)


def solution(mesh):
    in_specs = (P("leaf", "front"), P("leaf", "front"), P(), P(), P(), P(), P())
    out_specs = P("leaf", "front")
    return jax.shard_map(body, mesh=mesh, in_specs=in_specs, out_specs=out_specs, check_vma=False)
```

```python
import functools

import jax
import jax.numpy as jnp
from jax import lax
from jax.experimental import pallas as pl
from jax.experimental.pallas import tpu as pltpu
from jax.sharding import PartitionSpec as P

BLK = 128
SEP1 = 512
SEP2 = 512
SEP3 = 1024
RUP = 512


F32, BF16 = jnp.float32, jnp.bfloat16


def row_of(x, k):
    return jnp.broadcast_to(x[k : k + 1, :], (8, 128))


def along(x, c):
    return jnp.take_along_axis(x, jnp.full((8, 128), c, jnp.int32), axis=1)


def thirds(x):
    high = x.astype(BF16)
    rest = x - high.astype(F32)
    middle = rest.astype(BF16)
    return high, middle, (rest - middle.astype(F32)).astype(BF16)


def outer(p, s):
    ph, pm, pl_ = thirds(p)
    sh, sm, sl = thirds(s)
    left = jnp.concatenate([ph, ph, ph, pm, pm, pl_], axis=0)
    right = jnp.concatenate([sh, sm, sl, sh, sm, sh], axis=0)
    return lax.dot_general(left, right, (((0,), (0,)), ((), ())), preferred_element_type=F32)


def swept_rows(rows, base, lane, sub):
    e = [along(rows, base + j) for j in range(8)]
    inside = (lane >= base) & (lane < base + 8)
    m = jnp.where(lane == base + sub, -1.0, jnp.where(inside, 0.0, rows))
    for k in range(0, 8, 2):
        a, b, d = row_of(e[k], k), row_of(e[k + 1], k), row_of(e[k + 1], k + 1)
        scale = 1.0 / (a * d - b * b)
        first, cross, second = d * scale, b * scale, a * scale

        def go(t):
            upper, lower = row_of(t, k), row_of(t, k + 1)
            new_upper = first * upper - cross * lower
            new_lower = second * lower - cross * upper
            y = t - (e[k] * new_upper + e[k + 1] * new_lower)
            return jnp.where(sub == k, new_upper, jnp.where(sub == k + 1, new_lower, y))

        m = go(m)
        e = [go(x) if j > k + 1 else x for j, x in enumerate(e)]
    return m


def less_pivots(x, base, rows, inside):
    total = None
    for k in range(0, 8, 2):
        term = along(x, base + k) * rows[k] + along(x, base + k + 1) * rows[k + 1]
        total = term if total is None else total + term
    return jnp.where(inside, 0.0, x) - total


def invert(w):
    lane = lax.broadcasted_iota(jnp.int32, (8, 128), 1)
    sub = lax.broadcasted_iota(jnp.int32, (8, 128), 0)
    lanes = lax.broadcasted_iota(jnp.int32, (128, 128), 1)
    tiles = [w[8 * i : 8 * i + 8, :] for i in range(16)]
    diagonal = [jnp.where(lane == 8 * i + sub, x, 0.0) for i, x in enumerate(tiles)]
    total = functools.reduce(jnp.add, diagonal)
    across = lax.rsqrt(jnp.broadcast_to(jnp.sum(total, axis=0, keepdims=True), (8, 128)))
    down = [
        lax.rsqrt(jnp.broadcast_to(jnp.sum(x, axis=1, keepdims=True), (8, 128))) for x in diagonal
    ]
    for i in range(16):
        w[8 * i : 8 * i + 8, :] = tiles[i] * down[i] * across

    def at(t):
        return pl.ds(pl.multiple_of(8 * t, 8), 8)

    def panel(p, carry):
        rows, before, rows_before = carry
        base = 8 * p
        base_before = (base + 120) % 128
        inside_before = (lane >= base - 8) & (lane < base)
        following = w[at((p + 1) % 16), :]
        now = swept_rows(rows, base, lane, sub)
        following = less_pivots(
            following, base_before, [row_of(before, k) for k in range(8)], inside_before
        )
        following = less_pivots(
            following,
            base,
            [row_of(now, k) for k in range(8)],
            (lane >= base) & (lane < base + 8),
        )
        gone = (lanes >= base - 8) & (lanes < base)
        w[...] = jnp.where(gone, 0.0, w[...]) - outer(rows_before, before)

        @pl.when(p > 0)
        def _():
            w[at(p - 1), :] = before

        return following, now, rows

    zero = jnp.zeros((8, 128), F32)
    _, last, rows = lax.fori_loop(0, 16, panel, (w[0:8, :], zero, zero))
    w[...] = jnp.where(lanes >= 120, 0.0, w[...]) - outer(rows, last)
    w[120:128, :] = last
    for i in range(16):
        w[8 * i : 8 * i + 8, :] = -w[8 * i : 8 * i + 8, :] * down[i] * across


def halves(x):
    high = x.astype(BF16)
    return high, (x - high.astype(F32)).astype(BF16)


def put_left(ref, rows, x):
    high, low = halves(x)
    width = x.shape[1]
    ref[rows, :width] = high
    ref[rows, width : 2 * width] = high
    ref[rows, 2 * width : 3 * width] = low
    if ref.shape[1] > 3 * width:
        ref[rows, 3 * width :] = low


def put_right(ref, columns, x):
    high, low = halves(x)
    depth = x.shape[0]
    ref[:depth, columns] = high
    ref[depth : 2 * depth, columns] = low
    ref[2 * depth : 3 * depth, columns] = high
    if ref.shape[0] > 3 * depth:
        ref[3 * depth :, columns] = low


def dot(a, b):
    return jnp.dot(a, b, preferred_element_type=F32)


def eliminate(o, blocks, left, right, small_right, inverted):
    n = o.shape[0]
    whole = slice(None)
    eye = (
        lax.broadcasted_iota(jnp.int32, (BLK, BLK), 0)
        == lax.broadcasted_iota(jnp.int32, (BLK, BLK), 1)
    )

    def step(j, carry):
        at = pl.ds(pl.multiple_of(j * BLK, BLK), BLK)
        inverted[...] = o[at, at]
        put_right(right, whole, o[at, :])
        put_right(right, at, jnp.where(eye, -1.0, 0.0))
        put_left(left, whole, o[:, at])
        invert(inverted)
        put_right(small_right, whole, inverted[...])
        for t in range(0, n, 256):
            put_left(left, slice(t, t + 256), dot(left[t : t + 256, :], small_right[...]))
        put_left(left, at, -inverted[...])
        o[at, :] = jnp.zeros((BLK, n), F32)
        o[:, at] = jnp.zeros((n, BLK), F32)

        def tile(t, carry):
            these = pl.ds(pl.multiple_of(t * 512, 512), 512)
            o[these, :] = o[these, :] - dot(left[these, :], right[...])
            return carry

        lax.fori_loop(0, n // 512, tile, 0)
        return carry

    lax.fori_loop(0, blocks, step, 0)


def scratch_for(n):
    return [
        pltpu.VMEM((n, 4 * BLK), BF16),
        pltpu.VMEM((4 * BLK, n), BF16),
        pltpu.VMEM((4 * BLK, BLK), BF16),
        pltpu.VMEM((BLK, BLK), F32),
    ]


def at_block(b):
    return pl.ds(pl.multiple_of(b * BLK, BLK), BLK)


LOWER = [(a, b) for y in range(4) for a in (y, 7 - y) for b in range(a + 1)]
SHARE = [(i, j) for i in range(4) for j in range(i + 1)]


def pack_update(o, tri):
    for t, (i, j) in enumerate(SHARE):
        tri[t * BLK : (t + 1) * BLK, :] = o[
            SEP1 + i * BLK : SEP1 + (i + 1) * BLK, SEP1 + j * BLK : SEP1 + (j + 1) * BLK
        ]


def first_kernel(blocks, lower_ref, o_ref, tri_ref, *scratch):
    for t, (a, b) in enumerate(LOWER):
        part = lower_ref[t]
        o_ref[a * BLK : (a + 1) * BLK, b * BLK : (b + 1) * BLK] = part
        if a != b:
            o_ref[b * BLK : (b + 1) * BLK, a * BLK : (a + 1) * BLK] = part.T
    eliminate(o_ref, blocks, *scratch)
    pack_update(o_ref, tri_ref)


def add_child(o_ref, update, maps, child):
    for t, (i, j) in enumerate(SHARE):
        rows, columns = at_block(maps[child, i]), at_block(maps[child, j])
        part = update[t * BLK : (t + 1) * BLK, :]
        o_ref[rows, columns] = o_ref[rows, columns] + part
        if i != j:
            o_ref[columns, rows] = o_ref[columns, rows] + part.T


def next_kernel(blocks, packs, map_ref, entries_ref, mine_ref, other_ref, o_ref, *rest):
    tri_ref, rest = (rest[0], rest[1:]) if packs else (None, rest)
    copied, scratch = rest[0], rest[1:]
    n = o_ref.shape[0]
    start = pl.multiple_of(map_ref[2, 0] * n, 8)
    fetch = pltpu.make_async_copy(entries_ref.at[pl.ds(start, n), :], o_ref, copied)
    fetch.start()
    fetch.wait()
    add_child(o_ref, mine_ref, map_ref, 0)
    add_child(o_ref, other_ref, map_ref, 1)
    eliminate(o_ref, blocks, *scratch)
    if packs:
        pack_update(o_ref, tri_ref)


def remote(source, target, sent, received, leaf, front):
    return pltpu.make_async_remote_copy(
        src_ref=source,
        dst_ref=target,
        send_sem=sent,
        recv_sem=received,
        device_id=(leaf, front),
        device_id_type=pl.DeviceIdType.MESH,
    )


def greet(devices):
    barrier = pltpu.get_barrier_semaphore()
    for device in devices:
        pl.semaphore_signal(
            barrier, inc=1, device_id=device, device_id_type=pl.DeviceIdType.MESH
        )
    pl.semaphore_wait(barrier, len(devices))


def exchange_kernel(distance, tri_ref, o_ref, sent, got):
    leaf, y = lax.axis_index("leaf"), lax.axis_index("front")
    core, x = leaf % 2, (leaf // 2) % 4
    z = leaf // 8
    sibling = leaf + distance * (1 - 2 * ((leaf // distance) % 2))
    other_core = leaf + 1 - 2 * core
    rows = tri_ref.shape[0] // 32

    def in_x(d):
        return z * 8 + ((x + d) % 4) * 2 + core

    greet(
        [(sibling, y), (other_core, y)]
        + [(leaf, (y + d) % 4) for d in (1, 2, 3)]
        + [(in_x(d), y) for d in (1, 2, 3)]
    )

    def share(c, xx, yy):
        return pl.ds(pl.multiple_of(((c * 4 + xx) * 4 + yy) * rows, 8), rows)

    def row(c, xx):
        return pl.ds(pl.multiple_of((c * 4 + xx) * 4 * rows, 8), 4 * rows)

    mine = share(core, x, y)
    across = remote(tri_ref.at[mine], o_ref.at[mine], sent.at[0], got.at[0], sibling, y)
    across.start()
    across.wait_recv()
    spread = [
        remote(o_ref.at[mine], o_ref.at[mine], sent.at[d], got.at[d], leaf, (y + d) % 4)
        for d in (1, 2, 3)
    ]
    for copy in spread:
        copy.start()
    for copy in spread:
        copy.wait_recv()
    whole = row(core, x)
    wide = [
        remote(o_ref.at[whole], o_ref.at[whole], sent.at[3 + d], got.at[3 + d], in_x(d), y)
        for d in (1, 2, 3)
    ]
    for copy in wide:
        copy.start()
    last = []
    for d in (0, 3, 1, 2):
        if d:
            wide[d - 1].wait_recv()
        piece = row(core, (x - d + 4) % 4)
        copy = remote(o_ref.at[piece], o_ref.at[piece], sent.at[7 + d], got.at[7 + d], other_core, y)
        copy.start()
        last.append(copy)
    for copy in last:
        copy.wait_recv()
    for copy in [across] + spread + wide + last:
        copy.wait_send()


def gather_kernel(
    table_ref, leaf_ref, entries_ref, o_ref,
    met, partial, halves_in, own_entries,
    keep, sent, got, sent_e, got_e, sent_y, got_y, sent_x, got_x, sent_c, got_c,
):
    leaf, y = lax.axis_index("leaf"), lax.axis_index("front")
    m = leaf % 16
    base = leaf - m
    core, x, z = m % 2, (m // 2) % 4, m // 8
    me = m * 4 + y
    barrier = pltpu.get_barrier_semaphore()

    def meet(d, carry):
        other = (me + d) % 64
        pl.semaphore_signal(
            barrier,
            inc=1,
            device_id=(base + other // 4, other % 4),
            device_id_type=pl.DeviceIdType.MESH,
        )
        return carry

    lax.fori_loop(1, 64, meet, 0)
    met[:, 4] = jnp.zeros((16, 8, BLK), F32)
    pl.semaphore_wait(barrier, 63)

    kept = pltpu.make_async_copy(leaf_ref.at[:, m], met.at[m, 0:4], keep.at[0])
    kept.start()
    members = []
    for d in range(1, 16):
        to = (m + d) % 16
        members.append(
            remote(leaf_ref.at[:, to], met.at[m, 0:4], sent.at[d], got.at[d], base + to, y)
        )
        members[-1].start()
    a, half = m // 2, m % 2
    high = a // 4
    target_y = a + high * (7 - 2 * a)
    wide = pl.ds(pl.multiple_of(y * 256, 256), 256)
    for g in range(8):
        to = half * 8 + g
        source = entries_ref.at[pl.ds(8 * g, 8), :]
        target = own_entries.at[high, :, wide]
        stays = jnp.logical_and(to == m, target_y == y)

        @pl.when(stays)
        def _():
            copy = pltpu.make_async_copy(source, target, got_e.at[high, y])
            copy.start()

        @pl.when(jnp.logical_not(stays))
        def _():
            remote(
                source, target, sent_e.at[g], got_e.at[high, y], base + to, target_y
            ).start()

    kept.wait()
    for copy in members:
        copy.wait_recv()

    def sum_block(t, carry):
        total = met[table_ref[t, 0] // 5, table_ref[t, 0] % 5]
        for s in range(1, 16):
            index = table_ref[t, s]
            total = total + met[index // 5, index % 5]
        partial[t] = total
        return carry

    lax.fori_loop(0, 36, sum_block, 0)
    to_sum = []
    for d in (1, 2, 3):
        to = (y + d) % 4
        to_sum.append(
            remote(
                partial.at[pl.ds(9 * to, 9)], halves_in.at[d - 1],
                sent_y.at[d - 1], got_y.at[d - 1], leaf, to,
            )
        )
        to_sum[-1].start()
    for h in range(2):
        for c in range(4):
            pltpu.make_async_copy(
                entries_ref.at[pl.ds(0, 8), :],
                own_entries.at[h, :, pl.ds(c * 256, 256)],
                got_e.at[h, c],
            ).wait()
    for copy in to_sum:
        copy.wait_recv()
    rows = pl.ds(pl.multiple_of(m * 8, 8), 8)
    for t in range(9):
        second = (t + 8 - y) // 9
        b = t - second * (y + 1)
        entry = own_entries[second, :, pl.ds(pl.multiple_of(b * BLK, BLK), BLK)]
        value = partial[9 * y + t] + halves_in[0, t] + halves_in[1, t] + halves_in[2, t]
        o_ref[9 * y + t, rows, :] = value + entry
    spread = []
    own = o_ref.at[pl.ds(9 * y, 9), rows, :]
    for d in (1, 2, 3):
        spread.append(
            remote(own, own, sent_y.at[2 + d], got_y.at[2 + d], leaf, (y + d) % 4)
        )
        spread[-1].start()
    for copy in spread:
        copy.wait_recv()

    other_z = base + (m + 8) % 16
    other_core = base + m + 1 - 2 * core

    def piece(xx, zz, part):
        slot = pl.ds(pl.multiple_of((zz * 8 + xx * 2 + core) * 8, 8), 8)
        return o_ref.at[18 * part : 18 * part + 18, slot, :]

    def step_x(xx, zz, part, direction, slot):
        to = base + z * 8 + ((x + direction + 4) % 4) * 2 + core
        ref = piece(xx, zz, part)
        return remote(ref, ref, sent_x.at[slot], got_x.at[slot], to, y)

    def to_core(xx, zz, part, slot):
        ref = piece(xx, zz, part)
        return remote(ref, ref, sent_c.at[slot], got_c.at[slot], other_core, y)

    started = []

    def begin(copy):
        copy.start()
        started.append(copy)
        return copy

    left, right, far = (x + 3) % 4, (x + 1) % 4, (x + 2) % 4
    other = 1 - z
    over_z = []
    for part in range(2):
        ref = piece(x, z, part)
        over_z.append(begin(remote(ref, ref, sent_y.at[6 + part], got_y.at[6 + part], other_z, y)))
    passes, cores = [], []
    for stage, zz in ((0, z), (1, other)):
        if stage:
            for copy in over_z:
                copy.wait_recv()
        s = 6 * stage
        passes.append(
            [begin(step_x(x, zz, part, 1, s + part)) for part in range(2)]
            + [begin(step_x(x, zz, part, -1, s + 2 + part)) for part in range(2)]
        )
        for part in range(2):
            cores.append(begin(to_core(x, zz, part, 8 * stage + part)))
    for stage, zz in ((0, z), (1, other)):
        s = 6 * stage
        c = 8 * stage
        moves = passes[stage]
        moves[0].wait_recv()
        relay_right = begin(step_x(left, zz, 0, 1, s + 4))
        cores.append(begin(to_core(left, zz, 0, c + 2)))
        moves[3].wait_recv()
        relay_left = begin(step_x(right, zz, 1, -1, s + 5))
        cores.append(begin(to_core(right, zz, 1, c + 3)))
        moves[1].wait_recv()
        cores.append(begin(to_core(left, zz, 1, c + 4)))
        moves[2].wait_recv()
        cores.append(begin(to_core(right, zz, 0, c + 5)))
        passes.append((relay_right, relay_left))
    for stage, zz in ((0, z), (1, other)):
        relay_right, relay_left = passes[2 + stage]
        c = 8 * stage
        relay_right.wait_recv()
        cores.append(begin(to_core(far, zz, 0, c + 6)))
        relay_left.wait_recv()
        cores.append(begin(to_core(far, zz, 1, c + 7)))
    for copy in cores:
        copy.wait_recv()
    for copy in members + to_sum + spread + started:
        copy.wait_send()
    for g in range(8):
        to = half * 8 + g

        @pl.when(jnp.logical_not(jnp.logical_and(to == m, target_y == y)))
        def _():
            remote(
                entries_ref.at[pl.ds(8 * g, 8), :], own_entries.at[high, :, wide],
                sent_e.at[g], got_e.at[high, y], base + to, target_y,
            ).wait_send()


VMEM_SPEC = pl.BlockSpec(memory_space=pltpu.VMEM)
SMEM_SPEC = pl.BlockSpec(memory_space=pltpu.SMEM)
PARAMS = pltpu.CompilerParams(vmem_limit_bytes=60 * 1024 * 1024)


def gathered(table, leaf_update, entries):
    dma = pltpu.SemaphoreType.DMA
    return pl.pallas_call(
        gather_kernel,
        out_shape=jax.ShapeDtypeStruct((36, BLK, BLK), F32),
        in_specs=[SMEM_SPEC, VMEM_SPEC, VMEM_SPEC],
        out_specs=VMEM_SPEC,
        scratch_shapes=[
            pltpu.VMEM((16, 5, 8, BLK), F32),
            pltpu.VMEM((36, 8, BLK), F32),
            pltpu.VMEM((3, 9, 8, BLK), F32),
            pltpu.VMEM((2, 8, 1024), F32),
            dma((1,)), dma((16,)), dma((16,)), dma((8,)), dma((2, 4)), dma((8,)), dma((8,)),
            dma((12,)), dma((12,)), dma((16,)), dma((16,)),
        ],
        compiler_params=pltpu.CompilerParams(
            vmem_limit_bytes=32 * 1024 * 1024, collective_id=0, has_side_effects=True
        ),
    )(table, leaf_update.reshape(4, 16, 8, BLK), entries)


def exchanged(tri, distance, collective_id):
    dma = pltpu.SemaphoreType.DMA
    return pl.pallas_call(
        functools.partial(exchange_kernel, distance),
        out_shape=jax.ShapeDtypeStruct(tri.shape, F32),
        in_specs=[VMEM_SPEC],
        out_specs=VMEM_SPEC,
        scratch_shapes=[dma((11,)), dma((11,))],
        compiler_params=pltpu.CompilerParams(
            vmem_limit_bytes=16 * 1024 * 1024, collective_id=collective_id, has_side_effects=True
        ),
    )(tri)


def first_eliminated(lower, blocks):
    n = 8 * BLK
    return pl.pallas_call(
        functools.partial(first_kernel, blocks),
        out_shape=(
            jax.ShapeDtypeStruct((n, n), F32),
            jax.ShapeDtypeStruct((10 * BLK, BLK), F32),
        ),
        in_specs=[VMEM_SPEC],
        out_specs=(VMEM_SPEC, VMEM_SPEC),
        scratch_shapes=scratch_for(n),
        compiler_params=PARAMS,
    )(lower)


def next_eliminated(maps, entries, mine, other, blocks, packs):
    n = 8 * BLK
    out = [jax.ShapeDtypeStruct((n, n), F32)]
    if packs:
        out.append(jax.ShapeDtypeStruct((10 * BLK, BLK), F32))
    return pl.pallas_call(
        functools.partial(next_kernel, blocks, packs),
        out_shape=tuple(out),
        in_specs=[SMEM_SPEC, pl.BlockSpec(memory_space=pl.ANY), VMEM_SPEC, VMEM_SPEC],
        out_specs=tuple([VMEM_SPEC] * len(out)),
        scratch_shapes=[pltpu.SemaphoreType.DMA] + scratch_for(n),
        compiler_params=PARAMS,
    )(maps, entries, mine, other)


def column_of_inverse(swept, sigma, sigma_left, coupling_left, block, value, value_right, column):
    half = 4 * BLK
    whole = slice(None)

    @pl.when(block < 4)
    def _():
        put_right(value_right, whole, swept[half:, at_block(block)])
        value[...] = -dot(sigma_left[...], value_right[...])
        column[:half, :] = -swept[:half, at_block(block)]

    @pl.when(block >= 4)
    def _():
        value[...] = sigma[:, at_block(block - 4)]
        column[:half, :] = jnp.zeros((half, BLK), F32)

    lower = value[...]
    put_right(value_right, whole, lower)
    column[:half, :] = column[:half, :] - dot(coupling_left[...], value_right[...])
    column[half:, :] = lower


def back_kernel(
    map_ref, one_ref, two_ref, three_ref, o_ref, sigma, sigma_left, coupling_left, value, value_right, column, lower
):
    half = 4 * BLK
    whole = slice(None)
    for i in range(4):
        for j in range(4):
            picked = three_ref[at_block(map_ref[0, i]), at_block(map_ref[0, j])]
            sigma[i * BLK : (i + 1) * BLK, j * BLK : (j + 1) * BLK] = -picked
    put_left(sigma_left, whole, sigma[...])
    put_left(coupling_left, whole, two_ref[:half, half:])

    def step(j, carry):
        column_of_inverse(
            two_ref, sigma, sigma_left, coupling_left, map_ref[1, j], value, value_right, column
        )
        for i in range(4):
            lower[i * BLK : (i + 1) * BLK, at_block(j)] = column[at_block(map_ref[1, i]), :]
        return carry

    lax.fori_loop(0, 4, step, 0)
    put_left(sigma_left, whole, lower[...])
    put_left(coupling_left, whole, one_ref[:half, half:])
    column_of_inverse(
        one_ref, lower, sigma_left, coupling_left, map_ref[3, 0], value, value_right, column
    )
    for i in range(4):
        o_ref[i * BLK : (i + 1) * BLK, :] = column[at_block(map_ref[2, i]), :]


def back_substituted(maps, one, two, three):
    half = 4 * BLK
    return pl.pallas_call(
        back_kernel,
        out_shape=jax.ShapeDtypeStruct((half, BLK), F32),
        in_specs=[SMEM_SPEC, VMEM_SPEC, VMEM_SPEC, VMEM_SPEC],
        out_specs=VMEM_SPEC,
        scratch_shapes=[
            pltpu.VMEM((half, half), F32),
            pltpu.VMEM((half, 3 * half), BF16),
            pltpu.VMEM((half, 3 * half), BF16),
            pltpu.VMEM((half, BLK), F32),
            pltpu.VMEM((3 * half, BLK), BF16),
            pltpu.VMEM((2 * half, BLK), F32),
            pltpu.VMEM((half, half), F32),
        ],
        compiler_params=PARAMS,
    )(maps, one, two, three)


def with_place(maps, child, place):
    sibling = child + 1 - 2 * (child % 2)
    return jnp.stack([maps[child], maps[sibling], jnp.broadcast_to(place, (4,))], axis=0)


def body(leaf_update, front_entries1, front_entries2, front_entries3, map_leaf, map_mid, map_top):
    leaf_index = lax.axis_index("leaf")
    column = lax.axis_index("front")
    members = lax.axis_size("leaf") // 4
    first_node = leaf_index // members
    second_node = leaf_index // (2 * members)
    below = lax.dynamic_slice_in_dim(map_leaf, first_node * members, members, 0)
    rows = jnp.array([a for a, _ in LOWER], jnp.int32)[:, None]
    columns = jnp.array([b for _, b in LOWER], jnp.int32)[:, None]
    found = jnp.full((len(LOWER), members), 4, jnp.int32)
    for i in range(4):
        found = jnp.where(rows == below[:, i][None, :], i, found)
    landing = lax.dynamic_index_in_dim(below, column, 1, keepdims=False)
    found = jnp.where(columns == landing[None, :], found, 4)
    table = found + 5 * jnp.arange(members, dtype=jnp.int32)[None, :]
    lower = gathered(table, leaf_update, front_entries1)
    one, update = first_eliminated(lower, SEP1 // BLK)
    other = exchanged(update, members, 1)
    two, update = next_eliminated(
        with_place(map_mid, first_node, second_node), front_entries2, update, other, SEP2 // BLK, True
    )
    other = exchanged(update, 2 * members, 2)
    (three,) = next_eliminated(
        with_place(map_top, second_node, 0), front_entries3, update, other, SEP3 // BLK, False
    )
    leaf_blocks = map_leaf[leaf_index]
    own = jnp.broadcast_to(leaf_blocks[column], (4,))
    maps = jnp.stack([map_top[second_node], map_mid[first_node], leaf_blocks, own], axis=0)
    return back_substituted(maps, one, two, three)


def solution(mesh):
    in_specs = (P("leaf", "front"), P("leaf", "front"), P(), P(), P(), P(), P())
    out_specs = P("leaf", "front")
    return jax.shard_map(body, mesh=mesh, in_specs=in_specs, out_specs=out_specs, check_vma=False)
```

```python
import functools

import jax
import jax.numpy as jnp
from jax import lax
from jax.experimental import pallas as pl
from jax.experimental.pallas import tpu as pltpu
from jax.sharding import PartitionSpec as P

BLK = 128
SEP1 = 512
SEP2 = 512
SEP3 = 1024
RUP = 512


F32, BF16 = jnp.float32, jnp.bfloat16


def row_of(x, k):
    return jnp.broadcast_to(x[k : k + 1, :], (8, 128))


def along(x, c):
    return jnp.take_along_axis(x, jnp.full((8, 128), c, jnp.int32), axis=1)


def thirds(x):
    high = x.astype(BF16)
    rest = x - high.astype(F32)
    middle = rest.astype(BF16)
    return high, middle, (rest - middle.astype(F32)).astype(BF16)


def outer(p, s):
    ph, pm, pl_ = thirds(p)
    sh, sm, sl = thirds(s)
    left = jnp.concatenate([ph, ph, ph, pm, pm, pl_], axis=0)
    right = jnp.concatenate([sh, sm, sl, sh, sm, sh], axis=0)
    return lax.dot_general(left, right, (((0,), (0,)), ((), ())), preferred_element_type=F32)


def swept_rows(rows, base, lane, sub):
    e = [along(rows, base + j) for j in range(8)]
    inside = (lane >= base) & (lane < base + 8)
    m = jnp.where(lane == base + sub, -1.0, jnp.where(inside, 0.0, rows))
    for k in range(0, 8, 2):
        a, b, d = row_of(e[k], k), row_of(e[k + 1], k), row_of(e[k + 1], k + 1)
        scale = 1.0 / (a * d - b * b)
        first, cross, second = d * scale, b * scale, a * scale

        def go(t):
            upper, lower = row_of(t, k), row_of(t, k + 1)
            new_upper = first * upper - cross * lower
            new_lower = second * lower - cross * upper
            y = t - (e[k] * new_upper + e[k + 1] * new_lower)
            return jnp.where(sub == k, new_upper, jnp.where(sub == k + 1, new_lower, y))

        m = go(m)
        e = [go(x) if j > k + 1 else x for j, x in enumerate(e)]
    return m


def less_pivots(x, base, rows, inside):
    total = None
    for k in range(0, 8, 2):
        term = along(x, base + k) * rows[k] + along(x, base + k + 1) * rows[k + 1]
        total = term if total is None else total + term
    return jnp.where(inside, 0.0, x) - total


def invert(w):
    lane = lax.broadcasted_iota(jnp.int32, (8, 128), 1)
    sub = lax.broadcasted_iota(jnp.int32, (8, 128), 0)
    lanes = lax.broadcasted_iota(jnp.int32, (128, 128), 1)
    tiles = [w[8 * i : 8 * i + 8, :] for i in range(16)]
    diagonal = [jnp.where(lane == 8 * i + sub, x, 0.0) for i, x in enumerate(tiles)]
    total = functools.reduce(jnp.add, diagonal)
    across = lax.rsqrt(jnp.broadcast_to(jnp.sum(total, axis=0, keepdims=True), (8, 128)))
    down = [
        lax.rsqrt(jnp.broadcast_to(jnp.sum(x, axis=1, keepdims=True), (8, 128))) for x in diagonal
    ]
    for i in range(16):
        w[8 * i : 8 * i + 8, :] = tiles[i] * down[i] * across

    def at(t):
        return pl.ds(pl.multiple_of(8 * t, 8), 8)

    def panel(p, carry):
        rows, before, rows_before = carry
        base = 8 * p
        base_before = (base + 120) % 128
        inside_before = (lane >= base - 8) & (lane < base)
        following = w[at((p + 1) % 16), :]
        now = swept_rows(rows, base, lane, sub)
        following = less_pivots(
            following, base_before, [row_of(before, k) for k in range(8)], inside_before
        )
        following = less_pivots(
            following,
            base,
            [row_of(now, k) for k in range(8)],
            (lane >= base) & (lane < base + 8),
        )
        gone = (lanes >= base - 8) & (lanes < base)
        w[...] = jnp.where(gone, 0.0, w[...]) - outer(rows_before, before)

        @pl.when(p > 0)
        def _():
            w[at(p - 1), :] = before

        return following, now, rows

    zero = jnp.zeros((8, 128), F32)
    _, last, rows = lax.fori_loop(0, 16, panel, (w[0:8, :], zero, zero))
    w[...] = jnp.where(lanes >= 120, 0.0, w[...]) - outer(rows, last)
    w[120:128, :] = last
    for i in range(16):
        w[8 * i : 8 * i + 8, :] = -w[8 * i : 8 * i + 8, :] * down[i] * across


def halves(x):
    high = x.astype(BF16)
    return high, (x - high.astype(F32)).astype(BF16)


def put_left(ref, rows, x):
    high, low = halves(x)
    width = x.shape[1]
    ref[rows, :width] = high
    ref[rows, width : 2 * width] = high
    ref[rows, 2 * width : 3 * width] = low
    if ref.shape[1] > 3 * width:
        ref[rows, 3 * width :] = low


def put_right(ref, columns, x):
    high, low = halves(x)
    depth = x.shape[0]
    ref[:depth, columns] = high
    ref[depth : 2 * depth, columns] = low
    ref[2 * depth : 3 * depth, columns] = high
    if ref.shape[0] > 3 * depth:
        ref[3 * depth :, columns] = low


def dot(a, b):
    return jnp.dot(a, b, preferred_element_type=F32)


def eliminate(o, blocks, left, right, small_right, inverted):
    n = o.shape[0]
    whole = slice(None)
    eye = (
        lax.broadcasted_iota(jnp.int32, (BLK, BLK), 0)
        == lax.broadcasted_iota(jnp.int32, (BLK, BLK), 1)
    )

    def step(j, carry):
        at = pl.ds(pl.multiple_of(j * BLK, BLK), BLK)
        inverted[...] = o[at, at]
        put_right(right, whole, o[at, :])
        put_right(right, at, jnp.where(eye, -1.0, 0.0))
        put_left(left, whole, o[:, at])
        invert(inverted)
        put_right(small_right, whole, inverted[...])
        for t in range(0, n, 256):
            put_left(left, slice(t, t + 256), dot(left[t : t + 256, :], small_right[...]))
        put_left(left, at, -inverted[...])
        o[at, :] = jnp.zeros((BLK, n), F32)
        o[:, at] = jnp.zeros((n, BLK), F32)

        def tile(t, carry):
            these = pl.ds(pl.multiple_of(t * 512, 512), 512)
            o[these, :] = o[these, :] - dot(left[these, :], right[...])
            return carry

        lax.fori_loop(0, n // 512, tile, 0)
        return carry

    lax.fori_loop(0, blocks, step, 0)


def scratch_for(n):
    return [
        pltpu.VMEM((n, 4 * BLK), BF16),
        pltpu.VMEM((4 * BLK, n), BF16),
        pltpu.VMEM((4 * BLK, BLK), BF16),
        pltpu.VMEM((BLK, BLK), F32),
    ]


def at_block(b):
    return pl.ds(pl.multiple_of(b * BLK, BLK), BLK)


LOWER = [(a, b) for y in range(4) for a in (y, 7 - y) for b in range(a + 1)]
SHARE = [(i, j) for i in range(4) for j in range(i + 1)]


def pack_update(o, tri):
    for t, (i, j) in enumerate(SHARE):
        tri[t * BLK : (t + 1) * BLK, :] = o[
            SEP1 + i * BLK : SEP1 + (i + 1) * BLK, SEP1 + j * BLK : SEP1 + (j + 1) * BLK
        ]


def first_kernel(blocks, lower_ref, o_ref, tri_ref, *scratch):
    for t, (a, b) in enumerate(LOWER):
        part = lower_ref[t]
        o_ref[a * BLK : (a + 1) * BLK, b * BLK : (b + 1) * BLK] = part
        if a != b:
            o_ref[b * BLK : (b + 1) * BLK, a * BLK : (a + 1) * BLK] = part.T
    eliminate(o_ref, blocks, *scratch)
    pack_update(o_ref, tri_ref)


def add_child(o_ref, update, maps, child):
    for t, (i, j) in enumerate(SHARE):
        rows, columns = at_block(maps[child, i]), at_block(maps[child, j])
        part = update[t * BLK : (t + 1) * BLK, :]
        o_ref[rows, columns] = o_ref[rows, columns] + part
        if i != j:
            o_ref[columns, rows] = o_ref[columns, rows] + part.T


def next_kernel(blocks, packs, members, map_ref, base_ref, mine_ref, other_ref, o_ref, *rest):
    tri_ref, scratch = (rest[0], rest[1:]) if packs else (None, rest)
    child = lax.axis_index("leaf") // members
    add_child(o_ref, mine_ref, map_ref, child)
    add_child(o_ref, other_ref, map_ref, child + 1 - 2 * (child % 2))
    eliminate(o_ref, blocks, *scratch)
    if packs:
        pack_update(o_ref, tri_ref)


def remote(source, target, sent, received, leaf, front):
    return pltpu.make_async_remote_copy(
        src_ref=source,
        dst_ref=target,
        send_sem=sent,
        recv_sem=received,
        device_id=(leaf, front),
        device_id_type=pl.DeviceIdType.MESH,
    )


def greet(devices):
    barrier = pltpu.get_barrier_semaphore()
    for device in devices:
        pl.semaphore_signal(
            barrier, inc=1, device_id=device, device_id_type=pl.DeviceIdType.MESH
        )
    pl.semaphore_wait(barrier, len(devices))


def exchange_kernel(distance, tri_ref, entries_ref, o_ref, base_ref, sent, got, copied):
    leaf, y = lax.axis_index("leaf"), lax.axis_index("front")
    n = base_ref.shape[0]
    start = pl.multiple_of((leaf // (2 * distance)) % (entries_ref.shape[0] // n) * n, 8)
    fetch = pltpu.make_async_copy(entries_ref.at[pl.ds(start, n), :], base_ref, copied)
    fetch.start()
    core, x = leaf % 2, (leaf // 2) % 4
    z = leaf // 8
    sibling = leaf + distance * (1 - 2 * ((leaf // distance) % 2))
    other_core = leaf + 1 - 2 * core
    rows = tri_ref.shape[0] // 32

    def in_x(d):
        return z * 8 + ((x + d) % 4) * 2 + core

    greet(
        [(sibling, y), (other_core, y)]
        + [(leaf, (y + d) % 4) for d in (1, 2, 3)]
        + [(in_x(d), y) for d in (1, 2, 3)]
    )

    def share(c, xx, yy):
        return pl.ds(pl.multiple_of(((c * 4 + xx) * 4 + yy) * rows, 8), rows)

    def row(c, xx):
        return pl.ds(pl.multiple_of((c * 4 + xx) * 4 * rows, 8), 4 * rows)

    mine = share(core, x, y)
    across = remote(tri_ref.at[mine], o_ref.at[mine], sent.at[0], got.at[0], sibling, y)
    across.start()
    across.wait_recv()
    spread = [
        remote(o_ref.at[mine], o_ref.at[mine], sent.at[d], got.at[d], leaf, (y + d) % 4)
        for d in (1, 2, 3)
    ]
    for copy in spread:
        copy.start()
    for copy in spread:
        copy.wait_recv()
    whole = row(core, x)
    wide = [
        remote(o_ref.at[whole], o_ref.at[whole], sent.at[3 + d], got.at[3 + d], in_x(d), y)
        for d in (1, 2, 3)
    ]
    for copy in wide:
        copy.start()
    last = []
    for d in (0, 3, 1, 2):
        if d:
            wide[d - 1].wait_recv()
        piece = row(core, (x - d + 4) % 4)
        copy = remote(o_ref.at[piece], o_ref.at[piece], sent.at[7 + d], got.at[7 + d], other_core, y)
        copy.start()
        last.append(copy)
    for copy in last:
        copy.wait_recv()
    for copy in [across] + spread + wide + last:
        copy.wait_send()
    fetch.wait()


def gather_kernel(
    map_ref, leaf_ref, entries_ref, o_ref,
    met, partial, halves_in, own_entries, found_tile, table, told,
    keep, sent, got, sent_e, got_e, sent_y, got_y, sent_x, got_x, sent_c, got_c,
):
    leaf, y = lax.axis_index("leaf"), lax.axis_index("front")
    m = leaf % 16
    base = leaf - m
    core, x, z = m % 2, (m // 2) % 4, m // 8
    me = m * 4 + y
    barrier = pltpu.get_barrier_semaphore()

    def meet(d, carry):
        other = (me + d) % 64
        pl.semaphore_signal(
            barrier,
            inc=1,
            device_id=(base + other // 4, other % 4),
            device_id_type=pl.DeviceIdType.MESH,
        )
        return carry

    lax.fori_loop(1, 64, meet, 0)
    met[:, 4] = jnp.zeros((16, 8, BLK), F32)
    pl.semaphore_wait(barrier, 63)

    kept = pltpu.make_async_copy(leaf_ref.at[:, m], met.at[m, 0:4], keep.at[0])
    kept.start()
    members = []
    for d in range(1, 16):
        to = (m + d) % 16
        members.append(
            remote(leaf_ref.at[:, to], met.at[m, 0:4], sent.at[d], got.at[d], base + to, y)
        )
        members[-1].start()
    a, half = m // 2, m % 2
    high = a // 4
    target_y = a + high * (7 - 2 * a)
    wide = pl.ds(pl.multiple_of(y * 256, 256), 256)
    for g in range(8):
        to = half * 8 + g
        source = entries_ref.at[pl.ds(8 * g, 8), :]
        target = own_entries.at[high, :, wide]
        stays = jnp.logical_and(to == m, target_y == y)

        @pl.when(stays)
        def _():
            copy = pltpu.make_async_copy(source, target, got_e.at[high, y])
            copy.start()

        @pl.when(jnp.logical_not(stays))
        def _():
            remote(
                source, target, sent_e.at[g], got_e.at[high, y], base + to, target_y
            ).start()

    lane = lax.broadcasted_iota(jnp.int32, (16, BLK), 1)
    group = (
        (lane >= 9).astype(jnp.int32) + (lane >= 18).astype(jnp.int32) + (lane >= 27).astype(jnp.int32)
    )
    within = lane - 9 * group
    second = within > group
    block_row = jnp.where(second, 7 - group, group)
    block_column = jnp.where(second, within - group - 1, within)
    maps = map_ref[pl.ds(pl.multiple_of(base, 16), 16), :]
    found = jnp.full((16, BLK), 4, jnp.int32)
    landing = jnp.zeros((16, BLK), jnp.int32)
    for i in range(4):
        target = jnp.broadcast_to(maps[:, i : i + 1], (16, BLK))
        found = jnp.where(block_row == target, i, found)
        landing = landing + target * jnp.where(y == i, 1, 0)
    found_tile[...] = jnp.where(block_column == landing, found, 4)
    tell = pltpu.make_async_copy(found_tile, table, told)
    tell.start()
    tell.wait()
    kept.wait()
    for copy in members:
        copy.wait_recv()

    def sum_block(t, carry):
        terms = [met[s, table[s, t]] for s in range(16)]
        while len(terms) > 1:
            terms = [terms[i] + terms[i + 1] for i in range(0, len(terms), 2)]
        partial[t] = terms[0]
        return carry

    lax.fori_loop(0, 36, sum_block, 0)
    to_sum = []
    for d in (1, 2, 3):
        to = (y + d) % 4
        to_sum.append(
            remote(
                partial.at[pl.ds(9 * to, 9)], halves_in.at[d - 1],
                sent_y.at[d - 1], got_y.at[d - 1], leaf, to,
            )
        )
        to_sum[-1].start()
    for h in range(2):
        for c in range(4):
            pltpu.make_async_copy(
                entries_ref.at[pl.ds(0, 8), :],
                own_entries.at[h, :, pl.ds(c * 256, 256)],
                got_e.at[h, c],
            ).wait()
    for copy in to_sum:
        copy.wait_recv()
    rows = pl.ds(pl.multiple_of(m * 8, 8), 8)
    for t in range(9):
        second = (t + 8 - y) // 9
        b = t - second * (y + 1)
        entry = own_entries[second, :, pl.ds(pl.multiple_of(b * BLK, BLK), BLK)]
        value = partial[9 * y + t] + halves_in[0, t] + halves_in[1, t] + halves_in[2, t]
        o_ref[9 * y + t, rows, :] = value + entry
    spread = []
    own = o_ref.at[pl.ds(9 * y, 9), rows, :]
    for d in (1, 2, 3):
        spread.append(
            remote(own, own, sent_y.at[2 + d], got_y.at[2 + d], leaf, (y + d) % 4)
        )
        spread[-1].start()
    for copy in spread:
        copy.wait_recv()

    other_z = base + (m + 8) % 16
    other_core = base + m + 1 - 2 * core

    def piece(xx, zz, part):
        slot = pl.ds(pl.multiple_of((zz * 8 + xx * 2 + core) * 8, 8), 8)
        return o_ref.at[18 * part : 18 * part + 18, slot, :]

    def step_x(xx, zz, part, direction, slot):
        to = base + z * 8 + ((x + direction + 4) % 4) * 2 + core
        ref = piece(xx, zz, part)
        return remote(ref, ref, sent_x.at[slot], got_x.at[slot], to, y)

    def to_core(xx, zz, part, slot):
        ref = piece(xx, zz, part)
        return remote(ref, ref, sent_c.at[slot], got_c.at[slot], other_core, y)

    started = []

    def begin(copy):
        copy.start()
        started.append(copy)
        return copy

    left, right, far = (x + 3) % 4, (x + 1) % 4, (x + 2) % 4
    other = 1 - z
    over_z = []
    for part in range(2):
        ref = piece(x, z, part)
        over_z.append(begin(remote(ref, ref, sent_y.at[6 + part], got_y.at[6 + part], other_z, y)))
    passes, cores = [], []
    for stage, zz in ((0, z), (1, other)):
        if stage:
            for copy in over_z:
                copy.wait_recv()
        s = 6 * stage
        passes.append(
            [begin(step_x(x, zz, part, 1, s + part)) for part in range(2)]
            + [begin(step_x(x, zz, part, -1, s + 2 + part)) for part in range(2)]
        )
        for part in range(2):
            cores.append(begin(to_core(x, zz, part, 8 * stage + part)))
    for stage, zz in ((0, z), (1, other)):
        s = 6 * stage
        c = 8 * stage
        moves = passes[stage]
        moves[0].wait_recv()
        relay_right = begin(step_x(left, zz, 0, 1, s + 4))
        cores.append(begin(to_core(left, zz, 0, c + 2)))
        moves[3].wait_recv()
        relay_left = begin(step_x(right, zz, 1, -1, s + 5))
        cores.append(begin(to_core(right, zz, 1, c + 3)))
        moves[1].wait_recv()
        cores.append(begin(to_core(left, zz, 1, c + 4)))
        moves[2].wait_recv()
        cores.append(begin(to_core(right, zz, 0, c + 5)))
        passes.append((relay_right, relay_left))
    for stage, zz in ((0, z), (1, other)):
        relay_right, relay_left = passes[2 + stage]
        c = 8 * stage
        relay_right.wait_recv()
        cores.append(begin(to_core(far, zz, 0, c + 6)))
        relay_left.wait_recv()
        cores.append(begin(to_core(far, zz, 1, c + 7)))
    for copy in cores:
        copy.wait_recv()
    for copy in members + to_sum + spread + started:
        copy.wait_send()
    for g in range(8):
        to = half * 8 + g

        @pl.when(jnp.logical_not(jnp.logical_and(to == m, target_y == y)))
        def _():
            remote(
                entries_ref.at[pl.ds(8 * g, 8), :], own_entries.at[high, :, wide],
                sent_e.at[g], got_e.at[high, y], base + to, target_y,
            ).wait_send()


VMEM_SPEC = pl.BlockSpec(memory_space=pltpu.VMEM)
SMEM_SPEC = pl.BlockSpec(memory_space=pltpu.SMEM)
PARAMS = pltpu.CompilerParams(vmem_limit_bytes=24 * 1024 * 1024)


def gathered(map_leaf, leaf_update, entries):
    dma = pltpu.SemaphoreType.DMA
    return pl.pallas_call(
        gather_kernel,
        out_shape=jax.ShapeDtypeStruct((36, BLK, BLK), F32),
        in_specs=[VMEM_SPEC, VMEM_SPEC, VMEM_SPEC],
        out_specs=VMEM_SPEC,
        scratch_shapes=[
            pltpu.VMEM((16, 5, 8, BLK), F32),
            pltpu.VMEM((36, 8, BLK), F32),
            pltpu.VMEM((3, 9, 8, BLK), F32),
            pltpu.VMEM((2, 8, 1024), F32),
            pltpu.VMEM((16, BLK), jnp.int32),
            pltpu.SMEM((16, BLK), jnp.int32),
            dma,
            dma((1,)), dma((16,)), dma((16,)), dma((8,)), dma((2, 4)), dma((8,)), dma((8,)),
            dma((12,)), dma((12,)), dma((16,)), dma((16,)),
        ],
        compiler_params=pltpu.CompilerParams(
            vmem_limit_bytes=32 * 1024 * 1024, collective_id=0, has_side_effects=True
        ),
    )(map_leaf, leaf_update.reshape(4, 16, 8, BLK), entries)


def exchanged(tri, entries, distance, collective_id):
    dma = pltpu.SemaphoreType.DMA
    n = 8 * BLK
    return pl.pallas_call(
        functools.partial(exchange_kernel, distance),
        out_shape=(jax.ShapeDtypeStruct(tri.shape, F32), jax.ShapeDtypeStruct((n, n), F32)),
        in_specs=[VMEM_SPEC, pl.BlockSpec(memory_space=pltpu.HBM)],
        out_specs=(VMEM_SPEC, VMEM_SPEC),
        scratch_shapes=[dma((11,)), dma((11,)), dma],
        compiler_params=pltpu.CompilerParams(
            vmem_limit_bytes=(43 if collective_id == 1 else 16) * 1024 * 1024, collective_id=collective_id, has_side_effects=True
        ),
    )(tri, entries)


def first_eliminated(lower, blocks):
    n = 8 * BLK
    return pl.pallas_call(
        functools.partial(first_kernel, blocks),
        out_shape=(
            jax.ShapeDtypeStruct((n, n), F32),
            jax.ShapeDtypeStruct((10 * BLK, BLK), F32),
        ),
        in_specs=[VMEM_SPEC],
        out_specs=(VMEM_SPEC, VMEM_SPEC),
        scratch_shapes=scratch_for(n),
        compiler_params=PARAMS,
    )(lower)


def next_eliminated(maps, base, mine, other, blocks, packs, members):
    n = 8 * BLK
    out = [jax.ShapeDtypeStruct((n, n), F32)]
    if packs:
        out.append(jax.ShapeDtypeStruct((10 * BLK, BLK), F32))
    return pl.pallas_call(
        functools.partial(next_kernel, blocks, packs, members),
        out_shape=tuple(out),
        in_specs=[SMEM_SPEC, VMEM_SPEC, VMEM_SPEC, VMEM_SPEC],
        out_specs=tuple([VMEM_SPEC] * len(out)),
        scratch_shapes=scratch_for(n),
        input_output_aliases={1: 0},
        compiler_params=PARAMS,
    )(maps, base, mine, other)


def column_of_inverse(swept, sigma, sigma_left, coupling_left, block, value, value_right, column):
    half = 4 * BLK
    whole = slice(None)

    @pl.when(block < 4)
    def _():
        put_right(value_right, whole, swept[half:, at_block(block)])
        value[...] = -dot(sigma_left[...], value_right[...])
        column[:half, :] = -swept[:half, at_block(block)]

    @pl.when(block >= 4)
    def _():
        value[...] = sigma[:, at_block(block - 4)]
        column[:half, :] = jnp.zeros((half, BLK), F32)

    lower = value[...]
    put_right(value_right, whole, lower)
    column[:half, :] = column[:half, :] - dot(coupling_left[...], value_right[...])
    column[half:, :] = lower


def back_kernel(
    top_ref, mid_ref, leaf_ref, one_ref, two_ref, three_ref, o_ref, sigma, sigma_left, coupling_left, value, value_right, column, lower
):
    half = 4 * BLK
    whole = slice(None)
    leaf = lax.axis_index("leaf")
    first_node, second_node = leaf // 16, leaf // 32
    for i in range(4):
        for j in range(4):
            picked = three_ref[
                at_block(top_ref[second_node, i]), at_block(top_ref[second_node, j])
            ]
            sigma[i * BLK : (i + 1) * BLK, j * BLK : (j + 1) * BLK] = -picked
    put_left(sigma_left, whole, sigma[...])
    put_left(coupling_left, whole, two_ref[:half, half:])

    def step(j, carry):
        column_of_inverse(
            two_ref, sigma, sigma_left, coupling_left, mid_ref[first_node, j], value, value_right, column
        )
        for i in range(4):
            lower[i * BLK : (i + 1) * BLK, at_block(j)] = column[at_block(mid_ref[first_node, i]), :]
        return carry

    lax.fori_loop(0, 4, step, 0)
    put_left(sigma_left, whole, lower[...])
    put_left(coupling_left, whole, one_ref[:half, half:])
    column_of_inverse(
        one_ref, lower, sigma_left, coupling_left, leaf_ref[leaf, lax.axis_index("front")],
        value, value_right, column,
    )
    for i in range(4):
        o_ref[i * BLK : (i + 1) * BLK, :] = column[at_block(leaf_ref[leaf, i]), :]


def back_substituted(top, mid, leaf, one, two, three):
    half = 4 * BLK
    return pl.pallas_call(
        back_kernel,
        out_shape=jax.ShapeDtypeStruct((half, BLK), F32),
        in_specs=[SMEM_SPEC] * 3 + [VMEM_SPEC] * 3,
        out_specs=VMEM_SPEC,
        scratch_shapes=[
            pltpu.VMEM((half, half), F32),
            pltpu.VMEM((half, 3 * half), BF16),
            pltpu.VMEM((half, 3 * half), BF16),
            pltpu.VMEM((half, BLK), F32),
            pltpu.VMEM((3 * half, BLK), BF16),
            pltpu.VMEM((2 * half, BLK), F32),
            pltpu.VMEM((half, half), F32),
        ],
        compiler_params=PARAMS,
    )(top, mid, leaf, one, two, three)


def body(leaf_update, front_entries1, front_entries2, front_entries3, map_leaf, map_mid, map_top):
    members = lax.axis_size("leaf") // 4
    lower = gathered(map_leaf, leaf_update, front_entries1)
    one, update = first_eliminated(lower, SEP1 // BLK)
    other, base = exchanged(update, front_entries2, members, 1)
    two, update = next_eliminated(map_mid, base, update, other, SEP2 // BLK, True, members)
    other, base = exchanged(update, front_entries3, 2 * members, 2)
    (three,) = next_eliminated(map_top, base, update, other, SEP3 // BLK, False, 2 * members)
    return back_substituted(map_top, map_mid, map_leaf, one, two, three)


def solution(mesh):
    in_specs = (P("leaf", "front"), P("leaf", "front"), P(), P(), P(), P(), P())
    out_specs = P("leaf", "front")
    return jax.shard_map(body, mesh=mesh, in_specs=in_specs, out_specs=out_specs, check_vma=False)
```

```python
import functools

import jax
import jax.numpy as jnp
from jax import lax
from jax.experimental import pallas as pl
from jax.experimental.pallas import tpu as pltpu
from jax.sharding import PartitionSpec as P

BLK = 128
SEP1 = 512
SEP2 = 512
SEP3 = 1024
RUP = 512


F32, BF16 = jnp.float32, jnp.bfloat16
ROUNDS = 4


def row_of(x, k):
    return jnp.broadcast_to(x[k : k + 1, :], (8, 128))


def along(x, c):
    return jnp.take_along_axis(x, jnp.full((8, 128), c, jnp.int32), axis=1)


def thirds(x):
    high = x.astype(BF16)
    rest = x - high.astype(F32)
    middle = rest.astype(BF16)
    return high, middle, (rest - middle.astype(F32)).astype(BF16)


def outer_left(p):
    high, middle, low = thirds(p)
    return jnp.concatenate([high, high, high, middle, middle, low], axis=0).T


def outer_right(s):
    high, middle, low = thirds(s)
    return jnp.concatenate([high, middle, low, high, middle, high], axis=0)


def swept_rows(rows, base, lane, sub):
    e = [along(rows, base + j) for j in range(8)]
    inside = (lane >= base) & (lane < base + 8)
    m = jnp.where(lane == base + sub, -1.0, jnp.where(inside, 0.0, rows))
    for k in range(0, 8, 2):
        a, b, d = row_of(e[k], k), row_of(e[k + 1], k), row_of(e[k + 1], k + 1)
        is_first, is_second = sub == k, sub == k + 1
        pair = is_first | is_second
        left = jnp.where(is_first, -1.0, jnp.where(is_second, 0.0, e[k]))
        right = jnp.where(is_second, -1.0, jnp.where(is_first, 0.0, e[k + 1]))
        scale = 1.0 / (a * d - b * b)
        by_first = (d * left - b * right) * scale
        by_second = (a * right - b * left) * scale

        def go(t):
            return jnp.where(pair, 0.0, t) - by_first * row_of(t, k) - by_second * row_of(t, k + 1)

        m = go(m)
        e = [go(x) if j > k + 1 else x for j, x in enumerate(e)]
    return m


def sum_of(terms):
    while len(terms) > 1:
        terms = [terms[i] + terms[i + 1] for i in range(0, len(terms), 2)]
    return terms[0]


def less_pivots(x, base, rows, inside):
    total = None
    for k in range(0, 8, 2):
        term = along(x, base + k) * rows[k] + along(x, base + k + 1) * rows[k + 1]
        total = term if total is None else total + term
    return jnp.where(inside, 0.0, x) - total


def scaled_diagonal(w):
    lane = lax.broadcasted_iota(jnp.int32, (8, 128), 1)
    sub = lax.broadcasted_iota(jnp.int32, (8, 128), 0)
    tiles = [w[8 * i : 8 * i + 8, :] for i in range(16)]
    diagonal = [jnp.where(lane == 8 * i + sub, x, 0.0) for i, x in enumerate(tiles)]
    total = functools.reduce(jnp.add, diagonal)
    across = lax.rsqrt(jnp.broadcast_to(jnp.sum(total, axis=0, keepdims=True), (8, 128)))
    down = [
        lax.rsqrt(jnp.broadcast_to(jnp.sum(x, axis=1, keepdims=True), (8, 128))) for x in diagonal
    ]
    for i in range(16):
        w[8 * i : 8 * i + 8, :] = tiles[i] * down[i] * across
    return down, across


def invert(w, rounds, beside):
    lane = lax.broadcasted_iota(jnp.int32, (8, 128), 1)
    sub = lax.broadcasted_iota(jnp.int32, (8, 128), 0)
    lanes = lax.broadcasted_iota(jnp.int32, (128, 128), 1)
    down, across = scaled_diagonal(w)

    def at(t):
        return pl.ds(pl.multiple_of(8 * t, 8), 8)

    def panel(p, carry):
        rows, before, left_before = carry
        base = 8 * p
        base_before = (base + 120) % 128
        inside_before = (lane >= base - 8) & (lane < base)
        gone = (lanes >= base - 8) & (lanes < base)
        q = (p + 1) % 16
        following = w[at(q), :]
        now = swept_rows(rows, base, lane, sub)
        own = lane == 8 * q + sub
        entries = [
            jnp.broadcast_to(
                jnp.sum(jnp.where(own, row_of(rows, k), 0.0), axis=1, keepdims=True), (8, 128)
            )
            for k in range(8)
        ]
        following = less_pivots(
            following, base_before, [row_of(before, k) for k in range(8)], inside_before
        )
        inside = (lane >= base) & (lane < base + 8)
        following = jnp.where(inside, 0.0, following) - sum_of(
            [entries[k] * row_of(now, k) for k in range(8)]
        )
        w[:BLK, :] = jnp.where(gone, 0.0, w[:BLK, :]) - dot(left_before, outer_right(before))
        w[at((p + 16) % 17), :] = before
        return following, now, outer_left(rows)

    def turn(r, carry):
        for p in range(16 // rounds):
            carry = panel(r * (16 // rounds) + p, carry)
            if p == 0:
                beside(r)
        return carry

    start = (w[0:8, :], jnp.zeros((8, 128), F32), jnp.zeros((BLK, 48), BF16))
    _, last, left = lax.fori_loop(0, rounds, turn, start)
    w[:BLK, :] = jnp.where(lanes >= 120, 0.0, w[:BLK, :]) - dot(left, outer_right(last))
    w[120:128, :] = last
    for i in range(16):
        w[8 * i : 8 * i + 8, :] = -w[8 * i : 8 * i + 8, :] * down[i] * across


def halves(x):
    high = x.astype(BF16)
    return high, (x - high.astype(F32)).astype(BF16)


def put_left(ref, rows, x):
    high, low = halves(x)
    width = x.shape[1]
    ref[rows, :width] = high
    ref[rows, width : 2 * width] = high
    ref[rows, 2 * width : 3 * width] = low
    if ref.shape[1] > 3 * width:
        ref[rows, 3 * width :] = low


def put_right(ref, columns, x):
    high, low = halves(x)
    depth = x.shape[0]
    ref[:depth, columns] = high
    ref[depth : 2 * depth, columns] = low
    ref[2 * depth : 3 * depth, columns] = high
    if ref.shape[0] > 3 * depth:
        ref[3 * depth :, columns] = low


def dot(a, b):
    return jnp.dot(a, b, preferred_element_type=F32)


def eliminate(o, blocks, left, right, small_right, inverted):
    n = o.shape[0]
    whole = slice(None)
    eye = (
        lax.broadcasted_iota(jnp.int32, (BLK, BLK), 0)
        == lax.broadcasted_iota(jnp.int32, (BLK, BLK), 1)
    )

    def nothing(r):
        pass

    def prepare(j):
        at = pl.ds(pl.multiple_of(j * BLK, BLK), BLK)
        put_right(right, whole, o[at, :])
        put_right(right, at, jnp.where(eye, -1.0, 0.0))
        put_left(left, whole, o[:, at])
        put_right(small_right, whole, inverted[:BLK, :])
        for t in range(0, n, 256):
            put_left(left, slice(t, t + 256), dot(left[t : t + 256, :], small_right[...]))
        put_left(left, at, -inverted[:BLK, :])
        o[at, :] = jnp.zeros((BLK, n), F32)
        o[:, at] = jnp.zeros((n, BLK), F32)

    def update(size, t):
        these = pl.ds(pl.multiple_of(t * size, size), size)
        o[these, :] = o[these, :] - dot(left[these, :], right[...])

    inverted[:BLK, :] = o[:BLK, :BLK]
    invert(inverted, 16, nothing)

    def step(j, carry):
        prepare(j)
        after = pl.ds(pl.multiple_of((j + 1) * BLK, BLK), BLK)
        inverted[:BLK, :] = o[after, after] - dot(left[after, :], right[:, after])
        invert(inverted, ROUNDS, functools.partial(update, n // ROUNDS))
        return carry

    lax.fori_loop(0, blocks - 1, step, 0)
    prepare(blocks - 1)

    def tile(t, carry):
        update(512, t)
        return carry

    lax.fori_loop(0, n // 512, tile, 0)


def scratch_for(n):
    return [
        pltpu.VMEM((n, 4 * BLK), BF16),
        pltpu.VMEM((4 * BLK, n), BF16),
        pltpu.VMEM((4 * BLK, BLK), BF16),
        pltpu.VMEM((BLK + 8, BLK), F32),
    ]


def at_block(b):
    return pl.ds(pl.multiple_of(b * BLK, BLK), BLK)


LOWER = [(a, b) for y in range(4) for a in (y, 7 - y) for b in range(a + 1)]
SHARE = [(i, j) for i in range(4) for j in range(i + 1)]


def pack_update(o, tri):
    for t, (i, j) in enumerate(SHARE):
        tri[t * BLK : (t + 1) * BLK, :] = o[
            SEP1 + i * BLK : SEP1 + (i + 1) * BLK, SEP1 + j * BLK : SEP1 + (j + 1) * BLK
        ]


def first_kernel(blocks, lower_ref, o_ref, tri_ref, *scratch):
    for t, (a, b) in enumerate(LOWER):
        part = lower_ref[t]
        o_ref[a * BLK : (a + 1) * BLK, b * BLK : (b + 1) * BLK] = part
        if a != b:
            o_ref[b * BLK : (b + 1) * BLK, a * BLK : (a + 1) * BLK] = part.T
    eliminate(o_ref, blocks, *scratch)
    pack_update(o_ref, tri_ref)


def add_child(o_ref, update, maps, child):
    for t, (i, j) in enumerate(SHARE):
        rows, columns = at_block(maps[child, i]), at_block(maps[child, j])
        part = update[t * BLK : (t + 1) * BLK, :]
        o_ref[rows, columns] = o_ref[rows, columns] + part
        if i != j:
            o_ref[columns, rows] = o_ref[columns, rows] + part.T


def next_kernel(blocks, packs, members, map_ref, base_ref, mine_ref, other_ref, o_ref, *rest):
    tri_ref, scratch = (rest[0], rest[1:]) if packs else (None, rest)
    child = lax.axis_index("leaf") // members
    add_child(o_ref, mine_ref, map_ref, child)
    add_child(o_ref, other_ref, map_ref, child + 1 - 2 * (child % 2))
    eliminate(o_ref, blocks, *scratch)
    if packs:
        pack_update(o_ref, tri_ref)


def remote(source, target, sent, received, leaf, front):
    return pltpu.make_async_remote_copy(
        src_ref=source,
        dst_ref=target,
        send_sem=sent,
        recv_sem=received,
        device_id=(leaf, front),
        device_id_type=pl.DeviceIdType.MESH,
    )


def greet(devices):
    barrier = pltpu.get_barrier_semaphore()
    for device in devices:
        pl.semaphore_signal(
            barrier, inc=1, device_id=device, device_id_type=pl.DeviceIdType.MESH
        )
    pl.semaphore_wait(barrier, len(devices))


def exchange_kernel(distance, tri_ref, entries_ref, o_ref, base_ref, sent, got, copied):
    leaf, y = lax.axis_index("leaf"), lax.axis_index("front")
    n = base_ref.shape[0]
    start = pl.multiple_of((leaf // (2 * distance)) % (entries_ref.shape[0] // n) * n, 8)
    fetch = pltpu.make_async_copy(entries_ref.at[pl.ds(start, n), :], base_ref, copied)
    fetch.start()
    core, x = leaf % 2, (leaf // 2) % 4
    z = leaf // 8
    sibling = leaf + distance * (1 - 2 * ((leaf // distance) % 2))
    other_core = leaf + 1 - 2 * core
    rows = tri_ref.shape[0] // 32

    def in_x(d):
        return z * 8 + ((x + d) % 4) * 2 + core

    greet(
        [(sibling, y), (other_core, y)]
        + [(leaf, (y + d) % 4) for d in (1, 2, 3)]
        + [(in_x(d), y) for d in (1, 2, 3)]
    )

    def share(c, xx, yy):
        return pl.ds(pl.multiple_of(((c * 4 + xx) * 4 + yy) * rows, 8), rows)

    def row(c, xx):
        return pl.ds(pl.multiple_of((c * 4 + xx) * 4 * rows, 8), 4 * rows)

    mine = share(core, x, y)
    across = remote(tri_ref.at[mine], o_ref.at[mine], sent.at[0], got.at[0], sibling, y)
    across.start()
    across.wait_recv()
    spread = [
        remote(o_ref.at[mine], o_ref.at[mine], sent.at[d], got.at[d], leaf, (y + d) % 4)
        for d in (1, 2, 3)
    ]
    for copy in spread:
        copy.start()
    for copy in spread:
        copy.wait_recv()
    whole = row(core, x)
    wide = [
        remote(o_ref.at[whole], o_ref.at[whole], sent.at[3 + d], got.at[3 + d], in_x(d), y)
        for d in (1, 2, 3)
    ]
    for copy in wide:
        copy.start()
    last = []
    for d in (0, 3, 1, 2):
        if d:
            wide[d - 1].wait_recv()
        piece = row(core, (x - d + 4) % 4)
        copy = remote(o_ref.at[piece], o_ref.at[piece], sent.at[7 + d], got.at[7 + d], other_core, y)
        copy.start()
        last.append(copy)
    for copy in last:
        copy.wait_recv()
    for copy in [across] + spread + wide + last:
        copy.wait_send()
    fetch.wait()


def gather_kernel(
    map_ref, leaf_ref, entries_ref, o_ref,
    met, partial, halves_in, own_entries, found_tile, table, told,
    keep, sent, got, sent_e, got_e, sent_y, got_y, sent_x, got_x, sent_c, got_c,
):
    leaf, y = lax.axis_index("leaf"), lax.axis_index("front")
    m = leaf % 16
    base = leaf - m
    core, x, z = m % 2, (m // 2) % 4, m // 8
    me = m * 4 + y
    barrier = pltpu.get_barrier_semaphore()

    def meet(d, carry):
        other = (me + d) % 64
        pl.semaphore_signal(
            barrier,
            inc=1,
            device_id=(base + other // 4, other % 4),
            device_id_type=pl.DeviceIdType.MESH,
        )
        return carry

    lax.fori_loop(1, 64, meet, 0)
    met[:, 4] = jnp.zeros((16, 8, BLK), F32)
    pl.semaphore_wait(barrier, 63)

    kept = pltpu.make_async_copy(leaf_ref.at[:, m], met.at[m, 0:4], keep.at[0])
    kept.start()
    members = []
    for d in range(1, 16):
        to = (m + d) % 16
        members.append(
            remote(leaf_ref.at[:, to], met.at[m, 0:4], sent.at[d], got.at[d], base + to, y)
        )
        members[-1].start()
    a, half = m // 2, m % 2
    high = a // 4
    target_y = a + high * (7 - 2 * a)
    wide = pl.ds(pl.multiple_of(y * 256, 256), 256)
    for g in range(8):
        to = half * 8 + g
        source = entries_ref.at[pl.ds(8 * g, 8), :]
        target = own_entries.at[high, :, wide]
        stays = jnp.logical_and(to == m, target_y == y)

        @pl.when(stays)
        def _():
            copy = pltpu.make_async_copy(source, target, got_e.at[high, y])
            copy.start()

        @pl.when(jnp.logical_not(stays))
        def _():
            remote(
                source, target, sent_e.at[g], got_e.at[high, y], base + to, target_y
            ).start()

    lane = lax.broadcasted_iota(jnp.int32, (16, BLK), 1)
    group = (
        (lane >= 9).astype(jnp.int32) + (lane >= 18).astype(jnp.int32) + (lane >= 27).astype(jnp.int32)
    )
    within = lane - 9 * group
    second = within > group
    block_row = jnp.where(second, 7 - group, group)
    block_column = jnp.where(second, within - group - 1, within)
    maps = map_ref[pl.ds(pl.multiple_of(base, 16), 16), :]
    found = jnp.full((16, BLK), 4, jnp.int32)
    landing = jnp.zeros((16, BLK), jnp.int32)
    for i in range(4):
        target = jnp.broadcast_to(maps[:, i : i + 1], (16, BLK))
        found = jnp.where(block_row == target, i, found)
        landing = landing + target * jnp.where(y == i, 1, 0)
    found_tile[...] = jnp.where(block_column == landing, found, 4)
    tell = pltpu.make_async_copy(found_tile, table, told)
    tell.start()
    tell.wait()
    kept.wait()
    for copy in members:
        copy.wait_recv()

    def sum_block(t, carry):
        terms = [met[s, table[s, t]] for s in range(16)]
        while len(terms) > 1:
            terms = [terms[i] + terms[i + 1] for i in range(0, len(terms), 2)]
        partial[t] = terms[0]
        return carry

    lax.fori_loop(0, 36, sum_block, 0)
    to_sum = []
    for d in (1, 2, 3):
        to = (y + d) % 4
        to_sum.append(
            remote(
                partial.at[pl.ds(9 * to, 9)], halves_in.at[d - 1],
                sent_y.at[d - 1], got_y.at[d - 1], leaf, to,
            )
        )
        to_sum[-1].start()
    for h in range(2):
        for c in range(4):
            pltpu.make_async_copy(
                entries_ref.at[pl.ds(0, 8), :],
                own_entries.at[h, :, pl.ds(c * 256, 256)],
                got_e.at[h, c],
            ).wait()
    for copy in to_sum:
        copy.wait_recv()
    rows = pl.ds(pl.multiple_of(m * 8, 8), 8)
    for t in range(9):
        second = (t + 8 - y) // 9
        b = t - second * (y + 1)
        entry = own_entries[second, :, pl.ds(pl.multiple_of(b * BLK, BLK), BLK)]
        value = partial[9 * y + t] + halves_in[0, t] + halves_in[1, t] + halves_in[2, t]
        o_ref[9 * y + t, rows, :] = value + entry
    spread = []
    own = o_ref.at[pl.ds(9 * y, 9), rows, :]
    for d in (1, 2, 3):
        spread.append(
            remote(own, own, sent_y.at[2 + d], got_y.at[2 + d], leaf, (y + d) % 4)
        )
        spread[-1].start()
    for copy in spread:
        copy.wait_recv()

    other_z = base + (m + 8) % 16
    other_core = base + m + 1 - 2 * core

    def piece(xx, zz, part):
        slot = pl.ds(pl.multiple_of((zz * 8 + xx * 2 + core) * 8, 8), 8)
        return o_ref.at[18 * part : 18 * part + 18, slot, :]

    def step_x(xx, zz, part, direction, slot):
        to = base + z * 8 + ((x + direction + 4) % 4) * 2 + core
        ref = piece(xx, zz, part)
        return remote(ref, ref, sent_x.at[slot], got_x.at[slot], to, y)

    def to_core(xx, zz, part, slot):
        ref = piece(xx, zz, part)
        return remote(ref, ref, sent_c.at[slot], got_c.at[slot], other_core, y)

    started = []

    def begin(copy):
        copy.start()
        started.append(copy)
        return copy

    left, right, far = (x + 3) % 4, (x + 1) % 4, (x + 2) % 4
    other = 1 - z
    over_z = []
    for part in range(2):
        ref = piece(x, z, part)
        over_z.append(begin(remote(ref, ref, sent_y.at[6 + part], got_y.at[6 + part], other_z, y)))
    passes, cores = [], []
    for stage, zz in ((0, z), (1, other)):
        if stage:
            for copy in over_z:
                copy.wait_recv()
        s = 6 * stage
        passes.append(
            [begin(step_x(x, zz, part, 1, s + part)) for part in range(2)]
            + [begin(step_x(x, zz, part, -1, s + 2 + part)) for part in range(2)]
        )
        for part in range(2):
            cores.append(begin(to_core(x, zz, part, 8 * stage + part)))
    for stage, zz in ((0, z), (1, other)):
        s = 6 * stage
        c = 8 * stage
        moves = passes[stage]
        moves[0].wait_recv()
        relay_right = begin(step_x(left, zz, 0, 1, s + 4))
        cores.append(begin(to_core(left, zz, 0, c + 2)))
        moves[3].wait_recv()
        relay_left = begin(step_x(right, zz, 1, -1, s + 5))
        cores.append(begin(to_core(right, zz, 1, c + 3)))
        moves[1].wait_recv()
        cores.append(begin(to_core(left, zz, 1, c + 4)))
        moves[2].wait_recv()
        cores.append(begin(to_core(right, zz, 0, c + 5)))
        passes.append((relay_right, relay_left))
    for stage, zz in ((0, z), (1, other)):
        relay_right, relay_left = passes[2 + stage]
        c = 8 * stage
        relay_right.wait_recv()
        cores.append(begin(to_core(far, zz, 0, c + 6)))
        relay_left.wait_recv()
        cores.append(begin(to_core(far, zz, 1, c + 7)))
    for copy in cores:
        copy.wait_recv()
    for copy in members + to_sum + spread + started:
        copy.wait_send()
    for g in range(8):
        to = half * 8 + g

        @pl.when(jnp.logical_not(jnp.logical_and(to == m, target_y == y)))
        def _():
            remote(
                entries_ref.at[pl.ds(8 * g, 8), :], own_entries.at[high, :, wide],
                sent_e.at[g], got_e.at[high, y], base + to, target_y,
            ).wait_send()


VMEM_SPEC = pl.BlockSpec(memory_space=pltpu.VMEM)
SMEM_SPEC = pl.BlockSpec(memory_space=pltpu.SMEM)
PARAMS = pltpu.CompilerParams(vmem_limit_bytes=24 * 1024 * 1024)


def gathered(map_leaf, leaf_update, entries):
    dma = pltpu.SemaphoreType.DMA
    return pl.pallas_call(
        gather_kernel,
        out_shape=jax.ShapeDtypeStruct((36, BLK, BLK), F32),
        in_specs=[VMEM_SPEC, VMEM_SPEC, VMEM_SPEC],
        out_specs=VMEM_SPEC,
        scratch_shapes=[
            pltpu.VMEM((16, 5, 8, BLK), F32),
            pltpu.VMEM((36, 8, BLK), F32),
            pltpu.VMEM((3, 9, 8, BLK), F32),
            pltpu.VMEM((2, 8, 1024), F32),
            pltpu.VMEM((16, BLK), jnp.int32),
            pltpu.SMEM((16, BLK), jnp.int32),
            dma,
            dma((1,)), dma((16,)), dma((16,)), dma((8,)), dma((2, 4)), dma((8,)), dma((8,)),
            dma((12,)), dma((12,)), dma((16,)), dma((16,)),
        ],
        compiler_params=pltpu.CompilerParams(
            vmem_limit_bytes=32 * 1024 * 1024, collective_id=0, has_side_effects=True
        ),
    )(map_leaf, leaf_update.reshape(4, 16, 8, BLK), entries)


def exchanged(tri, entries, distance, collective_id):
    dma = pltpu.SemaphoreType.DMA
    n = 8 * BLK
    return pl.pallas_call(
        functools.partial(exchange_kernel, distance),
        out_shape=(jax.ShapeDtypeStruct(tri.shape, F32), jax.ShapeDtypeStruct((n, n), F32)),
        in_specs=[VMEM_SPEC, pl.BlockSpec(memory_space=pltpu.HBM)],
        out_specs=(VMEM_SPEC, VMEM_SPEC),
        scratch_shapes=[dma((11,)), dma((11,)), dma],
        compiler_params=pltpu.CompilerParams(
            vmem_limit_bytes=(43 if collective_id == 1 else 16) * 1024 * 1024, collective_id=collective_id, has_side_effects=True
        ),
    )(tri, entries)


def first_eliminated(lower, blocks):
    n = 8 * BLK
    return pl.pallas_call(
        functools.partial(first_kernel, blocks),
        out_shape=(
            jax.ShapeDtypeStruct((n, n), F32),
            jax.ShapeDtypeStruct((10 * BLK, BLK), F32),
        ),
        in_specs=[VMEM_SPEC],
        out_specs=(VMEM_SPEC, VMEM_SPEC),
        scratch_shapes=scratch_for(n),
        compiler_params=PARAMS,
    )(lower)


def next_eliminated(maps, base, mine, other, blocks, packs, members):
    n = 8 * BLK
    out = [jax.ShapeDtypeStruct((n, n), F32)]
    if packs:
        out.append(jax.ShapeDtypeStruct((10 * BLK, BLK), F32))
    return pl.pallas_call(
        functools.partial(next_kernel, blocks, packs, members),
        out_shape=tuple(out),
        in_specs=[SMEM_SPEC, VMEM_SPEC, VMEM_SPEC, VMEM_SPEC],
        out_specs=tuple([VMEM_SPEC] * len(out)),
        scratch_shapes=scratch_for(n),
        input_output_aliases={1: 0},
        compiler_params=PARAMS,
    )(maps, base, mine, other)


def column_of_inverse(swept, sigma, sigma_left, coupling_left, block, value, value_right, column):
    half = 4 * BLK
    whole = slice(None)

    @pl.when(block < 4)
    def _():
        put_right(value_right, whole, swept[half:, at_block(block)])
        value[...] = -dot(sigma_left[...], value_right[...])
        column[:half, :] = -swept[:half, at_block(block)]

    @pl.when(block >= 4)
    def _():
        value[...] = sigma[:, at_block(block - 4)]
        column[:half, :] = jnp.zeros((half, BLK), F32)

    lower = value[...]
    put_right(value_right, whole, lower)
    column[:half, :] = column[:half, :] - dot(coupling_left[...], value_right[...])
    column[half:, :] = lower


def back_kernel(
    top_ref, mid_ref, leaf_ref, one_ref, two_ref, three_ref, o_ref, sigma, sigma_left, coupling_left, value, value_right, column, lower
):
    half = 4 * BLK
    whole = slice(None)
    leaf = lax.axis_index("leaf")
    first_node, second_node = leaf // 16, leaf // 32
    for i in range(4):
        for j in range(4):
            picked = three_ref[
                at_block(top_ref[second_node, i]), at_block(top_ref[second_node, j])
            ]
            sigma[i * BLK : (i + 1) * BLK, j * BLK : (j + 1) * BLK] = -picked
    put_left(sigma_left, whole, sigma[...])
    put_left(coupling_left, whole, two_ref[:half, half:])

    def step(j, carry):
        column_of_inverse(
            two_ref, sigma, sigma_left, coupling_left, mid_ref[first_node, j], value, value_right, column
        )
        for i in range(4):
            lower[i * BLK : (i + 1) * BLK, at_block(j)] = column[at_block(mid_ref[first_node, i]), :]
        return carry

    lax.fori_loop(0, 4, step, 0)
    put_left(sigma_left, whole, lower[...])
    put_left(coupling_left, whole, one_ref[:half, half:])
    column_of_inverse(
        one_ref, lower, sigma_left, coupling_left, leaf_ref[leaf, lax.axis_index("front")],
        value, value_right, column,
    )
    for i in range(4):
        o_ref[i * BLK : (i + 1) * BLK, :] = column[at_block(leaf_ref[leaf, i]), :]


def back_substituted(top, mid, leaf, one, two, three):
    half = 4 * BLK
    return pl.pallas_call(
        back_kernel,
        out_shape=jax.ShapeDtypeStruct((half, BLK), F32),
        in_specs=[SMEM_SPEC] * 3 + [VMEM_SPEC] * 3,
        out_specs=VMEM_SPEC,
        scratch_shapes=[
            pltpu.VMEM((half, half), F32),
            pltpu.VMEM((half, 3 * half), BF16),
            pltpu.VMEM((half, 3 * half), BF16),
            pltpu.VMEM((half, BLK), F32),
            pltpu.VMEM((3 * half, BLK), BF16),
            pltpu.VMEM((2 * half, BLK), F32),
            pltpu.VMEM((half, half), F32),
        ],
        compiler_params=PARAMS,
    )(top, mid, leaf, one, two, three)


def body(leaf_update, front_entries1, front_entries2, front_entries3, map_leaf, map_mid, map_top):
    members = lax.axis_size("leaf") // 4
    lower = gathered(map_leaf, leaf_update, front_entries1)
    one, update = first_eliminated(lower, SEP1 // BLK)
    other, base = exchanged(update, front_entries2, members, 1)
    two, update = next_eliminated(map_mid, base, update, other, SEP2 // BLK, True, members)
    other, base = exchanged(update, front_entries3, 2 * members, 2)
    (three,) = next_eliminated(map_top, base, update, other, SEP3 // BLK, False, 2 * members)
    return back_substituted(map_top, map_mid, map_leaf, one, two, three)


def solution(mesh):
    in_specs = (P("leaf", "front"), P("leaf", "front"), P(), P(), P(), P(), P())
    out_specs = P("leaf", "front")
    return jax.shard_map(body, mesh=mesh, in_specs=in_specs, out_specs=out_specs, check_vma=False)
```

```python
import functools

import jax
import jax.numpy as jnp
from jax import lax
from jax.experimental import pallas as pl
from jax.experimental.pallas import tpu as pltpu
from jax.sharding import PartitionSpec as P

BLK = 128
SEP1 = 512
SEP2 = 512
SEP3 = 1024
RUP = 512


F32, BF16 = jnp.float32, jnp.bfloat16
ROUNDS = 4


def row_of(x, k):
    return jnp.broadcast_to(x[k : k + 1, :], (8, 128))


def along(x, c):
    return jnp.take_along_axis(x, jnp.full((8, 128), c, jnp.int32), axis=1)


def thirds(x):
    high = x.astype(BF16)
    rest = x - high.astype(F32)
    middle = rest.astype(BF16)
    return high, middle, (rest - middle.astype(F32)).astype(BF16)


def outer_left(p):
    high, middle, low = thirds(p)
    return jnp.concatenate([high, high, high, middle, middle, low], axis=0).T


def outer_right(s):
    high, middle, low = thirds(s)
    return jnp.concatenate([high, middle, low, high, middle, high], axis=0)


def swept_rows(rows, base, lane, sub):
    e = [along(rows, base + j) for j in range(8)]
    inside = (lane >= base) & (lane < base + 8)
    m = jnp.where(lane == base + sub, -1.0, jnp.where(inside, 0.0, rows))
    for k in range(0, 8, 2):
        a, b, d = row_of(e[k], k), row_of(e[k + 1], k), row_of(e[k + 1], k + 1)
        is_first, is_second = sub == k, sub == k + 1
        pair = is_first | is_second
        left = jnp.where(is_first, -1.0, jnp.where(is_second, 0.0, e[k]))
        right = jnp.where(is_second, -1.0, jnp.where(is_first, 0.0, e[k + 1]))
        scale = 1.0 / (a * d - b * b)
        by_first = (d * left - b * right) * scale
        by_second = (a * right - b * left) * scale

        def go(t):
            return jnp.where(pair, 0.0, t) - by_first * row_of(t, k) - by_second * row_of(t, k + 1)

        m = go(m)
        e = [go(x) if j > k + 1 else x for j, x in enumerate(e)]
    return m


def sum_of(terms):
    while len(terms) > 1:
        terms = [terms[i] + terms[i + 1] for i in range(0, len(terms), 2)]
    return terms[0]


def less_pivots(x, base, rows, inside):
    total = None
    for k in range(0, 8, 2):
        term = along(x, base + k) * rows[k] + along(x, base + k + 1) * rows[k + 1]
        total = term if total is None else total + term
    return jnp.where(inside, 0.0, x) - total


def scaled_diagonal(w):
    lane = lax.broadcasted_iota(jnp.int32, (8, 128), 1)
    sub = lax.broadcasted_iota(jnp.int32, (8, 128), 0)
    tiles = [w[8 * i : 8 * i + 8, :] for i in range(16)]
    diagonal = [jnp.where(lane == 8 * i + sub, x, 0.0) for i, x in enumerate(tiles)]
    total = functools.reduce(jnp.add, diagonal)
    across = lax.rsqrt(jnp.broadcast_to(jnp.sum(total, axis=0, keepdims=True), (8, 128)))
    down = [
        lax.rsqrt(jnp.broadcast_to(jnp.sum(x, axis=1, keepdims=True), (8, 128))) for x in diagonal
    ]
    for i in range(16):
        w[8 * i : 8 * i + 8, :] = tiles[i] * down[i] * across
    return down, across


def invert(w, rounds, beside):
    lane = lax.broadcasted_iota(jnp.int32, (8, 128), 1)
    sub = lax.broadcasted_iota(jnp.int32, (8, 128), 0)
    lanes = lax.broadcasted_iota(jnp.int32, (128, 128), 1)
    down, across = scaled_diagonal(w)

    def at(t):
        return pl.ds(pl.multiple_of(8 * t, 8), 8)

    def panel(p, carry):
        rows, before, left_before = carry
        base = 8 * p
        base_before = (base + 120) % 128
        inside_before = (lane >= base - 8) & (lane < base)
        gone = (lanes >= base - 8) & (lanes < base)
        q = (p + 1) % 16
        following = w[at(q), :]
        now = swept_rows(rows, base, lane, sub)
        own = lane == 8 * q + sub
        entries = [
            jnp.broadcast_to(
                jnp.sum(jnp.where(own, row_of(rows, k), 0.0), axis=1, keepdims=True), (8, 128)
            )
            for k in range(8)
        ]
        following = less_pivots(
            following, base_before, [row_of(before, k) for k in range(8)], inside_before
        )
        inside = (lane >= base) & (lane < base + 8)
        following = jnp.where(inside, 0.0, following) - sum_of(
            [entries[k] * row_of(now, k) for k in range(8)]
        )
        w[:BLK, :] = jnp.where(gone, 0.0, w[:BLK, :]) - dot(left_before, outer_right(before))
        w[at((p + 16) % 17), :] = before
        return following, now, outer_left(rows)

    def turn(r, carry):
        for p in range(16 // rounds):
            carry = panel(r * (16 // rounds) + p, carry)
            if p == 0:
                beside(r)
        return carry

    start = (w[0:8, :], jnp.zeros((8, 128), F32), jnp.zeros((BLK, 48), BF16))
    _, last, left = lax.fori_loop(0, rounds, turn, start)
    w[:BLK, :] = jnp.where(lanes >= 120, 0.0, w[:BLK, :]) - dot(left, outer_right(last))
    w[120:128, :] = last
    for i in range(16):
        w[8 * i : 8 * i + 8, :] = -w[8 * i : 8 * i + 8, :] * down[i] * across


def halves(x):
    high = x.astype(BF16)
    return high, (x - high.astype(F32)).astype(BF16)


def put_left(ref, rows, x):
    high, low = halves(x)
    width = x.shape[1]
    ref[rows, :width] = high
    ref[rows, width : 2 * width] = high
    ref[rows, 2 * width : 3 * width] = low
    if ref.shape[1] > 3 * width:
        ref[rows, 3 * width :] = low


def put_right(ref, columns, x):
    high, low = halves(x)
    depth = x.shape[0]
    ref[:depth, columns] = high
    ref[depth : 2 * depth, columns] = low
    ref[2 * depth : 3 * depth, columns] = high
    if ref.shape[0] > 3 * depth:
        ref[3 * depth :, columns] = low


def dot(a, b):
    return jnp.dot(a, b, preferred_element_type=F32)


def eliminate(o, blocks, left, right, small_right, inverted):
    n = o.shape[0]
    whole = slice(None)
    eye = (
        lax.broadcasted_iota(jnp.int32, (BLK, BLK), 0)
        == lax.broadcasted_iota(jnp.int32, (BLK, BLK), 1)
    )

    def nothing(r):
        pass

    def prepare(j):
        at = pl.ds(pl.multiple_of(j * BLK, BLK), BLK)
        put_right(right, whole, o[at, :])
        put_right(right, at, jnp.where(eye, -1.0, 0.0))
        put_left(left, whole, o[:, at])
        put_right(small_right, whole, inverted[:BLK, :])
        for t in range(0, n, 256):
            put_left(left, slice(t, t + 256), dot(left[t : t + 256, :], small_right[...]))
        put_left(left, at, -inverted[:BLK, :])
        o[at, :] = jnp.zeros((BLK, n), F32)
        o[:, at] = jnp.zeros((n, BLK), F32)

    def update(size, t):
        these = pl.ds(pl.multiple_of(t * size, size), size)
        o[these, :] = o[these, :] - dot(left[these, :], right[...])

    inverted[:BLK, :] = o[:BLK, :BLK]
    invert(inverted, 16, nothing)

    def step(j, carry):
        prepare(j)
        after = pl.ds(pl.multiple_of((j + 1) * BLK, BLK), BLK)
        inverted[:BLK, :] = o[after, after] - dot(left[after, :], right[:, after])
        invert(inverted, ROUNDS, functools.partial(update, n // ROUNDS))
        return carry

    lax.fori_loop(0, blocks - 1, step, 0)
    prepare(blocks - 1)

    def tile(t, carry):
        update(512, t)
        return carry

    lax.fori_loop(0, n // 512, tile, 0)


def scratch_for(n):
    return [
        pltpu.VMEM((n, 4 * BLK), BF16),
        pltpu.VMEM((4 * BLK, n), BF16),
        pltpu.VMEM((4 * BLK, BLK), BF16),
        pltpu.VMEM((BLK + 8, BLK), F32),
    ]


def at_block(b):
    return pl.ds(pl.multiple_of(b * BLK, BLK), BLK)


LOWER = [(a, b) for y in range(4) for a in (y, 7 - y) for b in range(a + 1)]
SHARE = [(i, j) for i in range(4) for j in range(i + 1)]


def pack_update(o, tri):
    for t, (i, j) in enumerate(SHARE):
        tri[t * BLK : (t + 1) * BLK, :] = o[
            SEP1 + i * BLK : SEP1 + (i + 1) * BLK, SEP1 + j * BLK : SEP1 + (j + 1) * BLK
        ]


def first_kernel(blocks, lower_ref, o_ref, tri_ref, *scratch):
    for t, (a, b) in enumerate(LOWER):
        part = lower_ref[t]
        o_ref[a * BLK : (a + 1) * BLK, b * BLK : (b + 1) * BLK] = part
        if a != b:
            o_ref[b * BLK : (b + 1) * BLK, a * BLK : (a + 1) * BLK] = part.T
    eliminate(o_ref, blocks, *scratch)
    pack_update(o_ref, tri_ref)


def add_child(o_ref, update, maps, child):
    for t, (i, j) in enumerate(SHARE):
        rows, columns = at_block(maps[child, i]), at_block(maps[child, j])
        part = update[t * BLK : (t + 1) * BLK, :]
        o_ref[rows, columns] = o_ref[rows, columns] + part
        if i != j:
            o_ref[columns, rows] = o_ref[columns, rows] + part.T


def next_kernel(blocks, packs, members, map_ref, base_ref, mine_ref, other_ref, o_ref, *rest):
    tri_ref, scratch = (rest[0], rest[1:]) if packs else (None, rest)
    child = lax.axis_index("leaf") // members
    add_child(o_ref, mine_ref, map_ref, child)
    add_child(o_ref, other_ref, map_ref, child + 1 - 2 * (child % 2))
    eliminate(o_ref, blocks, *scratch)
    if packs:
        pack_update(o_ref, tri_ref)


def remote(source, target, sent, received, leaf, front):
    return pltpu.make_async_remote_copy(
        src_ref=source,
        dst_ref=target,
        send_sem=sent,
        recv_sem=received,
        device_id=(leaf, front),
        device_id_type=pl.DeviceIdType.MESH,
    )


def greet(devices):
    barrier = pltpu.get_barrier_semaphore()
    for device in devices:
        pl.semaphore_signal(
            barrier, inc=1, device_id=device, device_id_type=pl.DeviceIdType.MESH
        )
    pl.semaphore_wait(barrier, len(devices))


def exchange_kernel(distance, tri_ref, entries_ref, o_ref, base_ref, sent, got, copied):
    leaf, y = lax.axis_index("leaf"), lax.axis_index("front")
    n = base_ref.shape[0]
    start = pl.multiple_of((leaf // (2 * distance)) % (entries_ref.shape[0] // n) * n, 8)
    fetch = pltpu.make_async_copy(entries_ref.at[pl.ds(start, n), :], base_ref, copied)
    fetch.start()
    core, x = leaf % 2, (leaf // 2) % 4
    z = leaf // 8
    sibling = leaf + distance * (1 - 2 * ((leaf // distance) % 2))
    other_core = leaf + 1 - 2 * core
    rows = tri_ref.shape[0] // 32
    apart = [(dx, dy) for dx in (0, 1, 3, 2) for dy in (0, 1, 3, 2)]

    def place(dx, dy):
        return z * 8 + ((x + dx) % 4) * 2 + core, (y + dy) % 4

    greet([(sibling, y), (other_core, y)] + [place(dx, dy) for dx, dy in apart[1:]])

    def share(c, xx, yy):
        return pl.ds(pl.multiple_of(((c * 4 + xx) * 4 + yy) * rows, 8), rows)

    mine = share(core, x, y)
    across = remote(tri_ref.at[mine], o_ref.at[mine], sent.at[0], got.at[0], sibling, y)
    across.start()
    across.wait_recv()
    spread = []
    for t, (dx, dy) in enumerate(apart):
        if t:
            spread.append(
                remote(o_ref.at[mine], o_ref.at[mine], sent.at[t], got.at[t], *place(dx, dy))
            )
            spread[-1].start()
    last = []
    for t, (dx, dy) in enumerate(apart):
        if t:
            spread[t - 1].wait_recv()
        piece = share(core, (x - dx + 4) % 4, (y - dy + 4) % 4)
        last.append(
            remote(o_ref.at[piece], o_ref.at[piece], sent.at[16 + t], got.at[16 + t], other_core, y)
        )
        last[-1].start()
    for copy in last:
        copy.wait_recv()
    for copy in [across] + spread + last:
        copy.wait_send()
    fetch.wait()


def gather_kernel(
    map_ref, leaf_ref, entries_ref, o_ref,
    met, partial, halves_in, own_entries, found_tile, table, told,
    keep, sent, got, sent_e, got_e, sent_y, got_y, sent_x, got_x, sent_c, got_c,
):
    leaf, y = lax.axis_index("leaf"), lax.axis_index("front")
    m = leaf % 16
    base = leaf - m
    core, x, z = m % 2, (m // 2) % 4, m // 8
    met[:, 4] = jnp.zeros((16, 8, BLK), F32)
    greet(
        [(base + (m + d) % 16, y) for d in range(1, 16)] + [(leaf, (y + d) % 4) for d in (1, 2, 3)]
    )

    kept = pltpu.make_async_copy(leaf_ref.at[:, m], met.at[m, 0:4], keep.at[0])
    kept.start()
    members = []
    for d in range(1, 16):
        to = (m + d) % 16
        members.append(
            remote(leaf_ref.at[:, to], met.at[m, 0:4], sent.at[d], got.at[d], base + to, y)
        )
        members[-1].start()
    a, half = m // 2, m % 2
    for g in range(8):
        to = half * 8 + g
        source = entries_ref.at[pl.ds(8 * g, 8), :]

        @pl.when(to == m)
        def _():
            pltpu.make_async_copy(source, own_entries.at[a], got_e.at[a]).start()

        @pl.when(to != m)
        def _():
            remote(source, own_entries.at[a], sent_e.at[g], got_e.at[a], base + to, y).start()

    lane = lax.broadcasted_iota(jnp.int32, (16, BLK), 1)
    group = (
        (lane >= 9).astype(jnp.int32) + (lane >= 18).astype(jnp.int32) + (lane >= 27).astype(jnp.int32)
    )
    within = lane - 9 * group
    second = within > group
    block_row = jnp.where(second, 7 - group, group)
    block_column = jnp.where(second, within - group - 1, within)
    maps = map_ref[pl.ds(pl.multiple_of(base, 16), 16), :]
    found = jnp.full((16, BLK), 4, jnp.int32)
    landing = jnp.zeros((16, BLK), jnp.int32)
    for i in range(4):
        target = jnp.broadcast_to(maps[:, i : i + 1], (16, BLK))
        found = jnp.where(block_row == target, i, found)
        landing = landing + target * jnp.where(y == i, 1, 0)
    found_tile[...] = jnp.where(block_column == landing, found, 4)
    tell = pltpu.make_async_copy(found_tile, table, told)
    tell.start()
    tell.wait()
    kept.wait()
    for copy in members:
        copy.wait_recv()

    def sum_block(t, carry):
        terms = [met[s, table[s, t]] for s in range(16)]
        while len(terms) > 1:
            terms = [terms[i] + terms[i + 1] for i in range(0, len(terms), 2)]
        partial[t] = terms[0]
        return carry

    lax.fori_loop(0, 36, sum_block, 0)
    for k in range(8):
        pltpu.make_async_copy(
            entries_ref.at[pl.ds(0, 8), :], own_entries.at[k], got_e.at[k]
        ).wait()
    for k in range(8):
        first = 9 * k if k < 4 else 9 * (7 - k) + 8 - k
        for h in range(2):
            b = 2 * y + h

            @pl.when(b <= k)
            def _():
                partial[first + b] = (
                    partial[first + b] + own_entries[k, :, h * BLK : (h + 1) * BLK]
                )

    to_sum = []
    for d in (1, 2, 3):
        to = (y + d) % 4
        to_sum.append(
            remote(
                partial.at[pl.ds(9 * to, 9)], halves_in.at[d - 1],
                sent_y.at[d - 1], got_y.at[d - 1], leaf, to,
            )
        )
        to_sum[-1].start()
    for copy in to_sum:
        copy.wait_recv()
    rows = pl.ds(pl.multiple_of(m * 8, 8), 8)
    for t in range(9):
        o_ref[9 * y + t, rows, :] = (
            partial[9 * y + t] + halves_in[0, t] + halves_in[1, t] + halves_in[2, t]
        )
    spread = []
    own = o_ref.at[pl.ds(9 * y, 9), rows, :]
    for d in (1, 2, 3):
        spread.append(
            remote(own, own, sent_y.at[2 + d], got_y.at[2 + d], leaf, (y + d) % 4)
        )
        spread[-1].start()
    for copy in spread:
        copy.wait_recv()

    other_z = base + (m + 8) % 16
    other_core = base + m + 1 - 2 * core

    def piece(xx, zz, part):
        slot = pl.ds(pl.multiple_of((zz * 8 + xx * 2 + core) * 8, 8), 8)
        return o_ref.at[18 * part : 18 * part + 18, slot, :]

    def step_x(xx, zz, part, direction, slot):
        to = base + z * 8 + ((x + direction + 4) % 4) * 2 + core
        ref = piece(xx, zz, part)
        return remote(ref, ref, sent_x.at[slot], got_x.at[slot], to, y)

    def to_core(xx, zz, part, slot):
        ref = piece(xx, zz, part)
        return remote(ref, ref, sent_c.at[slot], got_c.at[slot], other_core, y)

    started = []

    def begin(copy):
        copy.start()
        started.append(copy)
        return copy

    left, right, far = (x + 3) % 4, (x + 1) % 4, (x + 2) % 4
    other = 1 - z
    over_z = []
    for part in range(2):
        ref = piece(x, z, part)
        over_z.append(begin(remote(ref, ref, sent_y.at[6 + part], got_y.at[6 + part], other_z, y)))
    passes, cores = [], []
    for stage, zz in ((0, z), (1, other)):
        if stage:
            for copy in over_z:
                copy.wait_recv()
        s = 6 * stage
        passes.append(
            [begin(step_x(x, zz, part, 1, s + part)) for part in range(2)]
            + [begin(step_x(x, zz, part, -1, s + 2 + part)) for part in range(2)]
        )
        for part in range(2):
            cores.append(begin(to_core(x, zz, part, 8 * stage + part)))
    for stage, zz in ((0, z), (1, other)):
        s = 6 * stage
        c = 8 * stage
        moves = passes[stage]
        moves[0].wait_recv()
        relay_right = begin(step_x(left, zz, 0, 1, s + 4))
        cores.append(begin(to_core(left, zz, 0, c + 2)))
        moves[3].wait_recv()
        relay_left = begin(step_x(right, zz, 1, -1, s + 5))
        cores.append(begin(to_core(right, zz, 1, c + 3)))
        moves[1].wait_recv()
        cores.append(begin(to_core(left, zz, 1, c + 4)))
        moves[2].wait_recv()
        cores.append(begin(to_core(right, zz, 0, c + 5)))
        passes.append((relay_right, relay_left))
    for stage, zz in ((0, z), (1, other)):
        relay_right, relay_left = passes[2 + stage]
        c = 8 * stage
        relay_right.wait_recv()
        cores.append(begin(to_core(far, zz, 0, c + 6)))
        relay_left.wait_recv()
        cores.append(begin(to_core(far, zz, 1, c + 7)))
    for copy in cores:
        copy.wait_recv()
    for copy in members + to_sum + spread + started:
        copy.wait_send()
    for g in range(8):
        to = half * 8 + g

        @pl.when(to != m)
        def _():
            remote(
                entries_ref.at[pl.ds(8 * g, 8), :], own_entries.at[a],
                sent_e.at[g], got_e.at[a], base + to, y,
            ).wait_send()


VMEM_SPEC = pl.BlockSpec(memory_space=pltpu.VMEM)
SMEM_SPEC = pl.BlockSpec(memory_space=pltpu.SMEM)
PARAMS = pltpu.CompilerParams(vmem_limit_bytes=24 * 1024 * 1024)


def gathered(map_leaf, leaf_update, entries):
    dma = pltpu.SemaphoreType.DMA
    return pl.pallas_call(
        gather_kernel,
        out_shape=jax.ShapeDtypeStruct((36, BLK, BLK), F32),
        in_specs=[VMEM_SPEC, VMEM_SPEC, VMEM_SPEC],
        out_specs=VMEM_SPEC,
        scratch_shapes=[
            pltpu.VMEM((16, 5, 8, BLK), F32),
            pltpu.VMEM((36, 8, BLK), F32),
            pltpu.VMEM((3, 9, 8, BLK), F32),
            pltpu.VMEM((8, 8, 256), F32),
            pltpu.VMEM((16, BLK), jnp.int32),
            pltpu.SMEM((16, BLK), jnp.int32),
            dma,
            dma((1,)), dma((16,)), dma((16,)), dma((8,)), dma((8,)), dma((8,)), dma((8,)),
            dma((12,)), dma((12,)), dma((16,)), dma((16,)),
        ],
        compiler_params=pltpu.CompilerParams(
            vmem_limit_bytes=32 * 1024 * 1024, collective_id=0, has_side_effects=True
        ),
    )(map_leaf, leaf_update.reshape(4, 16, 8, BLK), entries)


def exchanged(tri, entries, distance, collective_id):
    dma = pltpu.SemaphoreType.DMA
    n = 8 * BLK
    return pl.pallas_call(
        functools.partial(exchange_kernel, distance),
        out_shape=(jax.ShapeDtypeStruct(tri.shape, F32), jax.ShapeDtypeStruct((n, n), F32)),
        in_specs=[VMEM_SPEC, pl.BlockSpec(memory_space=pltpu.HBM)],
        out_specs=(VMEM_SPEC, VMEM_SPEC),
        scratch_shapes=[dma((32,)), dma((32,)), dma],
        compiler_params=pltpu.CompilerParams(
            vmem_limit_bytes=(43 if collective_id == 1 else 16) * 1024 * 1024, collective_id=collective_id, has_side_effects=True
        ),
    )(tri, entries)


def first_eliminated(lower, blocks):
    n = 8 * BLK
    return pl.pallas_call(
        functools.partial(first_kernel, blocks),
        out_shape=(
            jax.ShapeDtypeStruct((n, n), F32),
            jax.ShapeDtypeStruct((10 * BLK, BLK), F32),
        ),
        in_specs=[VMEM_SPEC],
        out_specs=(VMEM_SPEC, VMEM_SPEC),
        scratch_shapes=scratch_for(n),
        compiler_params=PARAMS,
    )(lower)


def next_eliminated(maps, base, mine, other, blocks, packs, members):
    n = 8 * BLK
    out = [jax.ShapeDtypeStruct((n, n), F32)]
    if packs:
        out.append(jax.ShapeDtypeStruct((10 * BLK, BLK), F32))
    return pl.pallas_call(
        functools.partial(next_kernel, blocks, packs, members),
        out_shape=tuple(out),
        in_specs=[SMEM_SPEC, VMEM_SPEC, VMEM_SPEC, VMEM_SPEC],
        out_specs=tuple([VMEM_SPEC] * len(out)),
        scratch_shapes=scratch_for(n),
        input_output_aliases={1: 0},
        compiler_params=PARAMS,
    )(maps, base, mine, other)


def columns_of_inverse(swept, sigma, sigma_left, coupling_left, blocks, value, value_right, out):
    half = 4 * BLK
    for t, block in enumerate(blocks):
        here = slice(t * BLK, (t + 1) * BLK)

        @pl.when(block < 4)
        def _():
            put_right(value_right, here, swept[half:, at_block(block)])
            out[:half, here] = -swept[:half, at_block(block)]

        @pl.when(block >= 4)
        def _():
            value_right[:, here] = jnp.zeros((3 * half, BLK), BF16)
            out[:half, here] = jnp.zeros((half, BLK), F32)

    width = len(blocks) * BLK
    value[:, :width] = -dot(sigma_left[...], value_right[:, :width])
    for t, block in enumerate(blocks):
        here = slice(t * BLK, (t + 1) * BLK)

        @pl.when(block >= 4)
        def _():
            value[:, here] = sigma[:, at_block(block - 4)]

        lower = value[:, here]
        put_right(value_right, here, lower)
        out[half:, here] = lower
    out[:half, :width] = out[:half, :width] - dot(coupling_left[...], value_right[:, :width])


def back_kernel(
    top_ref, mid_ref, leaf_ref, one_ref, two_ref, three_ref, o_ref,
    sigma, sigma_left, coupling_left, value, value_right, columns, lower,
):
    half = 4 * BLK
    whole = slice(None)
    leaf = lax.axis_index("leaf")
    first_node, second_node = leaf // 16, leaf // 32
    for i in range(4):
        for j in range(4):
            picked = three_ref[
                at_block(top_ref[second_node, i]), at_block(top_ref[second_node, j])
            ]
            sigma[i * BLK : (i + 1) * BLK, j * BLK : (j + 1) * BLK] = -picked
    put_left(sigma_left, whole, sigma[...])
    put_left(coupling_left, whole, two_ref[:half, half:])
    blocks = [mid_ref[first_node, j] for j in range(4)]
    columns_of_inverse(
        two_ref, sigma, sigma_left, coupling_left, blocks, value, value_right, columns
    )
    for i in range(4):
        lower[i * BLK : (i + 1) * BLK, :] = columns[at_block(blocks[i]), :]
    put_left(sigma_left, whole, lower[...])
    put_left(coupling_left, whole, one_ref[:half, half:])
    columns_of_inverse(
        one_ref, lower, sigma_left, coupling_left, [leaf_ref[leaf, lax.axis_index("front")]],
        value, value_right, columns,
    )
    for i in range(4):
        o_ref[i * BLK : (i + 1) * BLK, :] = columns[at_block(leaf_ref[leaf, i]), :BLK]


def back_substituted(top, mid, leaf, one, two, three):
    half = 4 * BLK
    return pl.pallas_call(
        back_kernel,
        out_shape=jax.ShapeDtypeStruct((half, BLK), F32),
        in_specs=[SMEM_SPEC] * 3 + [VMEM_SPEC] * 3,
        out_specs=VMEM_SPEC,
        scratch_shapes=[
            pltpu.VMEM((half, half), F32),
            pltpu.VMEM((half, 3 * half), BF16),
            pltpu.VMEM((half, 3 * half), BF16),
            pltpu.VMEM((half, half), F32),
            pltpu.VMEM((3 * half, half), BF16),
            pltpu.VMEM((2 * half, half), F32),
            pltpu.VMEM((half, half), F32),
        ],
        compiler_params=PARAMS,
    )(top, mid, leaf, one, two, three)


def body(leaf_update, front_entries1, front_entries2, front_entries3, map_leaf, map_mid, map_top):
    members = lax.axis_size("leaf") // 4
    lower = gathered(map_leaf, leaf_update, front_entries1)
    one, update = first_eliminated(lower, SEP1 // BLK)
    other, base = exchanged(update, front_entries2, members, 1)
    two, update = next_eliminated(map_mid, base, update, other, SEP2 // BLK, True, members)
    other, base = exchanged(update, front_entries3, 2 * members, 2)
    (three,) = next_eliminated(map_top, base, update, other, SEP3 // BLK, False, 2 * members)
    return back_substituted(map_top, map_mid, map_leaf, one, two, three)


def solution(mesh):
    in_specs = (P("leaf", "front"), P("leaf", "front"), P(), P(), P(), P(), P())
    out_specs = P("leaf", "front")
    return jax.shard_map(body, mesh=mesh, in_specs=in_specs, out_specs=out_specs, check_vma=False)
```

```python
import functools

import jax
import jax.numpy as jnp
from jax import lax
from jax.experimental import pallas as pl
from jax.experimental.pallas import tpu as pltpu
from jax.sharding import PartitionSpec as P

BLK = 128
SEP1 = 512
SEP2 = 512
SEP3 = 1024
RUP = 512


F32, BF16 = jnp.float32, jnp.bfloat16
ROUNDS = 4


def row_of(x, k):
    return jnp.broadcast_to(x[k : k + 1, :], (8, 128))


def along(x, c):
    return jnp.take_along_axis(x, jnp.full((8, 128), c, jnp.int32), axis=1)


def thirds(x):
    high = x.astype(BF16)
    rest = x - high.astype(F32)
    middle = rest.astype(BF16)
    return high, middle, (rest - middle.astype(F32)).astype(BF16)


def outer_left(p):
    high, middle, low = thirds(p)
    return jnp.concatenate([high, high, high, middle, middle, low], axis=0).T


def outer_right(s):
    high, middle, low = thirds(s)
    return jnp.concatenate([high, middle, low, high, middle, high], axis=0)


def swept_rows(rows, base, lane, sub):
    e = [along(rows, base + j) for j in range(8)]
    inside = (lane >= base) & (lane < base + 8)
    m = jnp.where(lane == base + sub, -1.0, jnp.where(inside, 0.0, rows))
    for k in range(0, 8, 2):
        a, b, d = row_of(e[k], k), row_of(e[k + 1], k), row_of(e[k + 1], k + 1)
        is_first, is_second = sub == k, sub == k + 1
        pair = is_first | is_second
        left = jnp.where(is_first, -1.0, jnp.where(is_second, 0.0, e[k]))
        right = jnp.where(is_second, -1.0, jnp.where(is_first, 0.0, e[k + 1]))
        scale = 1.0 / (a * d - b * b)
        by_first = (d * left - b * right) * scale
        by_second = (a * right - b * left) * scale

        def go(t):
            return jnp.where(pair, 0.0, t) - by_first * row_of(t, k) - by_second * row_of(t, k + 1)

        m = go(m)
        e = [go(x) if j > k + 1 else x for j, x in enumerate(e)]
    return m


def sum_of(terms):
    while len(terms) > 1:
        terms = [terms[i] + terms[i + 1] for i in range(0, len(terms), 2)]
    return terms[0]


def less_pivots(x, base, rows, inside):
    total = None
    for k in range(0, 8, 2):
        term = along(x, base + k) * rows[k] + along(x, base + k + 1) * rows[k + 1]
        total = term if total is None else total + term
    return jnp.where(inside, 0.0, x) - total


def scaled_diagonal(w):
    lane = lax.broadcasted_iota(jnp.int32, (8, 128), 1)
    sub = lax.broadcasted_iota(jnp.int32, (8, 128), 0)
    tiles = [w[8 * i : 8 * i + 8, :] for i in range(16)]
    diagonal = [jnp.where(lane == 8 * i + sub, x, 0.0) for i, x in enumerate(tiles)]
    total = functools.reduce(jnp.add, diagonal)
    across = lax.rsqrt(jnp.broadcast_to(jnp.sum(total, axis=0, keepdims=True), (8, 128)))
    down = [
        lax.rsqrt(jnp.broadcast_to(jnp.sum(x, axis=1, keepdims=True), (8, 128))) for x in diagonal
    ]
    for i in range(16):
        w[8 * i : 8 * i + 8, :] = tiles[i] * down[i] * across
    return down, across


def invert(w, rounds, beside):
    lane = lax.broadcasted_iota(jnp.int32, (8, 128), 1)
    sub = lax.broadcasted_iota(jnp.int32, (8, 128), 0)
    lanes = lax.broadcasted_iota(jnp.int32, (128, 128), 1)
    down, across = scaled_diagonal(w)

    def at(t):
        return pl.ds(pl.multiple_of(8 * t, 8), 8)

    def panel(p, carry):
        rows, before, left_before = carry
        base = 8 * p
        base_before = (base + 120) % 128
        inside_before = (lane >= base - 8) & (lane < base)
        gone = (lanes >= base - 8) & (lanes < base)
        q = (p + 1) % 16
        following = w[at(q), :]
        now = swept_rows(rows, base, lane, sub)
        own = lane == 8 * q + sub
        entries = [
            jnp.broadcast_to(
                jnp.sum(jnp.where(own, row_of(rows, k), 0.0), axis=1, keepdims=True), (8, 128)
            )
            for k in range(8)
        ]
        following = less_pivots(
            following, base_before, [row_of(before, k) for k in range(8)], inside_before
        )
        inside = (lane >= base) & (lane < base + 8)
        following = jnp.where(inside, 0.0, following) - sum_of(
            [entries[k] * row_of(now, k) for k in range(8)]
        )
        w[:BLK, :] = jnp.where(gone, 0.0, w[:BLK, :]) - dot(left_before, outer_right(before))
        w[at((p + 16) % 17), :] = before
        return following, now, outer_left(rows)

    def turn(r, carry):
        for p in range(16 // rounds):
            carry = panel(r * (16 // rounds) + p, carry)
            if p == 1:
                beside(r)
        return carry

    start = (w[0:8, :], jnp.zeros((8, 128), F32), jnp.zeros((BLK, 48), BF16))
    _, last, left = lax.fori_loop(0, rounds, turn, start)
    w[:BLK, :] = jnp.where(lanes >= 120, 0.0, w[:BLK, :]) - dot(left, outer_right(last))
    w[120:128, :] = last
    for i in range(16):
        w[8 * i : 8 * i + 8, :] = -w[8 * i : 8 * i + 8, :] * down[i] * across


def halves(x):
    high = x.astype(BF16)
    return high, (x - high.astype(F32)).astype(BF16)


def put_left(ref, rows, x):
    high, low = halves(x)
    width = x.shape[1]
    ref[rows, :width] = high
    ref[rows, width : 2 * width] = high
    ref[rows, 2 * width : 3 * width] = low
    if ref.shape[1] > 3 * width:
        ref[rows, 3 * width :] = low


def put_right(ref, columns, x):
    high, low = halves(x)
    depth = x.shape[0]
    ref[:depth, columns] = high
    ref[depth : 2 * depth, columns] = low
    ref[2 * depth : 3 * depth, columns] = high
    if ref.shape[0] > 3 * depth:
        ref[3 * depth :, columns] = low


def dot(a, b):
    return jnp.dot(a, b, preferred_element_type=F32)


def eliminate(o, blocks, left, right, small_right, inverted):
    n = o.shape[0]
    whole = slice(None)
    eye = (
        lax.broadcasted_iota(jnp.int32, (BLK, BLK), 0)
        == lax.broadcasted_iota(jnp.int32, (BLK, BLK), 1)
    )

    def nothing(r):
        pass

    def prepare(j):
        at = pl.ds(pl.multiple_of(j * BLK, BLK), BLK)
        put_right(right, whole, o[at, :])
        put_right(right, at, jnp.where(eye, -1.0, 0.0))
        put_left(left, whole, o[:, at])
        put_right(small_right, whole, inverted[:BLK, :])
        for t in range(0, n, 256):
            put_left(left, slice(t, t + 256), dot(left[t : t + 256, :], small_right[...]))
        put_left(left, at, -inverted[:BLK, :])
        o[at, :] = jnp.zeros((BLK, n), F32)
        o[:, at] = jnp.zeros((n, BLK), F32)

    def update(size, t):
        these = pl.ds(pl.multiple_of(t * size, size), size)
        o[these, :] = o[these, :] - dot(left[these, :], right[...])

    inverted[:BLK, :] = o[:BLK, :BLK]
    invert(inverted, 16, nothing)

    def step(j, carry):
        prepare(j)
        after = pl.ds(pl.multiple_of((j + 1) * BLK, BLK), BLK)
        inverted[:BLK, :] = o[after, after] - dot(left[after, :], right[:, after])
        invert(inverted, ROUNDS, functools.partial(update, n // ROUNDS))
        return carry

    lax.fori_loop(0, blocks - 1, step, 0)
    prepare(blocks - 1)

    def tile(t, carry):
        update(512, t)
        return carry

    lax.fori_loop(0, n // 512, tile, 0)


def scratch_for(n):
    return [
        pltpu.VMEM((n, 4 * BLK), BF16),
        pltpu.VMEM((4 * BLK, n), BF16),
        pltpu.VMEM((4 * BLK, BLK), BF16),
        pltpu.VMEM((BLK + 8, BLK), F32),
    ]


def at_block(b):
    return pl.ds(pl.multiple_of(b * BLK, BLK), BLK)


LOWER = [(a, b) for y in range(4) for a in (y, 7 - y) for b in range(a + 1)]
SHARE = [(i, j) for i in range(4) for j in range(i + 1)]


def pack_update(o, tri):
    for t, (i, j) in enumerate(SHARE):
        tri[t * BLK : (t + 1) * BLK, :] = o[
            SEP1 + i * BLK : SEP1 + (i + 1) * BLK, SEP1 + j * BLK : SEP1 + (j + 1) * BLK
        ]


def first_kernel(blocks, lower_ref, o_ref, tri_ref, *scratch):
    for t, (a, b) in enumerate(LOWER):
        part = lower_ref[t]
        o_ref[a * BLK : (a + 1) * BLK, b * BLK : (b + 1) * BLK] = part
        if a != b:
            o_ref[b * BLK : (b + 1) * BLK, a * BLK : (a + 1) * BLK] = part.T
    eliminate(o_ref, blocks, *scratch)
    pack_update(o_ref, tri_ref)


def add_child(o_ref, update, maps, child):
    for t, (i, j) in enumerate(SHARE):
        rows, columns = at_block(maps[child, i]), at_block(maps[child, j])
        part = update[t * BLK : (t + 1) * BLK, :]
        o_ref[rows, columns] = o_ref[rows, columns] + part
        if i != j:
            o_ref[columns, rows] = o_ref[columns, rows] + part.T


def next_kernel(blocks, members, map_ref, base_ref, mine_ref, other_ref, o_ref, *rest):
    tri_ref, scratch = rest[0], rest[1:]
    child = lax.axis_index("leaf") // members
    add_child(o_ref, mine_ref, map_ref, child)
    add_child(o_ref, other_ref, map_ref, child + 1 - 2 * (child % 2))
    eliminate(o_ref, blocks, *scratch)
    pack_update(o_ref, tri_ref)


def top_kernel(
    members, map_ref, base_ref, mine_ref, other_ref, sigma_ref,
    order, position, o, low, left, right, small_right, inverted, low_left, low_right,
):
    child = lax.axis_index("leaf") // members
    other = child + 1 - 2 * (child % 2)
    count = jnp.int32(0)
    for b in range(8):
        named = jnp.int32(-1)
        for i in range(4):
            named = jnp.where(map_ref[child, i] == b, 4 + i, named)
        spot = jnp.where(named < 0, count, named)
        count = count + jnp.where(named < 0, 1, 0)
        order[spot] = b
        position[b] = spot
    for p in range(8):
        for q in range(8):
            o[p * BLK : (p + 1) * BLK, q * BLK : (q + 1) * BLK] = base_ref[
                at_block(order[p]), at_block(order[q])
            ]
    half = 4 * BLK
    for t, (i, j) in enumerate(SHARE):
        part = mine_ref[t * BLK : (t + 1) * BLK, :]
        rows = slice(half + i * BLK, half + (i + 1) * BLK)
        columns = slice(half + j * BLK, half + (j + 1) * BLK)
        o[rows, columns] = o[rows, columns] + part
        if i != j:
            o[columns, rows] = o[columns, rows] + part.T
    for t, (i, j) in enumerate(SHARE):
        part = other_ref[t * BLK : (t + 1) * BLK, :]
        rows, columns = at_block(position[map_ref[other, i]]), at_block(position[map_ref[other, j]])
        o[rows, columns] = o[rows, columns] + part
        if i != j:
            o[columns, rows] = o[columns, rows] + part.T
    eliminate(o, 4, left, right, small_right, inverted)
    low[...] = o[half:, half:]
    eliminate(low, 4, low_left, low_right, small_right, inverted)
    sigma_ref[...] = low[...]


def top_inverse(maps, base, mine, other, members):
    n, half = 8 * BLK, 4 * BLK
    return pl.pallas_call(
        functools.partial(top_kernel, members),
        out_shape=jax.ShapeDtypeStruct((half, half), F32),
        in_specs=[SMEM_SPEC, VMEM_SPEC, VMEM_SPEC, VMEM_SPEC],
        out_specs=VMEM_SPEC,
        scratch_shapes=[
            pltpu.SMEM((8,), jnp.int32),
            pltpu.SMEM((8,), jnp.int32),
            pltpu.VMEM((n, n), F32),
            pltpu.VMEM((half, half), F32),
        ]
        + scratch_for(n)
        + scratch_for(half)[:2],
        compiler_params=PARAMS,
    )(maps, base, mine, other)


def remote(source, target, sent, received, leaf, front):
    return pltpu.make_async_remote_copy(
        src_ref=source,
        dst_ref=target,
        send_sem=sent,
        recv_sem=received,
        device_id=(leaf, front),
        device_id_type=pl.DeviceIdType.MESH,
    )


def greet(devices):
    barrier = pltpu.get_barrier_semaphore()
    for device in devices:
        pl.semaphore_signal(
            barrier, inc=1, device_id=device, device_id_type=pl.DeviceIdType.MESH
        )
    pl.semaphore_wait(barrier, len(devices))


def exchange_kernel(distance, tri_ref, entries_ref, o_ref, base_ref, sent, got, copied):
    leaf, y = lax.axis_index("leaf"), lax.axis_index("front")
    n = base_ref.shape[0]
    start = pl.multiple_of((leaf // (2 * distance)) % (entries_ref.shape[0] // n) * n, 8)
    fetch = pltpu.make_async_copy(entries_ref.at[pl.ds(start, n), :], base_ref, copied)
    fetch.start()
    core, x = leaf % 2, (leaf // 2) % 4
    z = leaf // 8
    sibling = leaf + distance * (1 - 2 * ((leaf // distance) % 2))
    other_core = leaf + 1 - 2 * core
    rows = tri_ref.shape[0] // 32
    apart = [(dx, dy) for dx in (0, 1, 3, 2) for dy in (0, 1, 3, 2)]

    def place(dx, dy):
        return z * 8 + ((x + dx) % 4) * 2 + core, (y + dy) % 4

    greet([(sibling, y), (other_core, y)] + [place(dx, dy) for dx, dy in apart[1:]])

    def share(c, xx, yy):
        return pl.ds(pl.multiple_of(((c * 4 + xx) * 4 + yy) * rows, 8), rows)

    mine = share(core, x, y)
    across = remote(tri_ref.at[mine], o_ref.at[mine], sent.at[0], got.at[0], sibling, y)
    across.start()
    across.wait_recv()
    spread = []
    for t, (dx, dy) in enumerate(apart):
        if t:
            spread.append(
                remote(o_ref.at[mine], o_ref.at[mine], sent.at[t], got.at[t], *place(dx, dy))
            )
            spread[-1].start()
    last = []
    for t, (dx, dy) in enumerate(apart):
        if t:
            spread[t - 1].wait_recv()
        piece = share(core, (x - dx + 4) % 4, (y - dy + 4) % 4)
        last.append(
            remote(o_ref.at[piece], o_ref.at[piece], sent.at[16 + t], got.at[16 + t], other_core, y)
        )
        last[-1].start()
    for copy in last:
        copy.wait_recv()
    for copy in [across] + spread + last:
        copy.wait_send()
    fetch.wait()


def gather_kernel(
    map_ref, leaf_ref, entries_ref, o_ref,
    met, partial, halves_in, own_entries, found_tile, table, told,
    keep, sent, got, sent_e, got_e, sent_y, got_y, sent_x, got_x, sent_c, got_c,
):
    leaf, y = lax.axis_index("leaf"), lax.axis_index("front")
    m = leaf % 16
    base = leaf - m
    core, x, z = m % 2, (m // 2) % 4, m // 8
    met[:, 4] = jnp.zeros((16, 8, BLK), F32)
    greet(
        [(base + (m + d) % 16, y) for d in range(1, 16)] + [(leaf, (y + d) % 4) for d in (1, 2, 3)]
    )

    kept = pltpu.make_async_copy(leaf_ref.at[:, m], met.at[m, 0:4], keep.at[0])
    kept.start()
    members = []
    for d in range(1, 16):
        to = (m + d) % 16
        members.append(
            remote(leaf_ref.at[:, to], met.at[m, 0:4], sent.at[d], got.at[d], base + to, y)
        )
        members[-1].start()
    a, half = m // 2, m % 2
    for g in range(8):
        to = half * 8 + g
        source = entries_ref.at[pl.ds(8 * g, 8), :]

        @pl.when(to == m)
        def _():
            pltpu.make_async_copy(source, own_entries.at[a], got_e.at[a]).start()

        @pl.when(to != m)
        def _():
            remote(source, own_entries.at[a], sent_e.at[g], got_e.at[a], base + to, y).start()

    lane = lax.broadcasted_iota(jnp.int32, (16, BLK), 1)
    group = (
        (lane >= 9).astype(jnp.int32) + (lane >= 18).astype(jnp.int32) + (lane >= 27).astype(jnp.int32)
    )
    within = lane - 9 * group
    second = within > group
    block_row = jnp.where(second, 7 - group, group)
    block_column = jnp.where(second, within - group - 1, within)
    maps = map_ref[pl.ds(pl.multiple_of(base, 16), 16), :]
    found = jnp.full((16, BLK), 4, jnp.int32)
    landing = jnp.zeros((16, BLK), jnp.int32)
    for i in range(4):
        target = jnp.broadcast_to(maps[:, i : i + 1], (16, BLK))
        found = jnp.where(block_row == target, i, found)
        landing = landing + target * jnp.where(y == i, 1, 0)
    found_tile[...] = jnp.where(block_column == landing, found, 4)
    tell = pltpu.make_async_copy(found_tile, table, told)
    tell.start()
    tell.wait()
    kept.wait()
    for copy in members:
        copy.wait_recv()

    def sum_block(t, carry):
        terms = [met[s, table[s, t]] for s in range(16)]
        while len(terms) > 1:
            terms = [terms[i] + terms[i + 1] for i in range(0, len(terms), 2)]
        partial[t] = terms[0]
        return carry

    lax.fori_loop(0, 36, sum_block, 0)
    for k in range(8):
        pltpu.make_async_copy(
            entries_ref.at[pl.ds(0, 8), :], own_entries.at[k], got_e.at[k]
        ).wait()
    for k in range(8):
        first = 9 * k if k < 4 else 9 * (7 - k) + 8 - k
        for h in range(2):
            b = 2 * y + h

            @pl.when(b <= k)
            def _():
                partial[first + b] = (
                    partial[first + b] + own_entries[k, :, h * BLK : (h + 1) * BLK]
                )

    to_sum = []
    for d in (1, 2, 3):
        to = (y + d) % 4
        to_sum.append(
            remote(
                partial.at[pl.ds(9 * to, 9)], halves_in.at[d - 1],
                sent_y.at[d - 1], got_y.at[d - 1], leaf, to,
            )
        )
        to_sum[-1].start()
    for copy in to_sum:
        copy.wait_recv()
    rows = pl.ds(pl.multiple_of(m * 8, 8), 8)
    for t in range(9):
        o_ref[9 * y + t, rows, :] = (
            partial[9 * y + t] + halves_in[0, t] + halves_in[1, t] + halves_in[2, t]
        )
    spread = []
    own = o_ref.at[pl.ds(9 * y, 9), rows, :]
    for d in (1, 2, 3):
        spread.append(
            remote(own, own, sent_y.at[2 + d], got_y.at[2 + d], leaf, (y + d) % 4)
        )
        spread[-1].start()
    for copy in spread:
        copy.wait_recv()

    other_z = base + (m + 8) % 16
    other_core = base + m + 1 - 2 * core

    def piece(xx, zz, part):
        slot = pl.ds(pl.multiple_of((zz * 8 + xx * 2 + core) * 8, 8), 8)
        return o_ref.at[18 * part : 18 * part + 18, slot, :]

    def step_x(xx, zz, part, direction, slot):
        to = base + z * 8 + ((x + direction + 4) % 4) * 2 + core
        ref = piece(xx, zz, part)
        return remote(ref, ref, sent_x.at[slot], got_x.at[slot], to, y)

    def to_core(xx, zz, part, slot):
        ref = piece(xx, zz, part)
        return remote(ref, ref, sent_c.at[slot], got_c.at[slot], other_core, y)

    started = []

    def begin(copy):
        copy.start()
        started.append(copy)
        return copy

    left, right, far = (x + 3) % 4, (x + 1) % 4, (x + 2) % 4
    other = 1 - z
    over_z = []
    for part in range(2):
        ref = piece(x, z, part)
        over_z.append(begin(remote(ref, ref, sent_y.at[6 + part], got_y.at[6 + part], other_z, y)))
    passes, cores = [], []
    for stage, zz in ((0, z), (1, other)):
        if stage:
            for copy in over_z:
                copy.wait_recv()
        s = 6 * stage
        passes.append(
            [begin(step_x(x, zz, part, 1, s + part)) for part in range(2)]
            + [begin(step_x(x, zz, part, -1, s + 2 + part)) for part in range(2)]
        )
        for part in range(2):
            cores.append(begin(to_core(x, zz, part, 8 * stage + part)))
    for stage, zz in ((0, z), (1, other)):
        s = 6 * stage
        c = 8 * stage
        moves = passes[stage]
        moves[0].wait_recv()
        relay_right = begin(step_x(left, zz, 0, 1, s + 4))
        cores.append(begin(to_core(left, zz, 0, c + 2)))
        moves[3].wait_recv()
        relay_left = begin(step_x(right, zz, 1, -1, s + 5))
        cores.append(begin(to_core(right, zz, 1, c + 3)))
        moves[1].wait_recv()
        cores.append(begin(to_core(left, zz, 1, c + 4)))
        moves[2].wait_recv()
        cores.append(begin(to_core(right, zz, 0, c + 5)))
        passes.append((relay_right, relay_left))
    for stage, zz in ((0, z), (1, other)):
        relay_right, relay_left = passes[2 + stage]
        c = 8 * stage
        relay_right.wait_recv()
        cores.append(begin(to_core(far, zz, 0, c + 6)))
        relay_left.wait_recv()
        cores.append(begin(to_core(far, zz, 1, c + 7)))
    for copy in cores:
        copy.wait_recv()
    for copy in members + to_sum + spread + started:
        copy.wait_send()
    for g in range(8):
        to = half * 8 + g

        @pl.when(to != m)
        def _():
            remote(
                entries_ref.at[pl.ds(8 * g, 8), :], own_entries.at[a],
                sent_e.at[g], got_e.at[a], base + to, y,
            ).wait_send()


VMEM_SPEC = pl.BlockSpec(memory_space=pltpu.VMEM)
SMEM_SPEC = pl.BlockSpec(memory_space=pltpu.SMEM)
PARAMS = pltpu.CompilerParams(vmem_limit_bytes=24 * 1024 * 1024)


def gathered(map_leaf, leaf_update, entries):
    dma = pltpu.SemaphoreType.DMA
    return pl.pallas_call(
        gather_kernel,
        out_shape=jax.ShapeDtypeStruct((36, BLK, BLK), F32),
        in_specs=[VMEM_SPEC, VMEM_SPEC, VMEM_SPEC],
        out_specs=VMEM_SPEC,
        scratch_shapes=[
            pltpu.VMEM((16, 5, 8, BLK), F32),
            pltpu.VMEM((36, 8, BLK), F32),
            pltpu.VMEM((3, 9, 8, BLK), F32),
            pltpu.VMEM((8, 8, 256), F32),
            pltpu.VMEM((16, BLK), jnp.int32),
            pltpu.SMEM((16, BLK), jnp.int32),
            dma,
            dma((1,)), dma((16,)), dma((16,)), dma((8,)), dma((8,)), dma((8,)), dma((8,)),
            dma((12,)), dma((12,)), dma((16,)), dma((16,)),
        ],
        compiler_params=pltpu.CompilerParams(
            vmem_limit_bytes=32 * 1024 * 1024, collective_id=0, has_side_effects=True
        ),
    )(map_leaf, leaf_update.reshape(4, 16, 8, BLK), entries)


def exchanged(tri, entries, distance, collective_id):
    dma = pltpu.SemaphoreType.DMA
    n = 8 * BLK
    return pl.pallas_call(
        functools.partial(exchange_kernel, distance),
        out_shape=(jax.ShapeDtypeStruct(tri.shape, F32), jax.ShapeDtypeStruct((n, n), F32)),
        in_specs=[VMEM_SPEC, pl.BlockSpec(memory_space=pltpu.HBM)],
        out_specs=(VMEM_SPEC, VMEM_SPEC),
        scratch_shapes=[dma((32,)), dma((32,)), dma],
        compiler_params=pltpu.CompilerParams(
            vmem_limit_bytes=(43 if collective_id == 1 else 16) * 1024 * 1024, collective_id=collective_id, has_side_effects=True
        ),
    )(tri, entries)


def first_eliminated(lower, blocks):
    n = 8 * BLK
    return pl.pallas_call(
        functools.partial(first_kernel, blocks),
        out_shape=(
            jax.ShapeDtypeStruct((n, n), F32),
            jax.ShapeDtypeStruct((10 * BLK, BLK), F32),
        ),
        in_specs=[VMEM_SPEC],
        out_specs=(VMEM_SPEC, VMEM_SPEC),
        scratch_shapes=scratch_for(n),
        compiler_params=PARAMS,
    )(lower)


def next_eliminated(maps, base, mine, other, blocks, members):
    n = 8 * BLK
    out = (jax.ShapeDtypeStruct((n, n), F32), jax.ShapeDtypeStruct((10 * BLK, BLK), F32))
    return pl.pallas_call(
        functools.partial(next_kernel, blocks, members),
        out_shape=out,
        in_specs=[SMEM_SPEC, VMEM_SPEC, VMEM_SPEC, VMEM_SPEC],
        out_specs=(VMEM_SPEC, VMEM_SPEC),
        scratch_shapes=scratch_for(n),
        input_output_aliases={1: 0},
        compiler_params=PARAMS,
    )(maps, base, mine, other)


def columns_of_inverse(swept, sigma, sigma_left, coupling_left, blocks, value, value_right, out):
    half = 4 * BLK
    for t, block in enumerate(blocks):
        here = slice(t * BLK, (t + 1) * BLK)

        @pl.when(block < 4)
        def _():
            put_right(value_right, here, swept[half:, at_block(block)])
            out[:half, here] = -swept[:half, at_block(block)]

        @pl.when(block >= 4)
        def _():
            value_right[:, here] = jnp.zeros((3 * half, BLK), BF16)
            out[:half, here] = jnp.zeros((half, BLK), F32)

    width = len(blocks) * BLK
    value[:, :width] = -dot(sigma_left[...], value_right[:, :width])
    for t, block in enumerate(blocks):
        here = slice(t * BLK, (t + 1) * BLK)

        @pl.when(block >= 4)
        def _():
            value[:, here] = sigma[:, at_block(block - 4)]

        lower = value[:, here]
        put_right(value_right, here, lower)
        out[half:, here] = lower
    out[:half, :width] = out[:half, :width] - dot(coupling_left[...], value_right[:, :width])


def back_kernel(
    mid_ref, leaf_ref, one_ref, two_ref, top_ref, o_ref,
    sigma, sigma_left, coupling_left, value, value_right, columns, lower,
):
    half = 4 * BLK
    whole = slice(None)
    leaf = lax.axis_index("leaf")
    first_node = leaf // 16
    sigma[...] = -top_ref[...]
    put_left(sigma_left, whole, sigma[...])
    put_left(coupling_left, whole, two_ref[:half, half:])
    blocks = [mid_ref[first_node, j] for j in range(4)]
    columns_of_inverse(
        two_ref, sigma, sigma_left, coupling_left, blocks, value, value_right, columns
    )
    for i in range(4):
        lower[i * BLK : (i + 1) * BLK, :] = columns[at_block(blocks[i]), :]
    put_left(sigma_left, whole, lower[...])
    put_left(coupling_left, whole, one_ref[:half, half:])
    columns_of_inverse(
        one_ref, lower, sigma_left, coupling_left, [leaf_ref[leaf, lax.axis_index("front")]],
        value, value_right, columns,
    )
    for i in range(4):
        o_ref[i * BLK : (i + 1) * BLK, :] = columns[at_block(leaf_ref[leaf, i]), :BLK]


def back_substituted(mid, leaf, one, two, top):
    half = 4 * BLK
    return pl.pallas_call(
        back_kernel,
        out_shape=jax.ShapeDtypeStruct((half, BLK), F32),
        in_specs=[SMEM_SPEC] * 2 + [VMEM_SPEC] * 3,
        out_specs=VMEM_SPEC,
        scratch_shapes=[
            pltpu.VMEM((half, half), F32),
            pltpu.VMEM((half, 3 * half), BF16),
            pltpu.VMEM((half, 3 * half), BF16),
            pltpu.VMEM((half, half), F32),
            pltpu.VMEM((3 * half, half), BF16),
            pltpu.VMEM((2 * half, half), F32),
            pltpu.VMEM((half, half), F32),
        ],
        compiler_params=PARAMS,
    )(mid, leaf, one, two, top)


def body(leaf_update, front_entries1, front_entries2, front_entries3, map_leaf, map_mid, map_top):
    members = lax.axis_size("leaf") // 4
    lower = gathered(map_leaf, leaf_update, front_entries1)
    one, update = first_eliminated(lower, SEP1 // BLK)
    other, base = exchanged(update, front_entries2, members, 1)
    two, update = next_eliminated(map_mid, base, update, other, SEP2 // BLK, members)
    other, base = exchanged(update, front_entries3, 2 * members, 2)
    top = top_inverse(map_top, base, update, other, 2 * members)
    return back_substituted(map_mid, map_leaf, one, two, top)


def solution(mesh):
    in_specs = (P("leaf", "front"), P("leaf", "front"), P(), P(), P(), P(), P())
    out_specs = P("leaf", "front")
    return jax.shard_map(body, mesh=mesh, in_specs=in_specs, out_specs=out_specs, check_vma=False)
```

```python
import functools

import jax
import jax.numpy as jnp
from jax import lax
from jax.experimental import pallas as pl
from jax.experimental.pallas import tpu as pltpu
from jax.sharding import PartitionSpec as P

BLK = 128
SEP1 = 512
SEP2 = 512
SEP3 = 1024
RUP = 512


F32, BF16 = jnp.float32, jnp.bfloat16
ROUNDS = 4


def row_of(x, k):
    return jnp.broadcast_to(x[k : k + 1, :], (8, 128))


def along(x, c):
    return jnp.take_along_axis(x, jnp.full((8, 128), c, jnp.int32), axis=1)


def thirds(x):
    high = x.astype(BF16)
    rest = x - high.astype(F32)
    middle = rest.astype(BF16)
    return high, middle, (rest - middle.astype(F32)).astype(BF16)


def outer_left(p):
    high, middle, low = thirds(p)
    return jnp.concatenate([high, high, high, middle, middle, low], axis=0).T


def outer_right(s):
    high, middle, low = thirds(s)
    return jnp.concatenate([high, middle, low, high, middle, high], axis=0)


def swept_rows(rows, base, lane, sub):
    e = [along(rows, base + j) for j in range(8)]
    inside = (lane >= base) & (lane < base + 8)
    m = jnp.where(lane == base + sub, -1.0, jnp.where(inside, 0.0, rows))
    for k in range(0, 8, 2):
        a, b, d = row_of(e[k], k), row_of(e[k + 1], k), row_of(e[k + 1], k + 1)
        is_first, is_second = sub == k, sub == k + 1
        pair = is_first | is_second
        left = jnp.where(is_first, -1.0, jnp.where(is_second, 0.0, e[k]))
        right = jnp.where(is_second, -1.0, jnp.where(is_first, 0.0, e[k + 1]))
        scale = 1.0 / (a * d - b * b)
        by_first = (d * left - b * right) * scale
        by_second = (a * right - b * left) * scale

        def go(t):
            return jnp.where(pair, 0.0, t) - by_first * row_of(t, k) - by_second * row_of(t, k + 1)

        m = go(m)
        e = [go(x) if j > k + 1 else x for j, x in enumerate(e)]
    return m


def sum_of(terms):
    while len(terms) > 1:
        terms = [terms[i] + terms[i + 1] for i in range(0, len(terms), 2)]
    return terms[0]


def less_pivots(x, base, rows, inside):
    total = None
    for k in range(0, 8, 2):
        term = along(x, base + k) * rows[k] + along(x, base + k + 1) * rows[k + 1]
        total = term if total is None else total + term
    return jnp.where(inside, 0.0, x) - total


def scaled_diagonal(w):
    lane = lax.broadcasted_iota(jnp.int32, (8, 128), 1)
    sub = lax.broadcasted_iota(jnp.int32, (8, 128), 0)
    tiles = [w[8 * i : 8 * i + 8, :] for i in range(16)]
    diagonal = [jnp.where(lane == 8 * i + sub, x, 0.0) for i, x in enumerate(tiles)]
    total = functools.reduce(jnp.add, diagonal)
    across = lax.rsqrt(jnp.broadcast_to(jnp.sum(total, axis=0, keepdims=True), (8, 128)))
    down = [
        lax.rsqrt(jnp.broadcast_to(jnp.sum(x, axis=1, keepdims=True), (8, 128))) for x in diagonal
    ]
    for i in range(16):
        w[8 * i : 8 * i + 8, :] = tiles[i] * down[i] * across
    return down, across


def invert(w, rounds, beside):
    lane = lax.broadcasted_iota(jnp.int32, (8, 128), 1)
    sub = lax.broadcasted_iota(jnp.int32, (8, 128), 0)
    lanes = lax.broadcasted_iota(jnp.int32, (128, 128), 1)
    down, across = scaled_diagonal(w)

    def at(t):
        return pl.ds(pl.multiple_of(8 * t, 8), 8)

    def panel(p, carry):
        rows, before, left_before = carry
        base = 8 * p
        base_before = (base + 120) % 128
        inside_before = (lane >= base - 8) & (lane < base)
        gone = (lanes >= base - 8) & (lanes < base)
        q = (p + 1) % 16
        following = w[at(q), :]
        now = swept_rows(rows, base, lane, sub)
        own = lane == 8 * q + sub
        entries = [
            jnp.broadcast_to(
                jnp.sum(jnp.where(own, row_of(rows, k), 0.0), axis=1, keepdims=True), (8, 128)
            )
            for k in range(8)
        ]
        following = less_pivots(
            following, base_before, [row_of(before, k) for k in range(8)], inside_before
        )
        inside = (lane >= base) & (lane < base + 8)
        following = jnp.where(inside, 0.0, following) - sum_of(
            [entries[k] * row_of(now, k) for k in range(8)]
        )
        w[:BLK, :] = jnp.where(gone, 0.0, w[:BLK, :]) - dot(left_before, outer_right(before))
        w[at((p + 16) % 17), :] = before
        return following, now, outer_left(rows)

    def turn(r, carry):
        for p in range(16 // rounds):
            carry = panel(r * (16 // rounds) + p, carry)
            if p == 1:
                beside(r)
        return carry

    start = (w[0:8, :], jnp.zeros((8, 128), F32), jnp.zeros((BLK, 48), BF16))
    _, last, left = lax.fori_loop(0, rounds, turn, start)
    w[:BLK, :] = jnp.where(lanes >= 120, 0.0, w[:BLK, :]) - dot(left, outer_right(last))
    w[120:128, :] = last
    for i in range(16):
        w[8 * i : 8 * i + 8, :] = -w[8 * i : 8 * i + 8, :] * down[i] * across


def halves(x):
    high = x.astype(BF16)
    return high, (x - high.astype(F32)).astype(BF16)


def put_left(ref, rows, x):
    high, low = halves(x)
    width = x.shape[1]
    ref[rows, :width] = high
    ref[rows, width : 2 * width] = high
    ref[rows, 2 * width : 3 * width] = low
    if ref.shape[1] > 3 * width:
        ref[rows, 3 * width :] = low


def put_right(ref, columns, x):
    high, low = halves(x)
    depth = x.shape[0]
    ref[:depth, columns] = high
    ref[depth : 2 * depth, columns] = low
    ref[2 * depth : 3 * depth, columns] = high
    if ref.shape[0] > 3 * depth:
        ref[3 * depth :, columns] = low


def dot(a, b):
    return jnp.dot(a, b, preferred_element_type=F32)


def eliminate(o, blocks, left, right, small_right, inverted, begun=False, ahead=False):
    n = o.shape[0]
    whole = slice(None)
    eye = (
        lax.broadcasted_iota(jnp.int32, (BLK, BLK), 0)
        == lax.broadcasted_iota(jnp.int32, (BLK, BLK), 1)
    )

    def nothing(r):
        pass

    def prepare(j):
        at = pl.ds(pl.multiple_of(j * BLK, BLK), BLK)
        put_right(right, whole, o[at, :])
        put_right(right, at, jnp.where(eye, -1.0, 0.0))
        put_left(left, whole, o[:, at])
        put_right(small_right, whole, inverted[:BLK, :])
        for t in range(0, n, 256):
            put_left(left, slice(t, t + 256), dot(left[t : t + 256, :], small_right[...]))
        put_left(left, at, -inverted[:BLK, :])
        o[at, :] = jnp.zeros((BLK, n), F32)
        o[:, at] = jnp.zeros((n, BLK), F32)

    def update(size, t):
        these = pl.ds(pl.multiple_of(t * size, size), size)
        o[these, :] = o[these, :] - dot(left[these, :], right[...])

    if not begun:
        inverted[:BLK, :] = o[:BLK, :BLK]
        invert(inverted, 16, nothing)

    def step(j, carry):
        prepare(j)
        after = pl.ds(pl.multiple_of((j + 1) * BLK, BLK), BLK)
        inverted[:BLK, :] = o[after, after] - dot(left[after, :], right[:, after])
        invert(inverted, ROUNDS, functools.partial(update, n // ROUNDS))
        return carry

    lax.fori_loop(0, blocks if ahead else blocks - 1, step, 0)
    if ahead:
        return
    prepare(blocks - 1)

    def tile(t, carry):
        update(512, t)
        return carry

    lax.fori_loop(0, n // 512, tile, 0)


def scratch_for(n):
    return [
        pltpu.VMEM((n, 4 * BLK), BF16),
        pltpu.VMEM((4 * BLK, n), BF16),
        pltpu.VMEM((4 * BLK, BLK), BF16),
        pltpu.VMEM((BLK + 8, BLK), F32),
    ]


def at_block(b):
    return pl.ds(pl.multiple_of(b * BLK, BLK), BLK)


LOWER = [(a, b) for y in range(4) for a in (y, 7 - y) for b in range(a + 1)]
SHARE = [(i, j) for i in range(4) for j in range(i + 1)]


def pack_update(o, tri):
    for t, (i, j) in enumerate(SHARE):
        tri[t * BLK : (t + 1) * BLK, :] = o[
            SEP1 + i * BLK : SEP1 + (i + 1) * BLK, SEP1 + j * BLK : SEP1 + (j + 1) * BLK
        ]


def first_kernel(blocks, lower_ref, o_ref, tri_ref, *scratch):
    for t, (a, b) in enumerate(LOWER):
        part = lower_ref[t]
        o_ref[a * BLK : (a + 1) * BLK, b * BLK : (b + 1) * BLK] = part
        if a != b:
            o_ref[b * BLK : (b + 1) * BLK, a * BLK : (a + 1) * BLK] = part.T
    eliminate(o_ref, blocks, *scratch)
    pack_update(o_ref, tri_ref)


def add_child(o_ref, update, maps, child):
    for t, (i, j) in enumerate(SHARE):
        rows, columns = at_block(maps[child, i]), at_block(maps[child, j])
        part = update[t * BLK : (t + 1) * BLK, :]
        o_ref[rows, columns] = o_ref[rows, columns] + part
        if i != j:
            o_ref[columns, rows] = o_ref[columns, rows] + part.T


def next_kernel(blocks, members, map_ref, base_ref, mine_ref, other_ref, o_ref, *rest):
    tri_ref, scratch = rest[0], rest[1:]
    child = lax.axis_index("leaf") // members
    add_child(o_ref, mine_ref, map_ref, child)
    add_child(o_ref, other_ref, map_ref, child + 1 - 2 * (child % 2))
    eliminate(o_ref, blocks, *scratch)
    pack_update(o_ref, tri_ref)


def top_kernel(
    members, map_ref, base_ref, mine_ref, other_ref, sigma_ref,
    order, position, o, low, left, right, small_right, inverted, low_left, low_right,
):
    child = lax.axis_index("leaf") // members
    other = child + 1 - 2 * (child % 2)
    count = jnp.int32(0)
    for b in range(8):
        named = jnp.int32(-1)
        for i in range(4):
            named = jnp.where(map_ref[child, i] == b, 4 + i, named)
        spot = jnp.where(named < 0, count, named)
        count = count + jnp.where(named < 0, 1, 0)
        order[spot] = b
        position[b] = spot
    for p in range(8):
        for q in range(8):
            o[p * BLK : (p + 1) * BLK, q * BLK : (q + 1) * BLK] = base_ref[
                at_block(order[p]), at_block(order[q])
            ]
    half = 4 * BLK
    for t, (i, j) in enumerate(SHARE):
        part = mine_ref[t * BLK : (t + 1) * BLK, :]
        rows = slice(half + i * BLK, half + (i + 1) * BLK)
        columns = slice(half + j * BLK, half + (j + 1) * BLK)
        o[rows, columns] = o[rows, columns] + part
        if i != j:
            o[columns, rows] = o[columns, rows] + part.T
    for t, (i, j) in enumerate(SHARE):
        part = other_ref[t * BLK : (t + 1) * BLK, :]
        rows, columns = at_block(position[map_ref[other, i]]), at_block(position[map_ref[other, j]])
        o[rows, columns] = o[rows, columns] + part
        if i != j:
            o[columns, rows] = o[columns, rows] + part.T
    eliminate(o, 4, left, right, small_right, inverted, ahead=True)
    low[...] = o[half:, half:]
    eliminate(low, 4, low_left, low_right, small_right, inverted, begun=True)
    sigma_ref[...] = low[...]


def top_inverse(maps, base, mine, other, members):
    n, half = 8 * BLK, 4 * BLK
    return pl.pallas_call(
        functools.partial(top_kernel, members),
        out_shape=jax.ShapeDtypeStruct((half, half), F32),
        in_specs=[SMEM_SPEC, VMEM_SPEC, VMEM_SPEC, VMEM_SPEC],
        out_specs=VMEM_SPEC,
        scratch_shapes=[
            pltpu.SMEM((8,), jnp.int32),
            pltpu.SMEM((8,), jnp.int32),
            pltpu.VMEM((n, n), F32),
            pltpu.VMEM((half, half), F32),
        ]
        + scratch_for(n)
        + scratch_for(half)[:2],
        compiler_params=PARAMS,
    )(maps, base, mine, other)


def remote(source, target, sent, received, leaf, front):
    return pltpu.make_async_remote_copy(
        src_ref=source,
        dst_ref=target,
        send_sem=sent,
        recv_sem=received,
        device_id=(leaf, front),
        device_id_type=pl.DeviceIdType.MESH,
    )


def greet(devices):
    barrier = pltpu.get_barrier_semaphore()
    for device in devices:
        pl.semaphore_signal(
            barrier, inc=1, device_id=device, device_id_type=pl.DeviceIdType.MESH
        )
    pl.semaphore_wait(barrier, len(devices))


def exchange_kernel(distance, tri_ref, entries_ref, o_ref, base_ref, sent, got, copied):
    leaf, y = lax.axis_index("leaf"), lax.axis_index("front")
    n = base_ref.shape[0]
    start = pl.multiple_of((leaf // (2 * distance)) % (entries_ref.shape[0] // n) * n, 8)
    fetch = pltpu.make_async_copy(entries_ref.at[pl.ds(start, n), :], base_ref, copied)
    fetch.start()
    core, x = leaf % 2, (leaf // 2) % 4
    z = leaf // 8
    sibling = leaf + distance * (1 - 2 * ((leaf // distance) % 2))
    other_core = leaf + 1 - 2 * core
    rows = tri_ref.shape[0] // 32
    apart = [(dx, dy) for dx in (0, 1, 3, 2) for dy in (0, 1, 3, 2)]

    def place(dx, dy):
        return z * 8 + ((x + dx) % 4) * 2 + core, (y + dy) % 4

    greet([(sibling, y), (other_core, y)] + [place(dx, dy) for dx, dy in apart[1:]])

    def share(c, xx, yy):
        return pl.ds(pl.multiple_of(((c * 4 + xx) * 4 + yy) * rows, 8), rows)

    mine = share(core, x, y)
    across = remote(tri_ref.at[mine], o_ref.at[mine], sent.at[0], got.at[0], sibling, y)
    across.start()
    across.wait_recv()
    spread = []
    for t, (dx, dy) in enumerate(apart):
        if t:
            spread.append(
                remote(o_ref.at[mine], o_ref.at[mine], sent.at[t], got.at[t], *place(dx, dy))
            )
            spread[-1].start()
    last = []
    for t, (dx, dy) in enumerate(apart):
        if t:
            spread[t - 1].wait_recv()
        piece = share(core, (x - dx + 4) % 4, (y - dy + 4) % 4)
        last.append(
            remote(o_ref.at[piece], o_ref.at[piece], sent.at[16 + t], got.at[16 + t], other_core, y)
        )
        last[-1].start()
    for copy in last:
        copy.wait_recv()
    for copy in [across] + spread + last:
        copy.wait_send()
    fetch.wait()


def gather_kernel(
    map_ref, leaf_ref, entries_ref, o_ref,
    met, partial, halves_in, own_entries, found_tile, table, told,
    keep, sent, got, sent_e, got_e, sent_y, got_y, sent_x, got_x, sent_c, got_c,
):
    leaf, y = lax.axis_index("leaf"), lax.axis_index("front")
    m = leaf % 16
    base = leaf - m
    core, x, z = m % 2, (m // 2) % 4, m // 8
    met[:, 4] = jnp.zeros((16, 8, BLK), F32)
    greet(
        [(base + (m + d) % 16, y) for d in range(1, 16)] + [(leaf, (y + d) % 4) for d in (1, 2, 3)]
    )

    kept = pltpu.make_async_copy(leaf_ref.at[:, m], met.at[m, 0:4], keep.at[0])
    kept.start()
    members = []
    for d in range(1, 16):
        to = (m + d) % 16
        members.append(
            remote(leaf_ref.at[:, to], met.at[m, 0:4], sent.at[d], got.at[d], base + to, y)
        )
        members[-1].start()
    a, half = m // 2, m % 2
    for g in range(8):
        to = half * 8 + g
        source = entries_ref.at[pl.ds(8 * g, 8), :]

        @pl.when(to == m)
        def _():
            pltpu.make_async_copy(source, own_entries.at[a], got_e.at[a]).start()

        @pl.when(to != m)
        def _():
            remote(source, own_entries.at[a], sent_e.at[g], got_e.at[a], base + to, y).start()

    lane = lax.broadcasted_iota(jnp.int32, (16, BLK), 1)
    group = (
        (lane >= 9).astype(jnp.int32) + (lane >= 18).astype(jnp.int32) + (lane >= 27).astype(jnp.int32)
    )
    within = lane - 9 * group
    second = within > group
    block_row = jnp.where(second, 7 - group, group)
    block_column = jnp.where(second, within - group - 1, within)
    maps = map_ref[pl.ds(pl.multiple_of(base, 16), 16), :]
    found = jnp.full((16, BLK), 4, jnp.int32)
    landing = jnp.zeros((16, BLK), jnp.int32)
    for i in range(4):
        target = jnp.broadcast_to(maps[:, i : i + 1], (16, BLK))
        found = jnp.where(block_row == target, i, found)
        landing = landing + target * jnp.where(y == i, 1, 0)
    found_tile[...] = jnp.where(block_column == landing, found, 4)
    tell = pltpu.make_async_copy(found_tile, table, told)
    tell.start()
    tell.wait()
    kept.wait()
    for copy in members:
        copy.wait_recv()

    def sum_block(t, carry):
        terms = [met[s, table[s, t]] for s in range(16)]
        while len(terms) > 1:
            terms = [terms[i] + terms[i + 1] for i in range(0, len(terms), 2)]
        partial[t] = terms[0]
        return carry

    lax.fori_loop(0, 36, sum_block, 0)
    for k in range(8):
        pltpu.make_async_copy(
            entries_ref.at[pl.ds(0, 8), :], own_entries.at[k], got_e.at[k]
        ).wait()
    for k in range(8):
        first = 9 * k if k < 4 else 9 * (7 - k) + 8 - k
        for h in range(2):
            b = 2 * y + h

            @pl.when(b <= k)
            def _():
                partial[first + b] = (
                    partial[first + b] + own_entries[k, :, h * BLK : (h + 1) * BLK]
                )

    to_sum = []
    for d in (1, 2, 3):
        to = (y + d) % 4
        to_sum.append(
            remote(
                partial.at[pl.ds(9 * to, 9)], halves_in.at[d - 1],
                sent_y.at[d - 1], got_y.at[d - 1], leaf, to,
            )
        )
        to_sum[-1].start()
    for copy in to_sum:
        copy.wait_recv()
    rows = pl.ds(pl.multiple_of(m * 8, 8), 8)
    for t in range(9):
        o_ref[9 * y + t, rows, :] = (
            partial[9 * y + t] + halves_in[0, t] + halves_in[1, t] + halves_in[2, t]
        )
    spread = []
    own = o_ref.at[pl.ds(9 * y, 9), rows, :]
    for d in (1, 2, 3):
        spread.append(
            remote(own, own, sent_y.at[2 + d], got_y.at[2 + d], leaf, (y + d) % 4)
        )
        spread[-1].start()
    for copy in spread:
        copy.wait_recv()

    other_z = base + (m + 8) % 16
    other_core = base + m + 1 - 2 * core

    def piece(xx, zz, part):
        slot = pl.ds(pl.multiple_of((zz * 8 + xx * 2 + core) * 8, 8), 8)
        return o_ref.at[18 * part : 18 * part + 18, slot, :]

    def step_x(xx, zz, part, direction, slot):
        to = base + z * 8 + ((x + direction + 4) % 4) * 2 + core
        ref = piece(xx, zz, part)
        return remote(ref, ref, sent_x.at[slot], got_x.at[slot], to, y)

    def to_core(xx, zz, part, slot):
        ref = piece(xx, zz, part)
        return remote(ref, ref, sent_c.at[slot], got_c.at[slot], other_core, y)

    started = []

    def begin(copy):
        copy.start()
        started.append(copy)
        return copy

    left, right, far = (x + 3) % 4, (x + 1) % 4, (x + 2) % 4
    other = 1 - z
    over_z = []
    for part in range(2):
        ref = piece(x, z, part)
        over_z.append(begin(remote(ref, ref, sent_y.at[6 + part], got_y.at[6 + part], other_z, y)))
    passes, cores = [], []
    for stage, zz in ((0, z), (1, other)):
        if stage:
            for copy in over_z:
                copy.wait_recv()
        s = 6 * stage
        passes.append(
            [begin(step_x(x, zz, part, 1, s + part)) for part in range(2)]
            + [begin(step_x(x, zz, part, -1, s + 2 + part)) for part in range(2)]
        )
        for part in range(2):
            cores.append(begin(to_core(x, zz, part, 8 * stage + part)))
    for stage, zz in ((0, z), (1, other)):
        s = 6 * stage
        c = 8 * stage
        moves = passes[stage]
        moves[0].wait_recv()
        relay_right = begin(step_x(left, zz, 0, 1, s + 4))
        cores.append(begin(to_core(left, zz, 0, c + 2)))
        moves[3].wait_recv()
        relay_left = begin(step_x(right, zz, 1, -1, s + 5))
        cores.append(begin(to_core(right, zz, 1, c + 3)))
        moves[1].wait_recv()
        cores.append(begin(to_core(left, zz, 1, c + 4)))
        moves[2].wait_recv()
        cores.append(begin(to_core(right, zz, 0, c + 5)))
        passes.append((relay_right, relay_left))
    for stage, zz in ((0, z), (1, other)):
        relay_right, relay_left = passes[2 + stage]
        c = 8 * stage
        relay_right.wait_recv()
        cores.append(begin(to_core(far, zz, 0, c + 6)))
        relay_left.wait_recv()
        cores.append(begin(to_core(far, zz, 1, c + 7)))
    for copy in cores:
        copy.wait_recv()
    for copy in members + to_sum + spread + started:
        copy.wait_send()
    for g in range(8):
        to = half * 8 + g

        @pl.when(to != m)
        def _():
            remote(
                entries_ref.at[pl.ds(8 * g, 8), :], own_entries.at[a],
                sent_e.at[g], got_e.at[a], base + to, y,
            ).wait_send()


VMEM_SPEC = pl.BlockSpec(memory_space=pltpu.VMEM)
SMEM_SPEC = pl.BlockSpec(memory_space=pltpu.SMEM)
PARAMS = pltpu.CompilerParams(vmem_limit_bytes=24 * 1024 * 1024)


def gathered(map_leaf, leaf_update, entries):
    dma = pltpu.SemaphoreType.DMA
    return pl.pallas_call(
        gather_kernel,
        out_shape=jax.ShapeDtypeStruct((36, BLK, BLK), F32),
        in_specs=[VMEM_SPEC, VMEM_SPEC, VMEM_SPEC],
        out_specs=VMEM_SPEC,
        scratch_shapes=[
            pltpu.VMEM((16, 5, 8, BLK), F32),
            pltpu.VMEM((36, 8, BLK), F32),
            pltpu.VMEM((3, 9, 8, BLK), F32),
            pltpu.VMEM((8, 8, 256), F32),
            pltpu.VMEM((16, BLK), jnp.int32),
            pltpu.SMEM((16, BLK), jnp.int32),
            dma,
            dma((1,)), dma((16,)), dma((16,)), dma((8,)), dma((8,)), dma((8,)), dma((8,)),
            dma((12,)), dma((12,)), dma((16,)), dma((16,)),
        ],
        compiler_params=pltpu.CompilerParams(
            vmem_limit_bytes=32 * 1024 * 1024, collective_id=0, has_side_effects=True
        ),
    )(map_leaf, leaf_update.reshape(4, 16, 8, BLK), entries)


def exchanged(tri, entries, distance, collective_id):
    dma = pltpu.SemaphoreType.DMA
    n = 8 * BLK
    return pl.pallas_call(
        functools.partial(exchange_kernel, distance),
        out_shape=(jax.ShapeDtypeStruct(tri.shape, F32), jax.ShapeDtypeStruct((n, n), F32)),
        in_specs=[VMEM_SPEC, pl.BlockSpec(memory_space=pltpu.HBM)],
        out_specs=(VMEM_SPEC, VMEM_SPEC),
        scratch_shapes=[dma((32,)), dma((32,)), dma],
        compiler_params=pltpu.CompilerParams(
            vmem_limit_bytes=(43 if collective_id == 1 else 16) * 1024 * 1024, collective_id=collective_id, has_side_effects=True
        ),
    )(tri, entries)


def first_eliminated(lower, blocks):
    n = 8 * BLK
    return pl.pallas_call(
        functools.partial(first_kernel, blocks),
        out_shape=(
            jax.ShapeDtypeStruct((n, n), F32),
            jax.ShapeDtypeStruct((10 * BLK, BLK), F32),
        ),
        in_specs=[VMEM_SPEC],
        out_specs=(VMEM_SPEC, VMEM_SPEC),
        scratch_shapes=scratch_for(n),
        compiler_params=PARAMS,
    )(lower)


def next_eliminated(maps, base, mine, other, blocks, members):
    n = 8 * BLK
    out = (jax.ShapeDtypeStruct((n, n), F32), jax.ShapeDtypeStruct((10 * BLK, BLK), F32))
    return pl.pallas_call(
        functools.partial(next_kernel, blocks, members),
        out_shape=out,
        in_specs=[SMEM_SPEC, VMEM_SPEC, VMEM_SPEC, VMEM_SPEC],
        out_specs=(VMEM_SPEC, VMEM_SPEC),
        scratch_shapes=scratch_for(n),
        input_output_aliases={1: 0},
        compiler_params=PARAMS,
    )(maps, base, mine, other)


def columns_of_inverse(swept, sigma, sigma_left, coupling_left, blocks, value, value_right, out):
    half = 4 * BLK
    for t, block in enumerate(blocks):
        here = slice(t * BLK, (t + 1) * BLK)

        @pl.when(block < 4)
        def _():
            put_right(value_right, here, swept[half:, at_block(block)])
            out[:half, here] = -swept[:half, at_block(block)]

        @pl.when(block >= 4)
        def _():
            value_right[:, here] = jnp.zeros((3 * half, BLK), BF16)
            out[:half, here] = jnp.zeros((half, BLK), F32)

    width = len(blocks) * BLK
    value[:, :width] = -dot(sigma_left[...], value_right[:, :width])
    for t, block in enumerate(blocks):
        here = slice(t * BLK, (t + 1) * BLK)

        @pl.when(block >= 4)
        def _():
            value[:, here] = sigma[:, at_block(block - 4)]

        lower = value[:, here]
        put_right(value_right, here, lower)
        out[half:, here] = lower
    out[:half, :width] = out[:half, :width] - dot(coupling_left[...], value_right[:, :width])


def back_kernel(
    mid_ref, leaf_ref, one_ref, two_ref, top_ref, o_ref,
    sigma, sigma_left, coupling_left, value, value_right, columns, lower,
):
    half = 4 * BLK
    whole = slice(None)
    leaf = lax.axis_index("leaf")
    first_node = leaf // 16
    sigma[...] = -top_ref[...]
    put_left(sigma_left, whole, sigma[...])
    put_left(coupling_left, whole, two_ref[:half, half:])
    blocks = [mid_ref[first_node, j] for j in range(4)]
    columns_of_inverse(
        two_ref, sigma, sigma_left, coupling_left, blocks, value, value_right, columns
    )
    for i in range(4):
        lower[i * BLK : (i + 1) * BLK, :] = columns[at_block(blocks[i]), :]
    put_left(sigma_left, whole, lower[...])
    put_left(coupling_left, whole, one_ref[:half, half:])
    columns_of_inverse(
        one_ref, lower, sigma_left, coupling_left, [leaf_ref[leaf, lax.axis_index("front")]],
        value, value_right, columns,
    )
    for i in range(4):
        o_ref[i * BLK : (i + 1) * BLK, :] = columns[at_block(leaf_ref[leaf, i]), :BLK]


def back_substituted(mid, leaf, one, two, top):
    half = 4 * BLK
    return pl.pallas_call(
        back_kernel,
        out_shape=jax.ShapeDtypeStruct((half, BLK), F32),
        in_specs=[SMEM_SPEC] * 2 + [VMEM_SPEC] * 3,
        out_specs=VMEM_SPEC,
        scratch_shapes=[
            pltpu.VMEM((half, half), F32),
            pltpu.VMEM((half, 3 * half), BF16),
            pltpu.VMEM((half, 3 * half), BF16),
            pltpu.VMEM((half, half), F32),
            pltpu.VMEM((3 * half, half), BF16),
            pltpu.VMEM((2 * half, half), F32),
            pltpu.VMEM((half, half), F32),
        ],
        compiler_params=PARAMS,
    )(mid, leaf, one, two, top)


def body(leaf_update, front_entries1, front_entries2, front_entries3, map_leaf, map_mid, map_top):
    members = lax.axis_size("leaf") // 4
    lower = gathered(map_leaf, leaf_update, front_entries1)
    one, update = first_eliminated(lower, SEP1 // BLK)
    other, base = exchanged(update, front_entries2, members, 1)
    two, update = next_eliminated(map_mid, base, update, other, SEP2 // BLK, members)
    other, base = exchanged(update, front_entries3, 2 * members, 2)
    top = top_inverse(map_top, base, update, other, 2 * members)
    return back_substituted(map_mid, map_leaf, one, two, top)


def solution(mesh):
    in_specs = (P("leaf", "front"), P("leaf", "front"), P(), P(), P(), P(), P())
    out_specs = P("leaf", "front")
    return jax.shard_map(body, mesh=mesh, in_specs=in_specs, out_specs=out_specs, check_vma=False)
```

```python
import functools

import jax
import jax.numpy as jnp
from jax import lax
from jax.experimental import pallas as pl
from jax.experimental.pallas import tpu as pltpu
from jax.sharding import PartitionSpec as P

BLK = 128
SEP1 = 512
SEP2 = 512
SEP3 = 1024
RUP = 512


F32, BF16 = jnp.float32, jnp.bfloat16
ROUNDS = 4


def row_of(x, k):
    return jnp.broadcast_to(x[k : k + 1, :], (8, 128))


def along(x, c):
    return jnp.take_along_axis(x, jnp.full((8, 128), c, jnp.int32), axis=1)


def thirds(x):
    high = x.astype(BF16)
    rest = x - high.astype(F32)
    middle = rest.astype(BF16)
    return high, middle, (rest - middle.astype(F32)).astype(BF16)


def outer_left(p):
    high, middle, low = thirds(p)
    return jnp.concatenate([high, high, high, middle, middle, low], axis=0).T


def outer_right(s):
    high, middle, low = thirds(s)
    return jnp.concatenate([high, middle, low, high, middle, high], axis=0)


def swept_rows(rows, base, lane, sub):
    e = [along(rows, base + j) for j in range(8)]
    inside = (lane >= base) & (lane < base + 8)
    m = jnp.where(lane == base + sub, -1.0, jnp.where(inside, 0.0, rows))
    for k in range(0, 8, 2):
        a, b, d = row_of(e[k], k), row_of(e[k + 1], k), row_of(e[k + 1], k + 1)
        is_first, is_second = sub == k, sub == k + 1
        pair = is_first | is_second
        left = jnp.where(is_first, -1.0, jnp.where(is_second, 0.0, e[k]))
        right = jnp.where(is_second, -1.0, jnp.where(is_first, 0.0, e[k + 1]))
        scale = 1.0 / (a * d - b * b)
        by_first = (d * left - b * right) * scale
        by_second = (a * right - b * left) * scale

        def go(t):
            return jnp.where(pair, 0.0, t) - by_first * row_of(t, k) - by_second * row_of(t, k + 1)

        m = go(m)
        e = [go(x) if j > k + 1 else x for j, x in enumerate(e)]
    return m


def sum_of(terms):
    while len(terms) > 1:
        terms = [terms[i] + terms[i + 1] for i in range(0, len(terms), 2)]
    return terms[0]


def less_pivots(x, base, rows, inside):
    total = None
    for k in range(0, 8, 2):
        term = along(x, base + k) * rows[k] + along(x, base + k + 1) * rows[k + 1]
        total = term if total is None else total + term
    return jnp.where(inside, 0.0, x) - total


def scaled_diagonal(w):
    lane = lax.broadcasted_iota(jnp.int32, (8, 128), 1)
    sub = lax.broadcasted_iota(jnp.int32, (8, 128), 0)
    tiles = [w[8 * i : 8 * i + 8, :] for i in range(16)]
    diagonal = [jnp.where(lane == 8 * i + sub, x, 0.0) for i, x in enumerate(tiles)]
    total = functools.reduce(jnp.add, diagonal)
    across = lax.rsqrt(jnp.broadcast_to(jnp.sum(total, axis=0, keepdims=True), (8, 128)))
    down = [
        lax.rsqrt(jnp.broadcast_to(jnp.sum(x, axis=1, keepdims=True), (8, 128))) for x in diagonal
    ]
    for i in range(16):
        w[8 * i : 8 * i + 8, :] = tiles[i] * down[i] * across
    return down, across


def invert(w, rounds, beside):
    lane = lax.broadcasted_iota(jnp.int32, (8, 128), 1)
    sub = lax.broadcasted_iota(jnp.int32, (8, 128), 0)
    lanes = lax.broadcasted_iota(jnp.int32, (128, 128), 1)
    down, across = scaled_diagonal(w)

    def at(t):
        return pl.ds(pl.multiple_of(8 * t, 8), 8)

    def panel(p, carry):
        rows, before, left_before = carry
        base = 8 * p
        base_before = (base + 120) % 128
        inside_before = (lane >= base - 8) & (lane < base)
        gone = (lanes >= base - 8) & (lanes < base)
        q = (p + 1) % 16
        following = w[at(q), :]
        now = swept_rows(rows, base, lane, sub)
        own = lane == 8 * q + sub
        entries = [
            jnp.broadcast_to(
                jnp.sum(jnp.where(own, row_of(rows, k), 0.0), axis=1, keepdims=True), (8, 128)
            )
            for k in range(8)
        ]
        following = less_pivots(
            following, base_before, [row_of(before, k) for k in range(8)], inside_before
        )
        inside = (lane >= base) & (lane < base + 8)
        following = jnp.where(inside, 0.0, following) - sum_of(
            [entries[k] * row_of(now, k) for k in range(8)]
        )
        w[:BLK, :] = jnp.where(gone, 0.0, w[:BLK, :]) - dot(left_before, outer_right(before))
        w[at((p + 16) % 17), :] = before
        return following, now, outer_left(rows)

    def turn(r, carry):
        for p in range(16 // rounds):
            carry = panel(r * (16 // rounds) + p, carry)
            if p == 1:
                beside(r)
        return carry

    start = (w[0:8, :], jnp.zeros((8, 128), F32), jnp.zeros((BLK, 48), BF16))
    _, last, left = lax.fori_loop(0, rounds, turn, start)
    w[:BLK, :] = jnp.where(lanes >= 120, 0.0, w[:BLK, :]) - dot(left, outer_right(last))
    w[120:128, :] = last
    for i in range(16):
        w[8 * i : 8 * i + 8, :] = -w[8 * i : 8 * i + 8, :] * down[i] * across


def halves(x):
    high = x.astype(BF16)
    return high, (x - high.astype(F32)).astype(BF16)


def put_left(ref, rows, x):
    high, low = halves(x)
    width = x.shape[1]
    ref[rows, :width] = high
    ref[rows, width : 2 * width] = high
    ref[rows, 2 * width : 3 * width] = low
    if ref.shape[1] > 3 * width:
        ref[rows, 3 * width :] = low


def put_right(ref, columns, x):
    high, low = halves(x)
    depth = x.shape[0]
    ref[:depth, columns] = high
    ref[depth : 2 * depth, columns] = low
    ref[2 * depth : 3 * depth, columns] = high
    if ref.shape[0] > 3 * depth:
        ref[3 * depth :, columns] = low


def dot(a, b):
    return jnp.dot(a, b, preferred_element_type=F32)


def eliminate(o, blocks, left, right, small_right, inverted, begun=False, ahead=False):
    n = o.shape[0]
    whole = slice(None)
    eye = (
        lax.broadcasted_iota(jnp.int32, (BLK, BLK), 0)
        == lax.broadcasted_iota(jnp.int32, (BLK, BLK), 1)
    )

    def nothing(r):
        pass

    def prepare(j):
        at = pl.ds(pl.multiple_of(j * BLK, BLK), BLK)
        put_right(right, whole, o[at, :])
        put_right(right, at, jnp.where(eye, -1.0, 0.0))
        put_left(left, whole, o[:, at])
        put_right(small_right, whole, inverted[:BLK, :])
        for t in range(0, n, 256):
            put_left(left, slice(t, t + 256), dot(left[t : t + 256, :], small_right[...]))
        put_left(left, at, -inverted[:BLK, :])
        o[at, :] = jnp.zeros((BLK, n), F32)
        o[:, at] = jnp.zeros((n, BLK), F32)

    def update(size, t):
        these = pl.ds(pl.multiple_of(t * size, size), size)
        o[these, :] = o[these, :] - dot(left[these, :], right[...])

    if not begun:
        inverted[:BLK, :] = o[:BLK, :BLK]
        invert(inverted, 16, nothing)

    def step(j, carry):
        prepare(j)
        after = pl.ds(pl.multiple_of((j + 1) * BLK, BLK), BLK)
        inverted[:BLK, :] = o[after, after] - dot(left[after, :], right[:, after])
        invert(inverted, ROUNDS, functools.partial(update, n // ROUNDS))
        return carry

    lax.fori_loop(0, blocks if ahead else blocks - 1, step, 0)
    if ahead:
        return
    prepare(blocks - 1)

    def tile(t, carry):
        update(512, t)
        return carry

    lax.fori_loop(0, n // 512, tile, 0)


def scratch_for(n):
    return [
        pltpu.VMEM((n, 4 * BLK), BF16),
        pltpu.VMEM((4 * BLK, n), BF16),
        pltpu.VMEM((4 * BLK, BLK), BF16),
        pltpu.VMEM((BLK + 8, BLK), F32),
    ]


def at_block(b):
    return pl.ds(pl.multiple_of(b * BLK, BLK), BLK)


LOWER = [(a, b) for y in range(4) for a in (y, 7 - y) for b in range(a + 1)]
SHARE = [(i, j) for i in range(4) for j in range(i + 1)]


def pack_update(o, tri):
    for t, (i, j) in enumerate(SHARE):
        tri[t * BLK : (t + 1) * BLK, :] = o[
            SEP1 + i * BLK : SEP1 + (i + 1) * BLK, SEP1 + j * BLK : SEP1 + (j + 1) * BLK
        ]


def first_kernel(blocks, lower_ref, o_ref, tri_ref, *scratch):
    for t, (a, b) in enumerate(LOWER):
        part = lower_ref[t]
        o_ref[a * BLK : (a + 1) * BLK, b * BLK : (b + 1) * BLK] = part
        if a != b:
            o_ref[b * BLK : (b + 1) * BLK, a * BLK : (a + 1) * BLK] = part.T
    eliminate(o_ref, blocks, *scratch)
    pack_update(o_ref, tri_ref)


def add_child(o_ref, update, maps, child):
    for t, (i, j) in enumerate(SHARE):
        rows, columns = at_block(maps[child, i]), at_block(maps[child, j])
        part = update[t * BLK : (t + 1) * BLK, :]
        o_ref[rows, columns] = o_ref[rows, columns] + part
        if i != j:
            o_ref[columns, rows] = o_ref[columns, rows] + part.T


def next_kernel(blocks, members, map_ref, base_ref, mine_ref, other_ref, o_ref, *rest):
    tri_ref, scratch = rest[0], rest[1:]
    child = lax.axis_index("leaf") // members
    add_child(o_ref, mine_ref, map_ref, child)
    add_child(o_ref, other_ref, map_ref, child + 1 - 2 * (child % 2))
    eliminate(o_ref, blocks, *scratch)
    pack_update(o_ref, tri_ref)


def top_kernel(
    members, map_ref, base_ref, mine_ref, other_ref, sigma_ref,
    order, position, o, low, left, right, small_right, inverted, low_left, low_right,
):
    child = lax.axis_index("leaf") // members
    other = child + 1 - 2 * (child % 2)
    count = jnp.int32(0)
    for b in range(8):
        named = jnp.int32(-1)
        for i in range(4):
            named = jnp.where(map_ref[child, i] == b, 4 + i, named)
        spot = jnp.where(named < 0, count, named)
        count = count + jnp.where(named < 0, 1, 0)
        order[spot] = b
        position[b] = spot
    for p in range(8):
        for q in range(8):
            o[p * BLK : (p + 1) * BLK, q * BLK : (q + 1) * BLK] = base_ref[
                at_block(order[p]), at_block(order[q])
            ]
    half = 4 * BLK
    for t, (i, j) in enumerate(SHARE):
        part = mine_ref[t * BLK : (t + 1) * BLK, :]
        rows = slice(half + i * BLK, half + (i + 1) * BLK)
        columns = slice(half + j * BLK, half + (j + 1) * BLK)
        o[rows, columns] = o[rows, columns] + part
        if i != j:
            o[columns, rows] = o[columns, rows] + part.T
    for t, (i, j) in enumerate(SHARE):
        part = other_ref[t * BLK : (t + 1) * BLK, :]
        rows, columns = at_block(position[map_ref[other, i]]), at_block(position[map_ref[other, j]])
        o[rows, columns] = o[rows, columns] + part
        if i != j:
            o[columns, rows] = o[columns, rows] + part.T
    eliminate(o, 4, left, right, small_right, inverted, ahead=True)
    low[...] = o[half:, half:]
    eliminate(low, 4, low_left, low_right, small_right, inverted, begun=True)
    sigma_ref[...] = low[...]


def top_inverse(maps, base, mine, other, members):
    n, half = 8 * BLK, 4 * BLK
    return pl.pallas_call(
        functools.partial(top_kernel, members),
        out_shape=jax.ShapeDtypeStruct((half, half), F32),
        in_specs=[SMEM_SPEC, VMEM_SPEC, VMEM_SPEC, VMEM_SPEC],
        out_specs=VMEM_SPEC,
        scratch_shapes=[
            pltpu.SMEM((8,), jnp.int32),
            pltpu.SMEM((8,), jnp.int32),
            pltpu.VMEM((n, n), F32),
            pltpu.VMEM((half, half), F32),
        ]
        + scratch_for(n)
        + scratch_for(half)[:2],
        compiler_params=PARAMS,
    )(maps, base, mine, other)


def remote(source, target, sent, received, leaf, front):
    return pltpu.make_async_remote_copy(
        src_ref=source,
        dst_ref=target,
        send_sem=sent,
        recv_sem=received,
        device_id=(leaf, front),
        device_id_type=pl.DeviceIdType.MESH,
    )


def greet(devices):
    barrier = pltpu.get_barrier_semaphore()
    for device in devices:
        pl.semaphore_signal(
            barrier, inc=1, device_id=device, device_id_type=pl.DeviceIdType.MESH
        )
    pl.semaphore_wait(barrier, len(devices))


def exchange_kernel(distance, tri_ref, entries_ref, o_ref, base_ref, sent, got, copied):
    leaf, y = lax.axis_index("leaf"), lax.axis_index("front")
    n = base_ref.shape[0]
    start = pl.multiple_of((leaf // (2 * distance)) % (entries_ref.shape[0] // n) * n, 8)
    fetch = pltpu.make_async_copy(entries_ref.at[pl.ds(start, n), :], base_ref, copied)
    fetch.start()
    core, x = leaf % 2, (leaf // 2) % 4
    z = leaf // 8
    sibling = leaf + distance * (1 - 2 * ((leaf // distance) % 2))
    other_core = leaf + 1 - 2 * core
    rows = tri_ref.shape[0] // 32
    apart = [(dx, dy) for dx in (0, 1, 3, 2) for dy in (0, 1, 3, 2)]

    def place(dx, dy):
        return z * 8 + ((x + dx) % 4) * 2 + core, (y + dy) % 4

    greet([(sibling, y), (other_core, y)] + [place(dx, dy) for dx, dy in apart[1:]])

    def share(c, xx, yy):
        return pl.ds(pl.multiple_of(((c * 4 + xx) * 4 + yy) * rows, 8), rows)

    mine = share(core, x, y)
    across = remote(tri_ref.at[mine], o_ref.at[mine], sent.at[0], got.at[0], sibling, y)
    across.start()
    across.wait_recv()
    spread = []
    for t, (dx, dy) in enumerate(apart):
        if t:
            spread.append(
                remote(o_ref.at[mine], o_ref.at[mine], sent.at[t], got.at[t], *place(dx, dy))
            )
    for copy in reversed(spread):
        copy.start()
    last = []
    for t, (dx, dy) in enumerate(apart):
        if t:
            spread[t - 1].wait_recv()
        piece = share(core, (x - dx + 4) % 4, (y - dy + 4) % 4)
        last.append(
            remote(o_ref.at[piece], o_ref.at[piece], sent.at[16 + t], got.at[16 + t], other_core, y)
        )
        last[-1].start()
    for copy in last:
        copy.wait_recv()
    for copy in [across] + spread + last:
        copy.wait_send()
    fetch.wait()


def gather_kernel(
    map_ref, leaf_ref, entries_ref, o_ref,
    met, partial, halves_in, own_entries, found_tile, table, told,
    keep, sent, got, sent_e, got_e, sent_y, got_y, sent_x, got_x, sent_c, got_c,
):
    leaf, y = lax.axis_index("leaf"), lax.axis_index("front")
    m = leaf % 16
    base = leaf - m
    core, x, z = m % 2, (m // 2) % 4, m // 8
    met[:, 4] = jnp.zeros((16, 8, BLK), F32)
    greet(
        [(base + (m + d) % 16, y) for d in range(1, 16)] + [(leaf, (y + d) % 4) for d in (1, 2, 3)]
    )

    kept = pltpu.make_async_copy(leaf_ref.at[:, m], met.at[m, 0:4], keep.at[0])
    kept.start()
    members = []
    for d in range(1, 16):
        to = (m + d) % 16
        members.append(
            remote(leaf_ref.at[:, to], met.at[m, 0:4], sent.at[d], got.at[d], base + to, y)
        )
        members[-1].start()
    a, half = m // 2, m % 2
    for g in range(8):
        to = half * 8 + g
        source = entries_ref.at[pl.ds(8 * g, 8), :]

        @pl.when(to == m)
        def _():
            pltpu.make_async_copy(source, own_entries.at[a], got_e.at[a]).start()

        @pl.when(to != m)
        def _():
            remote(source, own_entries.at[a], sent_e.at[g], got_e.at[a], base + to, y).start()

    lane = lax.broadcasted_iota(jnp.int32, (16, BLK), 1)
    group = (
        (lane >= 9).astype(jnp.int32) + (lane >= 18).astype(jnp.int32) + (lane >= 27).astype(jnp.int32)
    )
    within = lane - 9 * group
    second = within > group
    block_row = jnp.where(second, 7 - group, group)
    block_column = jnp.where(second, within - group - 1, within)
    maps = map_ref[pl.ds(pl.multiple_of(base, 16), 16), :]
    found = jnp.full((16, BLK), 4, jnp.int32)
    landing = jnp.zeros((16, BLK), jnp.int32)
    for i in range(4):
        target = jnp.broadcast_to(maps[:, i : i + 1], (16, BLK))
        found = jnp.where(block_row == target, i, found)
        landing = landing + target * jnp.where(y == i, 1, 0)
    found_tile[...] = jnp.where(block_column == landing, found, 4)
    tell = pltpu.make_async_copy(found_tile, table, told)
    tell.start()
    tell.wait()
    kept.wait()
    for copy in members:
        copy.wait_recv()

    def sum_block(t, carry):
        terms = [met[s, table[s, t]] for s in range(16)]
        while len(terms) > 1:
            terms = [terms[i] + terms[i + 1] for i in range(0, len(terms), 2)]
        partial[t] = terms[0]
        return carry

    lax.fori_loop(0, 36, sum_block, 0)
    for k in range(8):
        pltpu.make_async_copy(
            entries_ref.at[pl.ds(0, 8), :], own_entries.at[k], got_e.at[k]
        ).wait()
    for k in range(8):
        first = 9 * k if k < 4 else 9 * (7 - k) + 8 - k
        for h in range(2):
            b = 2 * y + h

            @pl.when(b <= k)
            def _():
                partial[first + b] = (
                    partial[first + b] + own_entries[k, :, h * BLK : (h + 1) * BLK]
                )

    to_sum = []
    for d in (1, 2, 3):
        to = (y + d) % 4
        to_sum.append(
            remote(
                partial.at[pl.ds(9 * to, 9)], halves_in.at[d - 1],
                sent_y.at[d - 1], got_y.at[d - 1], leaf, to,
            )
        )
        to_sum[-1].start()
    for copy in to_sum:
        copy.wait_recv()
    rows = pl.ds(pl.multiple_of(m * 8, 8), 8)
    for t in range(9):
        o_ref[9 * y + t, rows, :] = (
            partial[9 * y + t] + halves_in[0, t] + halves_in[1, t] + halves_in[2, t]
        )
    spread = []
    own = o_ref.at[pl.ds(9 * y, 9), rows, :]
    for d in (1, 2, 3):
        spread.append(
            remote(own, own, sent_y.at[2 + d], got_y.at[2 + d], leaf, (y + d) % 4)
        )
        spread[-1].start()
    for copy in spread:
        copy.wait_recv()

    other_z = base + (m + 8) % 16
    other_core = base + m + 1 - 2 * core

    def piece(xx, zz, part):
        slot = pl.ds(pl.multiple_of((zz * 8 + xx * 2 + core) * 8, 8), 8)
        return o_ref.at[18 * part : 18 * part + 18, slot, :]

    def step_x(xx, zz, part, direction, slot):
        to = base + z * 8 + ((x + direction + 4) % 4) * 2 + core
        ref = piece(xx, zz, part)
        return remote(ref, ref, sent_x.at[slot], got_x.at[slot], to, y)

    def to_core(xx, zz, part, slot):
        ref = piece(xx, zz, part)
        return remote(ref, ref, sent_c.at[slot], got_c.at[slot], other_core, y)

    started = []

    def begin(copy):
        copy.start()
        started.append(copy)
        return copy

    left, right, far = (x + 3) % 4, (x + 1) % 4, (x + 2) % 4
    other = 1 - z
    over_z = []
    for part in range(2):
        ref = piece(x, z, part)
        over_z.append(begin(remote(ref, ref, sent_y.at[6 + part], got_y.at[6 + part], other_z, y)))
    passes, cores = [], []
    for stage, zz in ((0, z), (1, other)):
        if stage:
            for copy in over_z:
                copy.wait_recv()
        s = 6 * stage
        passes.append(
            [begin(step_x(x, zz, part, 1, s + part)) for part in range(2)]
            + [begin(step_x(x, zz, part, -1, s + 2 + part)) for part in range(2)]
        )
        for part in range(2):
            cores.append(begin(to_core(x, zz, part, 8 * stage + part)))
    for stage, zz in ((0, z), (1, other)):
        s = 6 * stage
        c = 8 * stage
        moves = passes[stage]
        moves[0].wait_recv()
        relay_right = begin(step_x(left, zz, 0, 1, s + 4))
        cores.append(begin(to_core(left, zz, 0, c + 2)))
        moves[3].wait_recv()
        relay_left = begin(step_x(right, zz, 1, -1, s + 5))
        cores.append(begin(to_core(right, zz, 1, c + 3)))
        moves[1].wait_recv()
        cores.append(begin(to_core(left, zz, 1, c + 4)))
        moves[2].wait_recv()
        cores.append(begin(to_core(right, zz, 0, c + 5)))
        passes.append((relay_right, relay_left))
    for stage, zz in ((0, z), (1, other)):
        relay_right, relay_left = passes[2 + stage]
        c = 8 * stage
        relay_right.wait_recv()
        cores.append(begin(to_core(far, zz, 0, c + 6)))
        relay_left.wait_recv()
        cores.append(begin(to_core(far, zz, 1, c + 7)))
    for copy in cores:
        copy.wait_recv()
    for copy in members + to_sum + spread + started:
        copy.wait_send()
    for g in range(8):
        to = half * 8 + g

        @pl.when(to != m)
        def _():
            remote(
                entries_ref.at[pl.ds(8 * g, 8), :], own_entries.at[a],
                sent_e.at[g], got_e.at[a], base + to, y,
            ).wait_send()


VMEM_SPEC = pl.BlockSpec(memory_space=pltpu.VMEM)
SMEM_SPEC = pl.BlockSpec(memory_space=pltpu.SMEM)
PARAMS = pltpu.CompilerParams(vmem_limit_bytes=24 * 1024 * 1024)


def gathered(map_leaf, leaf_update, entries):
    dma = pltpu.SemaphoreType.DMA
    return pl.pallas_call(
        gather_kernel,
        out_shape=jax.ShapeDtypeStruct((36, BLK, BLK), F32),
        in_specs=[VMEM_SPEC, VMEM_SPEC, VMEM_SPEC],
        out_specs=VMEM_SPEC,
        scratch_shapes=[
            pltpu.VMEM((16, 5, 8, BLK), F32),
            pltpu.VMEM((36, 8, BLK), F32),
            pltpu.VMEM((3, 9, 8, BLK), F32),
            pltpu.VMEM((8, 8, 256), F32),
            pltpu.VMEM((16, BLK), jnp.int32),
            pltpu.SMEM((16, BLK), jnp.int32),
            dma,
            dma((1,)), dma((16,)), dma((16,)), dma((8,)), dma((8,)), dma((8,)), dma((8,)),
            dma((12,)), dma((12,)), dma((16,)), dma((16,)),
        ],
        compiler_params=pltpu.CompilerParams(
            vmem_limit_bytes=32 * 1024 * 1024, collective_id=0, has_side_effects=True
        ),
    )(map_leaf, leaf_update.reshape(4, 16, 8, BLK), entries)


def exchanged(tri, entries, distance, collective_id):
    dma = pltpu.SemaphoreType.DMA
    n = 8 * BLK
    return pl.pallas_call(
        functools.partial(exchange_kernel, distance),
        out_shape=(jax.ShapeDtypeStruct(tri.shape, F32), jax.ShapeDtypeStruct((n, n), F32)),
        in_specs=[VMEM_SPEC, pl.BlockSpec(memory_space=pltpu.HBM)],
        out_specs=(VMEM_SPEC, VMEM_SPEC),
        scratch_shapes=[dma((32,)), dma((32,)), dma],
        compiler_params=pltpu.CompilerParams(
            vmem_limit_bytes=(43 if collective_id == 1 else 16) * 1024 * 1024, collective_id=collective_id, has_side_effects=True
        ),
    )(tri, entries)


def first_eliminated(lower, blocks):
    n = 8 * BLK
    return pl.pallas_call(
        functools.partial(first_kernel, blocks),
        out_shape=(
            jax.ShapeDtypeStruct((n, n), F32),
            jax.ShapeDtypeStruct((10 * BLK, BLK), F32),
        ),
        in_specs=[VMEM_SPEC],
        out_specs=(VMEM_SPEC, VMEM_SPEC),
        scratch_shapes=scratch_for(n),
        compiler_params=PARAMS,
    )(lower)


def next_eliminated(maps, base, mine, other, blocks, members):
    n = 8 * BLK
    out = (jax.ShapeDtypeStruct((n, n), F32), jax.ShapeDtypeStruct((10 * BLK, BLK), F32))
    return pl.pallas_call(
        functools.partial(next_kernel, blocks, members),
        out_shape=out,
        in_specs=[SMEM_SPEC, VMEM_SPEC, VMEM_SPEC, VMEM_SPEC],
        out_specs=(VMEM_SPEC, VMEM_SPEC),
        scratch_shapes=scratch_for(n),
        input_output_aliases={1: 0},
        compiler_params=PARAMS,
    )(maps, base, mine, other)


def columns_of_inverse(swept, sigma, sigma_left, coupling_left, blocks, value, value_right, out):
    half = 4 * BLK
    for t, block in enumerate(blocks):
        here = slice(t * BLK, (t + 1) * BLK)

        @pl.when(block < 4)
        def _():
            put_right(value_right, here, swept[half:, at_block(block)])
            out[:half, here] = -swept[:half, at_block(block)]

        @pl.when(block >= 4)
        def _():
            value_right[:, here] = jnp.zeros((3 * half, BLK), BF16)
            out[:half, here] = jnp.zeros((half, BLK), F32)

    width = len(blocks) * BLK
    value[:, :width] = -dot(sigma_left[...], value_right[:, :width])
    for t, block in enumerate(blocks):
        here = slice(t * BLK, (t + 1) * BLK)

        @pl.when(block >= 4)
        def _():
            value[:, here] = sigma[:, at_block(block - 4)]

        lower = value[:, here]
        put_right(value_right, here, lower)
        out[half:, here] = lower
    out[:half, :width] = out[:half, :width] - dot(coupling_left[...], value_right[:, :width])


def back_kernel(
    mid_ref, leaf_ref, one_ref, two_ref, top_ref, o_ref,
    sigma, sigma_left, coupling_left, value, value_right, columns, lower,
):
    half = 4 * BLK
    whole = slice(None)
    leaf = lax.axis_index("leaf")
    first_node = leaf // 16
    sigma[...] = -top_ref[...]
    put_left(sigma_left, whole, sigma[...])
    put_left(coupling_left, whole, two_ref[:half, half:])
    blocks = [mid_ref[first_node, j] for j in range(4)]
    columns_of_inverse(
        two_ref, sigma, sigma_left, coupling_left, blocks, value, value_right, columns
    )
    for i in range(4):
        lower[i * BLK : (i + 1) * BLK, :] = columns[at_block(blocks[i]), :]
    put_left(sigma_left, whole, lower[...])
    put_left(coupling_left, whole, one_ref[:half, half:])
    columns_of_inverse(
        one_ref, lower, sigma_left, coupling_left, [leaf_ref[leaf, lax.axis_index("front")]],
        value, value_right, columns,
    )
    for i in range(4):
        o_ref[i * BLK : (i + 1) * BLK, :] = columns[at_block(leaf_ref[leaf, i]), :BLK]


def back_substituted(mid, leaf, one, two, top):
    half = 4 * BLK
    return pl.pallas_call(
        back_kernel,
        out_shape=jax.ShapeDtypeStruct((half, BLK), F32),
        in_specs=[SMEM_SPEC] * 2 + [VMEM_SPEC] * 3,
        out_specs=VMEM_SPEC,
        scratch_shapes=[
            pltpu.VMEM((half, half), F32),
            pltpu.VMEM((half, 3 * half), BF16),
            pltpu.VMEM((half, 3 * half), BF16),
            pltpu.VMEM((half, half), F32),
            pltpu.VMEM((3 * half, half), BF16),
            pltpu.VMEM((2 * half, half), F32),
            pltpu.VMEM((half, half), F32),
        ],
        compiler_params=PARAMS,
    )(mid, leaf, one, two, top)


def body(leaf_update, front_entries1, front_entries2, front_entries3, map_leaf, map_mid, map_top):
    members = lax.axis_size("leaf") // 4
    lower = gathered(map_leaf, leaf_update, front_entries1)
    one, update = first_eliminated(lower, SEP1 // BLK)
    other, base = exchanged(update, front_entries2, members, 1)
    two, update = next_eliminated(map_mid, base, update, other, SEP2 // BLK, members)
    other, base = exchanged(update, front_entries3, 2 * members, 2)
    top = top_inverse(map_top, base, update, other, 2 * members)
    return back_substituted(map_mid, map_leaf, one, two, top)


def solution(mesh):
    in_specs = (P("leaf", "front"), P("leaf", "front"), P(), P(), P(), P(), P())
    out_specs = P("leaf", "front")
    return jax.shard_map(body, mesh=mesh, in_specs=in_specs, out_specs=out_specs, check_vma=False)
```
